32 devices in a mesh: wide: 16 (over z, y, core), narrow: 2 (over x).
Axes of the slice: x: 2, y: 2, z: 4, core: 2. Of those that a mesh axis runs over, the one named last changes fastest.
Arguments:
- tokens: bfloat16 [64, 1024, 768], P('wide', 'narrow'), may hold values from -6 to 6
- cotangent: bfloat16 [64, 1024, 768], P('wide', 'narrow'), may hold values from -6 to 6
- conv_attn: bfloat16 [9, 768], P(None, 'wide'), may hold values from -2 to 2
- qkv_weight: bfloat16 [768, 2304], P('wide'), may hold values from -0.21875 to 0.21875
- out_weight: bfloat16 [768, 768], P('wide'), may hold values from -0.875 to 0.875
- up_weight: bfloat16 [768, 3072], P('wide'), may hold values from -0.21875 to 0.21875
- conv_ffn: bfloat16 [9, 3072], P(None, 'wide'), may hold values from -2 to 2
- down_weight: bfloat16 [3072, 768], P('wide'), may hold values from -0.109375 to 0.109375
- ada_weight: bfloat16 [768, 4608], P('wide'), may hold values from -0.21875 to 0.21875
- class_table: bfloat16 [1000, 768], P(None, 'wide'), may hold values from -6 to 6
- timesteps: int32 [64, 4], replicated, may hold values from 0 to 999
- labels: int32 [64, 4], replicated, may hold values from 0 to 999
- layout: int32 [64], replicated, may hold values from 0 to 2
- counts: int32 [64], replicated, may hold values from 0 to 1024, as said below
Outputs:
- output: bfloat16 [64, 1024, 768], P('wide', 'narrow')
- grad_tokens: bfloat16 [64, 1024, 768], P('wide', 'narrow')
- grad_conv_attn: float32 [9, 768], P(None, 'wide')
- grad_qkv_weight: float32 [768, 2304], P('wide')
- grad_out_weight: float32 [768, 768], P('wide')
- grad_up_weight: float32 [768, 3072], P('wide')
- grad_conv_ffn: float32 [9, 3072], P(None, 'wide')
- grad_down_weight: float32 [3072, 768], P('wide')
- grad_ada_weight: float32 [768, 4608], P('wide')
- grad_class_table: float32 [1000, 768], P(None, 'wide')
The draws below stay inside these ranges and needn't reach their ends.
Inputs may be any that keep to these rules, and one draw needn't show every extreme that they name: Owner o holds the 4 canvas slots o * 4 to (o + 1) * 4 - 1, those with a nonzero count first. Owners o and o + 8 together hold exactly 4 canvases with nonzero counts, and some owner holds 4. Nonzero counts are 256 or more.
All inputs are finite; a program needn't handle non-finite values.
Results may differ from the reference program's by a relative error of at most 0.02.
The reference program's roundings to bfloat16 on the way count: a program that leaves them out, or rounds other values in their place, can miss the bound.
Values may be sent and summed in bfloat16 or wider, within the bound.
No kernel may reach another device: no remote copies, remote signals or barrier semaphores. Data moves between devices by JAX's collectives and lax.ppermute only.
A program may use at most 512 MiB of HBM per device.

```python
import math
import jax
import jax.numpy as jnp
from jax import lax

D = 768
HEADS = 12
HEAD_DIM = 64
FF = 3072
CLASSES = 1000
GRID = 32
SLOTS = 4
OWNERS = 16
CANVASES = 64
TOK = 1024


def draw_counts(key, part):
    load_key = jax.random.fold_in(key, 101)
    pick_key = jax.random.fold_in(key, 202)
    side_key = jax.random.fold_in(key, 303)
    jitter_key = jax.random.fold_in(key, 404)
    pair_count = OWNERS // 2
    split_load = jax.random.randint(load_key, (pair_count,), 0, SLOTS + 1)
    chosen_pair = jax.random.randint(pick_key, (), 0, pair_count)
    split_load = jnp.where(jnp.arange(pair_count) == chosen_pair, SLOTS, split_load)
    side_bits = jax.random.randint(side_key, (pair_count,), 0, 2)
    lower_load = jnp.where(side_bits == 1, split_load, SLOTS - split_load)
    owner_loads = jnp.concatenate([lower_load, SLOTS - lower_load])
    slot_ids = jnp.arange(SLOTS)[None, :]
    owner_ids = jnp.arange(OWNERS)[:, None]
    rising = 256 + 736 * owner_ids // max(OWNERS - 1, 1)
    jitter_values = jax.random.randint(jitter_key, (OWNERS, SLOTS), 0, 33)
    values = jnp.where(slot_ids < owner_loads[:, None], rising + jitter_values, 0)
    return values.reshape(OWNERS * SLOTS).astype(jnp.int32)


def place_ends(entries, rng, least, top_value):
    longest = entries.shape.index(max(entries.shape))
    spots = []
    for shift in (0, 1):
        where = [jax.random.randint(jax.random.fold_in(rng, axis), (), 0, length) for axis, length in enumerate(entries.shape)]
        where[longest] = (where[longest] + shift) % entries.shape[longest]
        spots.append(tuple(where))
    return entries.at[spots[0]].set(least).at[spots[1]].set(top_value)


def block_scale(rng, dims, cuts, low, top_value):
    def one(dim, blocks):
        heights = jax.random.uniform(jax.random.fold_in(jax.random.fold_in(rng, 6), dim), (blocks,), jnp.float32, low / len(cuts), top_value / len(cuts))
        return jnp.repeat(jnp.exp(heights), dims[dim] // blocks).reshape((-1,) + (1,) * (len(dims) - dim - 1))

    level = one(*cuts[0])
    for cut in cuts[1:]:
        level = level * one(*cut)
    return level


def noise(own_key, extent, width, bound, cuts=(), kind=jnp.bfloat16):
    values = width * jax.random.normal(own_key, extent, jnp.float32)
    if cuts:
        values = values * block_scale(own_key, extent, cuts, -0.22, 0.18)
    return jnp.clip(values, -bound, bound).astype(kind)


def setup_inputs(seed: int = 0) -> dict:
    seeds = jax.random.split(jax.random.key(seed), 15)
    return {
        "tokens": noise(seeds[0], (CANVASES, TOK, D), 1.0, 6.0, ((0, 16), (1, 2))),
        "cotangent": noise(seeds[1], (CANVASES, TOK, D), 1.0, 6.0, ((0, 16), (1, 2))),
        "conv_attn": noise(seeds[2], (9, D), 9 ** -0.5, 2.0, ((1, 16),)),
        "qkv_weight": noise(seeds[3], (D, 3 * D), D ** -0.5, 0.21875, ((0, 16),)),
        "out_weight": noise(seeds[4], (D, D), (D // 16) ** -0.5, 0.875, ((0, 16),)),
        "up_weight": noise(seeds[5], (D, FF), D ** -0.5, 0.21875, ((0, 16),)),
        "conv_ffn": noise(seeds[6], (9, FF), 9 ** -0.5, 2.0, ((1, 16),)),
        "down_weight": noise(seeds[7], (FF, D), FF ** -0.5, 0.109375, ((0, 16),)),
        "ada_weight": noise(seeds[8], (D, 6 * D), D ** -0.5, 0.21875, ((0, 16),)),
        "class_table": noise(seeds[9], (CLASSES, D), 1.0, 6.0, ((1, 16),)),
        "timesteps": place_ends(jax.random.randint(seeds[10], (CANVASES, 4), 0, 1000), jax.random.fold_in(seeds[10], 1), 0, 999).astype(jnp.int32),
        "labels": place_ends(jax.random.randint(seeds[11], (CANVASES, 4), 0, CLASSES), jax.random.fold_in(seeds[11], 1), 0, CLASSES - 1).astype(jnp.int32),
        "layout": place_ends(jax.random.randint(seeds[12], (CANVASES,), 0, 3), jax.random.fold_in(seeds[12], 1), 0, 2).astype(jnp.int32),
        "counts": draw_counts(jax.random.fold_in(seeds[14], 71), 0),
    }


@jax.custom_vjp
def low(v):
    return lax.optimization_barrier(v.astype(jnp.bfloat16)).astype(jnp.float32)

@jax.custom_vjp
def low_back(v):
    return v

def low_keep(v):
    return (low(v), None)

def low_pass(kept, grad):
    return (grad,)

def back_keep(v):
    return (v, None)

def back_low(kept, grad):
    return (low(grad),)
low.defvjp(low_keep, low_pass)
low_back.defvjp(back_keep, back_low)
highest = lax.Precision.HIGHEST
norm_eps = 1e-06
masked_score = -1e+30

def canvas_segments(layout_one):
    row_ids = jnp.arange(GRID, dtype=jnp.int32)[:, None]
    col_ids = jnp.arange(GRID, dtype=jnp.int32)[None, :]
    quarter = 2 * (row_ids // (GRID // 2)) + col_ids // (GRID // 2)
    across = row_ids // (GRID // 4) + 0 * col_ids
    downward = col_ids // (GRID // 4) + 0 * row_ids
    return jnp.where(layout_one == 0, quarter, jnp.where(layout_one == 1, across, downward)).astype(jnp.int32)

def depthwise(values, taps, segment):
    padded = jnp.pad(values, ((1, 1), (1, 1), (0, 0)))
    seg_padded = jnp.pad(segment, 1, constant_values=-1)
    total = jnp.zeros(values.shape, values.dtype)
    for row_step in range(3):
        for col_step in range(3):
            nearby = padded[row_step:row_step + GRID, col_step:col_step + GRID]
            same = seg_padded[row_step:row_step + GRID, col_step:col_step + GRID] == segment
            total = total + jnp.where(same[:, :, None], nearby, 0.0) * taps[3 * row_step + col_step]
    return total

def to_subgrids(values):
    viewed = values.reshape(GRID // 2, 2, GRID // 2, 2, HEADS, HEAD_DIM)
    return viewed.transpose(1, 3, 4, 0, 2, 5).reshape(2, 2, HEADS, (GRID // 2) ** 2, HEAD_DIM)

def from_subgrids(values):
    viewed = values.reshape(2, 2, HEADS, GRID // 2, GRID // 2, HEAD_DIM)
    return viewed.transpose(3, 0, 4, 1, 2, 5).reshape(GRID, GRID, HEADS * HEAD_DIM)

def layer_norm(values):
    centred = values - lax.optimization_barrier(jnp.mean(values, axis=-1, keepdims=True))
    inverse = lax.rsqrt(lax.optimization_barrier(jnp.mean(centred * centred, axis=-1, keepdims=True)) + norm_eps)
    return centred * inverse

def canvas_forward(canvas_tokens, conv_attn, qkv_weight, out_weight, up_weight, conv_ffn, down_weight, ada_weight, class_table, steps_here, labels_here, layout_here):
    half_width = D // 2
    freqs = jnp.exp(-math.log(10000.0) * jnp.arange(half_width, dtype=jnp.float32) / half_width)
    angles = steps_here.astype(jnp.float32)[:, None] * freqs[None, :]
    sinus = jnp.concatenate([jnp.cos(angles), jnp.sin(angles)], axis=1)
    label_hot = (labels_here[:, None] == jnp.arange(CLASSES, dtype=jnp.int32)[None, :]).astype(jnp.float32)
    embed = sinus + jnp.dot(label_hot, class_table, precision=highest)
    activ = low(jax.nn.silu(embed))
    modulation = jnp.dot(activ, ada_weight, precision=highest)
    segment = canvas_segments(layout_here)
    seg_hot = (segment.reshape(TOK)[:, None] == jnp.arange(4, dtype=jnp.int32)[None, :]).astype(jnp.float32)
    per_token = jnp.dot(seg_hot, modulation, precision=highest)
    shift_a, scale_a, gate_a, shift_b, scale_b, gate_b = jnp.split(per_token, 6, axis=1)
    hidden = low(layer_norm(canvas_tokens) * (1.0 + scale_a) + shift_a)
    mixed = low(low_back(depthwise(hidden.reshape(GRID, GRID, D), conv_attn, segment))).reshape(TOK, D)
    projected = jnp.dot(mixed, qkv_weight, precision=highest)
    query = low(low_back(projected[:, :D]))
    keys = low(low_back(projected[:, D:2 * D]))
    values = low(low_back(projected[:, 2 * D:]))
    q_sub = to_subgrids(query.reshape(GRID, GRID, D))
    k_sub = to_subgrids(keys.reshape(GRID, GRID, D))
    v_sub = to_subgrids(values.reshape(GRID, GRID, D))
    seg_sub = segment.reshape(GRID // 2, 2, GRID // 2, 2).transpose(1, 3, 0, 2).reshape(2, 2, (GRID // 2) ** 2)
    allowed = seg_sub[:, :, None, :, None] == seg_sub[:, :, None, None, :]
    scores = low_back(jnp.einsum('abhqd,abhkd->abhqk', q_sub, k_sub, precision=highest) * 0.125)
    masked = jnp.where(allowed, scores, masked_score)
    top = lax.optimization_barrier(jnp.max(masked, axis=-1, keepdims=True))
    expo = jnp.exp(masked - top)
    probs = low(expo / lax.optimization_barrier(jnp.sum(expo, axis=-1, keepdims=True)))
    attended = jnp.einsum('abhqk,abhkd->abhqd', probs, v_sub, precision=highest)
    attended = low(low_back(from_subgrids(attended).reshape(TOK, D)))
    branch_a = low_back(jnp.dot(attended, out_weight, precision=highest))
    middle = canvas_tokens + gate_a * branch_a
    ffn_in = low(layer_norm(middle) * (1.0 + scale_b) + shift_b)
    upward = low(low_back(jnp.dot(ffn_in, up_weight, precision=highest)))
    spread = low_back(depthwise(upward.reshape(GRID, GRID, FF), conv_ffn, segment))
    activated = low(jax.nn.gelu(spread, approximate=True)).reshape(TOK, FF)
    branch_b = low_back(jnp.dot(activated, down_weight, precision=highest))
    return middle + gate_b * branch_b

def reference(tokens, cotangent, conv_attn, qkv_weight, out_weight, up_weight, conv_ffn, down_weight, ada_weight, class_table, timesteps, labels, layout, counts):
    params = tuple((weight.astype(jnp.float32) for weight in (conv_attn, qkv_weight, out_weight, up_weight, conv_ffn, down_weight, ada_weight, class_table)))
    count_float = counts.astype(jnp.float32)
    scales = count_float * float(CANVASES) / jnp.sum(count_float)

    def one_canvas(carry, inputs):
        canvas_tokens, canvas_cot, steps_here, labels_here, layout_here, scale_here = inputs

        def forward(token_values, *weights):
            return canvas_forward(token_values, *weights, steps_here, labels_here, layout_here)
        result, pullback = jax.vjp(forward, canvas_tokens.astype(jnp.float32), *params)
        grads = pullback(canvas_cot.astype(jnp.float32) * scale_here)
        alive = scale_here > 0.0
        new_carry = tuple((summed + grad_part for summed, grad_part in zip(carry, grads[1:])))
        shown = jnp.where(alive, result, 0.0).astype(jnp.bfloat16)
        return (new_carry, (shown, grads[0].astype(jnp.bfloat16)))
    start_carry = tuple((jnp.zeros(weight.shape, jnp.float32) for weight in params))
    final_carry, stacked = lax.scan(one_canvas, start_carry, (tokens, cotangent, timesteps, labels, layout, scales))
    return (stacked[0], stacked[1], final_carry[0], final_carry[1], final_carry[2], final_carry[3], final_carry[4], final_carry[5], final_carry[6], final_carry[7])
```

```python
from functools import partial
import math

import jax
import jax.numpy as jnp
import numpy as np
from jax import lax
from jax.experimental import pallas as pl
from jax.experimental.pallas import tpu as pltpu
from jax.sharding import PartitionSpec as P

HEAD_DIM = 64
GRID = 32
LATENT = 256
HALF = 2 * LATENT
PARTS = 2
ROWS = 128
GROUP = 256
VMEM_BYTES = 67000000

norm_eps = 1e-06
bf16 = jnp.bfloat16
f32 = jnp.float32


def dot(a, b):
    return lax.dot_general(a, b, (((1,), (0,)), ((), ())), preferred_element_type=f32)


def dot_nt(a, b):
    return lax.dot_general(a, b, (((1,), (1,)), ((), ())), preferred_element_type=f32)


def dot_tn(a, b):
    return lax.dot_general(a, b, (((0,), (0,)), ((), ())), preferred_element_type=f32)


def norm_parts(values):
    centred = values - jnp.mean(values, axis=-1, keepdims=True)
    inverse = lax.rsqrt(jnp.mean(centred * centred, axis=-1, keepdims=True) + norm_eps)
    return centred * inverse, inverse


def norm_back(grad_normed, normed, inverse):
    return inverse * (
        grad_normed
        - jnp.mean(grad_normed, axis=-1, keepdims=True)
        - normed * jnp.mean(grad_normed * normed, axis=-1, keepdims=True)
    )


def edges(narrow_grid):
    place = lax.broadcasted_iota(jnp.int32, (64, 128), 0)
    place = jnp.where(narrow_grid, place % 8, place % 16)
    return place == 0, place == jnp.where(narrow_grid, 7, 15)


def neighbours(blocks, narrow_grid, ends):
    first, last = ends
    gap = jnp.zeros((16, 128), blocks[0].dtype)

    def earlier(v):
        padded = jnp.concatenate([gap, v], 0)
        return jnp.where(narrow_grid, padded[8:72], padded[:64])

    def later(v):
        padded = jnp.concatenate([v, gap], 0)
        return jnp.where(narrow_grid, padded[8:72], padded[16:80])

    columns, moved = [], []
    for row_parity in range(2):
        even, odd = blocks[2 * row_parity], blocks[2 * row_parity + 1]
        before = jnp.where(first, 0.0, pltpu.roll(odd, 1, 0))
        after = jnp.where(last, 0.0, pltpu.roll(even, 63, 0))
        shift = later if row_parity == 0 else earlier
        b, e, o, a = [shift(v) for v in (before, even, odd, after)]
        columns.append(((before, even, odd), (even, odd, after)))
        moved.append(((b, e, o), (e, o, a)))
    found = []
    for row_parity in range(2):
        for parity in range(2):
            same, other, far = columns[row_parity][parity], columns[1 - row_parity][parity], moved[1 - row_parity][parity]
            found.append((*far, *same, *other) if row_parity == 0 else (*other, *same, *far))
    return found


def weighted(found, taps):
    total = found[0] * taps[0]
    for tap in range(1, 9):
        total = total + found[tap] * taps[tap]
    return total


def phase_rows(latent):
    return [slice(latent * LATENT + 64 * phase, latent * LATENT + 64 * phase + 64) for phase in range(4)]


def add_taps(store, which, lanes, found, grads):
    for tap in range(9):
        total = found[0][tap] * grads[0]
        for phase in range(1, 4):
            total = total + found[phase][tap] * grads[phase]
        store[which, 8 * tap : 8 * tap + 8, lanes] += jnp.sum(total.reshape(8, 8, total.shape[1]), axis=0)


def head_mask():
    rows = lax.broadcasted_iota(jnp.int32, (GROUP, GROUP), 0) // HEAD_DIM
    cols = lax.broadcasted_iota(jnp.int32, (GROUP, GROUP), 1) // HEAD_DIM
    return jnp.where(rows == cols, 1.0, 0.0).astype(bf16)


def spread_heads(values, mask):
    return jnp.concatenate([values] * 4, 0) * mask


def head_max(values):
    low = lax.broadcasted_iota(jnp.int32, values.shape, 1) < HEAD_DIM
    lower = jnp.max(jnp.where(low, values, -jnp.inf), axis=-1, keepdims=True)
    upper = jnp.max(jnp.where(low, -jnp.inf, values), axis=-1, keepdims=True)
    return jnp.where(low, lower, upper)


def row_block(step, size, start=0):
    return pl.ds(pl.multiple_of(start + step * size, size), size)


def arrange(base, meta, tok, far_tok, places, out):
    @pl.when(meta[pl.program_id(0) + base] > 0)
    def _():
        @pl.loop(0, HALF // ROWS)
        def _(step):
            rows = row_block(step, ROWS)
            source = lax.broadcasted_iota(jnp.int32, (ROWS, 3 * LATENT), 1)
            hot = jnp.where(places[0, rows, :] == source, 1.0, 0.0).astype(bf16)
            values = dot(hot[:, :HALF], tok[0]) + dot(hot[:, HALF:], far_tok[0])
            out[0, rows, :] = values.astype(bf16)


def put_back(result, spots, own, far):
    for step in range(3 * LATENT // ROWS):
        target = lax.broadcasted_iota(jnp.int32, (ROWS, HALF), 0) + step * ROWS
        hot = jnp.where(spots[0] == target, 1.0, 0.0).astype(bf16)
        values = dot(hot, result[0]).astype(bf16)
        if step * ROWS < HALF:
            own[0, step * ROWS : (step + 1) * ROWS, :] = values
        else:
            far[0, step * ROWS - HALF : (step + 1) * ROWS - HALF, :] = values


def place_back(meta, result, spots, own, far):
    @pl.when(meta[3] > 0)
    def _():
        put_back(result, spots, own, far)


def mix_tokens(base, taken, meta, *refs):
    if taken:
        x, other, mod, taps, x_o, mix_o, hidden = refs
    else:
        x, mod, taps, x_o, mix_o, hidden = refs
    unit = pl.program_id(0) + base

    @pl.when(meta[unit] > 0)
    def _():
        for latent in range(2):
            shift, scale = mod[0, latent, 0:1, :], 1.0 + mod[0, latent, 1:2, :]

            @pl.loop(0, LATENT // ROWS)
            def _(step):
                rows = row_block(step, ROWS, latent * LATENT)
                values = x[0, rows, :].astype(f32)
                if taken:
                    values = jnp.where(meta[0] > 0, values, other[0, rows, :].astype(f32))
                x_o[0, rows, :] = values.astype(bf16)
                normed, _ = norm_parts(values)
                hidden[rows, :] = (normed * scale + shift).astype(bf16).astype(f32)

        narrow_grid = meta[meta.shape[0] // 2 + unit] == 0
        ends = edges(narrow_grid)

        @pl.loop(0, x.shape[2] // 128)
        def _(step):
            lanes = row_block(step, 128)
            weights = [taps[0, tap : tap + 1, lanes] for tap in range(9)]
            for latent in range(2):
                found = neighbours([hidden[r, lanes] for r in phase_rows(latent)], narrow_grid, ends)
                for rows, near in zip(phase_rows(latent), found):
                    mix_o[0, rows, lanes] = weighted(near, weights).astype(bf16)


def attend(base, meta, x, mix, mod, weights_p, weights_q, qkv_o, prob_o, att_o, branch_o, mid_o, ffn_o):
    unit = pl.program_id(0) + base
    width = x.shape[2]
    groups = width // GROUP

    @pl.when(meta[unit] > 0)
    def _():
        @pl.loop(0, weights_p.shape[1] // 256)
        def _(step):
            lanes = row_block(step, 256)
            qkv_o[0, :, lanes] = dot(mix[0], weights_p[:, lanes]).astype(bf16)

        qkv_o[0, :, 3 * width - GROUP :] = dot(mix[0], weights_q[:, :GROUP]).astype(bf16)

        mask = head_mask()

        @pl.loop(0, HALF // 128)
        def _(step):
            chains = []
            for block in range(2):
                rows = row_block(step * 2 + block, 64)
                for group in range(groups):
                    at = GROUP * group
                    keys = spread_heads(qkv_o[0, rows, width + at : width + at + GROUP], mask)
                    chains.append((rows, group, dot_nt(qkv_o[0, rows, at : at + GROUP], keys) * 0.125))
            raised = [
                jnp.concatenate([jnp.exp(s[:, c : c + 128] - head_max(s[:, c : c + 128])) for c in (0, 128)], 1)
                for _, _, s in chains
            ]
            totals = [dot(e.astype(bf16), mask) for e in raised]
            for (rows, group, _), e, total in zip(chains, raised, totals):
                probs = (e / total).astype(bf16)
                at = GROUP * group
                values = spread_heads(qkv_o[0, rows, 2 * width + at : 2 * width + at + GROUP], mask)
                prob_o[0, rows, at : at + GROUP] = probs
                att_o[0, rows, at : at + GROUP] = dot(probs, values).astype(bf16)

        for latent in range(2):
            gate_a = mod[0, latent, 2:3, :]
            shift, scale = mod[0, latent, 3:4, :], 1.0 + mod[0, latent, 4:5, :]

            @pl.loop(0, LATENT // ROWS)
            def _(step):
                rows = row_block(step, ROWS, latent * LATENT)
                branch = dot(att_o[0, rows, :], weights_q[:, GROUP:])
                branch_o[0, rows, :] = branch.astype(bf16)
                middle = x[0, rows, :].astype(f32) + gate_a * branch
                mid_o[0, rows, :] = middle
                normed, _ = norm_parts(middle)
                ffn_o[0, rows, :] = (normed * scale + shift).astype(bf16)


def feed_forward(part, shard, taken, meta, *refs):
    if part == 0:
        if taken:
            cot, other, mod, ffn, up_w, down_w, taps, *refs = refs
        else:
            cot, mod, ffn, up_w, down_w, taps, *refs = refs
        gbb_o, bb_o, gf_o, up_o, down_o, dtap_o, *refs = refs
        gbb = gbb_o
    else:
        gbb, ffn, up_w, down_w, taps, bb_i, gf_i, mid, mod, spots, down_i, *refs = refs
        gf_o, y_o, own_o, far_o, grad_o, dtap_o, bb_o, *refs = refs
    ffn_t, gbb_t, acc_up, acc_down, *slots = refs
    unit = pl.program_id(0)
    width = ffn.shape[2]
    columns = taps.shape[2]
    items = columns // 256

    @pl.when(unit == 0)
    def _():
        acc_up[...] = jnp.zeros_like(acc_up)
        acc_down[...] = jnp.zeros_like(acc_down)
        dtap_o[...] = jnp.zeros_like(dtap_o)

    @pl.when(meta[unit] > 0)
    def _():
        if part == 0:
            for latent in range(2):
                gate, weight = mod[0, latent, 5:6, :], mod[0, latent, 6:7, :]

                @pl.loop(0, LATENT // 64)
                def _(step):
                    rows = row_block(step, 64, latent * LATENT)
                    grads = cot[0, rows, :].astype(f32)
                    if taken:
                        from_other = jnp.logical_and(unit == 2, meta[0] == 0)
                        grads = jnp.where(from_other, other[0, rows, :].astype(f32), grads)
                    gbb_o[0, rows, :] = (gate * (grads * weight)).astype(bf16)

        ffn_t[...] = ffn[0].T
        gbb_t[...] = gbb[0].T
        layout = meta[meta.shape[0] // 2 + unit]
        which = jnp.where(layout == 2, 1, 0)
        narrow_grid = layout == 0
        ends = edges(narrow_grid)
        uses = [slots[i::2] for i in range(2)]
        uses[1][2][...] = jnp.zeros_like(uses[1][2])
        uses[1][3][...] = jnp.zeros_like(uses[1][3])
        root = math.sqrt(2.0 / math.pi)

        @pl.loop(0, HALF // 128)
        def _(step):
            rows = row_block(step, 128)
            if part == 0:
                bb_o[0, rows, :] = jnp.zeros((128, width), f32)
                gf_o[0, rows, :] = jnp.zeros((128, width), f32)
            else:
                bb_o[0, rows, :] = bb_i[0, rows, :]
                gf_o[0, rows, :] = gf_i[0, rows, :]

        def project(item, use):
            upward, grad_act = use[0], use[1]
            here = row_block(item, 256)
            upward[...] = dot(ffn[0], up_w[:, here]).astype(bf16).astype(f32)
            grad_act[...] = dot_nt(gbb[0], down_w[here, :])

        def collect(item, use):
            act, grad_up = use[2], use[3]
            here = row_block(item, 256)
            bb_o[0] += dot(act[...], down_w[here, :])
            gf_o[0] += dot_nt(grad_up[...], up_w[:, here])
            acc_up[:, here] += dot(ffn_t[...], grad_up[...])
            acc_down[:, here] += dot(gbb_t[...], act[...])

        def convolve(item, use):
            upward, grad_act, act, grad_up = use
            for side in range(2):
                cols = slice(128 * side, 128 * side + 128)
                lanes = row_block(2 * item + side, 128)
                taken_taps = [taps[0, tap : tap + 1, lanes] for tap in range(9)]
                for latent in range(2):
                    rows = phase_rows(latent)
                    found = neighbours([upward[r, cols] for r in rows], narrow_grid, ends)
                    grads = []
                    for r, near in zip(rows, found):
                        spread = weighted(near, taken_taps)
                        square = spread * spread
                        bent = jnp.tanh(spread * (root + root * 0.044715 * square))
                        half = 0.5 + 0.5 * bent
                        act[r, cols] = (spread * half).astype(bf16)
                        slope = half + (0.5 * spread) * (1.0 - bent * bent) * (
                            root + 3.0 * root * 0.044715 * square
                        )
                        grads.append((grad_act[r, cols] * slope).astype(bf16).astype(f32))
                    add_taps(dtap_o, which, lanes, found, grads)
                    for r, near in zip(rows, neighbours(grads, narrow_grid, ends)):
                        grad_up[r, cols] = weighted(near, taken_taps[::-1]).astype(bf16)

        project(0, uses[0])

        @pl.loop(0, items // 2)
        def _(pair):
            for side in range(2):
                item = 2 * pair + side
                convolve(item, uses[side])
                project(jnp.minimum(item + 1, items - 1), uses[1 - side])
                collect(jnp.maximum(item - 1, 0), uses[1 - side])

        collect(items - 1, uses[1])

        if part == PARTS - 1:
            for latent in range(2):
                gate = mod[0, latent, 5:6, :]

                @pl.loop(0, LATENT // 64)
                def _(step):
                    rows = row_block(step, 64, latent * LATENT)
                    y_o[0, rows, :] = (mid[0, rows, :] + gate * bb_o[0, rows, :]).astype(bf16)

            put_back(y_o, spots, own_o, far_o)

    @pl.when(unit == pl.num_programs(0) - 1)
    def _():
        blocks = PARTS * columns // width
        if part == 0:
            up_o[...] = acc_up[...].astype(bf16)
            store, row_at, col_at = down_o, 0, 0
        else:
            grad_o[:, :columns] = acc_up[...].astype(bf16)
            grad_o[: width // 2, columns:] = down_i[...]
            store, row_at, col_at = grad_o, width // 2, columns
        for start in range(0, columns, width):
            turned_rows = acc_down[:, start : start + width].T
            for piece in range(width // shard):
                owner, block = divmod(start // shard + piece, blocks)
                rows = slice(row_at + owner * shard, row_at + owner * shard + shard)
                lanes = slice(col_at + block * width, col_at + block * width + width)
                store[rows, lanes] = turned_rows[piece * shard : piece * shard + shard].astype(bf16)


def backward_middle(taken, meta, *refs):
    if taken:
        cot, other, *refs = refs
    else:
        cot, *refs = refs
    bb, gf, mid, branch, att, mod, weights_q, grad_mid, grad_att, mod_o, dout_o, gba, acc_out = refs
    unit = pl.program_id(0)
    width = cot.shape[2]

    @pl.when(unit == 0)
    def _():
        acc_out[...] = jnp.zeros_like(acc_out)

    @pl.when(meta[unit] > 0)
    def _():
        mod_o[...] = jnp.zeros_like(mod_o)
        for latent in range(2):
            gate_a, scale_b = mod[0, latent, 2:3, :], 1.0 + mod[0, latent, 4:5, :]
            weight = mod[0, latent, 6:7, :]

            def tally(block, values):
                mod_o[0, latent, block : block + 1, :] += jnp.sum(values, axis=0, keepdims=True)

            @pl.loop(0, 4)
            def _(step):
                rows = row_block(step, 64, latent * LATENT)
                grads = cot[0, rows, :].astype(f32)
                if taken:
                    from_other = jnp.logical_and(unit == 2, meta[0] == 0)
                    grads = jnp.where(from_other, other[0, rows, :].astype(f32), grads)
                grad_out = grads * weight
                tally(3, grad_out * bb[0, rows, :])
                grad_ffn = gf[0, rows, :]
                normed, inverse = norm_parts(mid[0, rows, :])
                tally(1, grad_ffn)
                tally(2, grad_ffn * normed)
                total = grad_out + norm_back(grad_ffn * scale_b, normed, inverse)
                grad_mid[0, rows, :] = total
                tally(0, total * branch[0, rows, :].astype(f32))
                gba[rows, :] = (gate_a * total).astype(bf16)

        @pl.loop(0, width // 256)
        def _(step):
            lanes = row_block(step, 256)
            acc_out[:, lanes] += dot_tn(att[0], gba[:, lanes])
            grad_att[0, :, lanes] = dot_nt(gba[...], weights_q[lanes, GROUP:]).astype(bf16)

    @pl.when(unit == pl.num_programs(0) - 1)
    def _():
        dout_o[...] = acc_out[...].astype(bf16)


def backward_heads(meta, qkv, grad_att, prob, mix, dout, dqkv_o, grad_o, acc):
    unit = pl.program_id(0)
    width = grad_att.shape[2]

    @pl.when(unit == 0)
    def _():
        acc[...] = jnp.zeros_like(acc)

    @pl.when(meta[unit] > 0)
    def _():
        mask = head_mask()
        low = lax.broadcasted_iota(jnp.int32, (64, 128), 1) < HEAD_DIM

        @pl.loop(0, HALF // 128)
        def _(step):
            chains = []
            for block in range(2):
                rows = row_block(2 * step + block, 64)
                for at in range(0, width, GROUP):
                    grads = grad_att[0, rows, at : at + GROUP]
                    values = spread_heads(qkv[0, rows, 2 * width + at : 2 * width + at + GROUP], mask)
                    chains.append((rows, at, grads, dot_nt(grads, values), prob[0, rows, at : at + GROUP]))
            inners = []
            for _, _, _, grad_probs, probs in chains:
                product = probs.astype(f32) * grad_probs
                high = product.astype(bf16)
                rest = (product - high.astype(f32)).astype(bf16)
                inners.append(dot(high, mask) + dot(rest, mask))
            scores = [
                (probs.astype(f32) * (grad_probs - inner)).astype(bf16)
                for (_, _, _, grad_probs, probs), inner in zip(chains, inners)
            ]
            for (rows, at, grads, _, probs), grad_scores in zip(chains, scores):
                query = qkv[0, rows, at : at + GROUP]
                keys = spread_heads(qkv[0, rows, width + at : width + at + GROUP], mask)
                dqkv_o[0, rows, at : at + GROUP] = (dot(grad_scores, keys) * 0.125).astype(bf16)
                for pair in range(2):
                    lanes = slice(128 * pair, 128 * pair + 128)
                    both = dot_tn(grad_scores[:, lanes], query[:, lanes]) * 0.125
                    to = width + at + 128 * pair
                    dqkv_o[0, rows, to : to + 128] = jnp.where(low, both[:64], both[64:]).astype(bf16)
                    both = dot_tn(probs[:, lanes], grads[:, lanes])
                    to = 2 * width + at + 128 * pair
                    dqkv_o[0, rows, to : to + 128] = jnp.where(low, both[:64], both[64:]).astype(bf16)

        @pl.loop(0, 3 * width // 256)
        def _(step):
            lanes = row_block(step, 256)
            acc[:, lanes] += dot_tn(mix[0], dqkv_o[0, :, lanes])

    @pl.when(unit == pl.num_programs(0) - 1)
    def _():
        grad_o[:, : 3 * width] = acc[...].astype(bf16)
        grad_o[:, 3 * width :] = dout[...]


def backward_tokens(
    base, meta, dqkv, x, gm, mod, taps, spots, weights_p, weights_q,
    dx_o, own_o, far_o, mod_o, dtap_o, grad_mix, hidden, grad_hidden,
):
    unit = pl.program_id(0) + base
    width = x.shape[2]

    @pl.when(pl.program_id(0) == 0)
    def _():
        dtap_o[...] = jnp.zeros_like(dtap_o)

    @pl.when(meta[unit] > 0)
    def _():
        mod_o[...] = jnp.zeros_like(mod_o)

        @pl.loop(0, width // 256)
        def _(step):
            rows = row_block(step, 256)
            total = dot_nt(dqkv[0, :, : 3 * width - GROUP], weights_p[rows, :])
            total = total + dot_nt(dqkv[0, :, 3 * width - GROUP :], weights_q[rows, :GROUP])
            grad_mix[:, rows] = total.astype(bf16).astype(f32)

        for latent in range(2):
            shift, scale = mod[0, latent, 0:1, :], 1.0 + mod[0, latent, 1:2, :]

            @pl.loop(0, 4)
            def _(step):
                rows = row_block(step, 64, latent * LATENT)
                normed, _ = norm_parts(x[0, rows, :].astype(f32))
                hidden[rows, :] = (normed * scale + shift).astype(bf16).astype(f32)

        layout = meta[meta.shape[0] // 2 + unit]
        which = jnp.where(layout == 2, 1, 0)
        narrow_grid = layout == 0
        ends = edges(narrow_grid)

        @pl.loop(0, width // 128)
        def _(step):
            lanes = row_block(step, 128)
            weights = [taps[0, tap : tap + 1, lanes] for tap in range(9)]
            for latent in range(2):
                rows = phase_rows(latent)
                grads = [grad_mix[r, lanes] for r in rows]
                found = neighbours([hidden[r, lanes] for r in rows], narrow_grid, ends)
                add_taps(dtap_o, which, lanes, found, grads)
                for r, near in zip(rows, neighbours(grads, narrow_grid, ends)):
                    grad_hidden[r, lanes] = weighted(near, weights[::-1])

        for latent in range(2):
            scale = 1.0 + mod[0, latent, 1:2, :]

            def tally(block, values):
                mod_o[0, latent, block : block + 1, :] += jnp.sum(values, axis=0, keepdims=True)

            @pl.loop(0, 4)
            def _(step):
                rows = row_block(step, 64, latent * LATENT)
                normed, inverse = norm_parts(x[0, rows, :].astype(f32))
                grads = grad_hidden[rows, :]
                tally(0, grads)
                tally(1, grads * normed)
                total = gm[0, rows, :] + norm_back(grads * scale, normed, inverse)
                dx_o[0, rows, :] = total.astype(bf16)

        put_back(dx_o, spots, own_o, far_o)


def source_places(layouts, half):
    p = jnp.arange(HALF, dtype=jnp.int32)
    latent, q = p // LATENT, p % 64
    row_parity, column_parity = (p // 128) % 2, (p // 64) % 2
    square = (2 * (q // 8) + row_parity) * GRID + 16 * latent + 2 * (q % 8) + column_parity
    low_row, wide_col = 2 * (q // 16) + row_parity, 2 * (q % 16) + column_parity
    across = (8 * latent + low_row) * GRID + wide_col
    column = 8 * latent + low_row
    own = (wide_col - 16 * half) * GRID + 16 * half + column
    other = HALF + (wide_col - 16 * (1 - half)) * 16 + column
    downward = jnp.where(wide_col // 16 == half, own, other)
    kind = layouts[:, None]
    return jnp.where(kind == 0, square, jnp.where(kind == 1, across, downward))


def turned(taps):
    return taps.reshape(taps.shape[:-2] + (3, 3, taps.shape[-1])).swapaxes(-3, -2).reshape(taps.shape)


def tap_sum(parts):
    summed = parts.reshape(2, 9, 8, -1).sum(2)
    return summed[0] + turned(summed[1])


def bit_of(index, bit):
    return (index // bit) % 2


def swapped(values, bit):
    count = lax.axis_size("wide")
    return lax.ppermute(values, "wide", [(i, i ^ bit) for i in range(count)])


def bits_of(count):
    return [1 << b for b in range(count.bit_length() - 1)]


def ordered(values, other, bit):
    low = bit_of(lax.axis_index("wide"), bit) == 0
    return jnp.where(low, values, other), jnp.where(low, other, values)


def gathered_rows(values, crosswise):
    count = lax.axis_size("wide")
    far_bits = bits_of(count)[2:]

    def direct(v):
        found = {0: v}
        for mask in range(4, count, 4):
            found[mask] = swapped(v, mask)
        for bit in far_bits:
            found = {
                mask: jnp.stack(ordered(found[mask], found[mask | bit], bit), 0)
                for mask in found if not mask & bit
            }
        return found[0].reshape((count // 4,) + v.shape)

    if crosswise:
        near = direct(jnp.stack(ordered(values, swapped(values, 2), 2)))
    else:
        far = direct(values)
        near = jnp.stack(ordered(far, swapped(far, 2), 2), 1)
    full = jnp.stack(ordered(near, swapped(near, 1), 1), 2)
    return full.reshape(count * values.shape[0], values.shape[1])


def gathered_everywhere(values):
    lane, count = lax.axis_index("narrow"), lax.axis_size("narrow")
    if count == 2:
        other = lax.ppermute(values, "narrow", [(0, 1), (1, 0)])
        values = jnp.where(lane == 0, jnp.stack([values, other]), jnp.stack([other, values]))
    else:
        values = lax.all_gather(values, "narrow", axis=0)
    values = values[None]
    for bit in reversed(bits_of(lax.axis_size("wide"))):
        values = jnp.stack(ordered(values, swapped(values, bit), bit), 1)
        values = values.reshape((-1,) + values.shape[2:])
    return values


def after(value, *earlier):
    return lax.optimization_barrier((value, *earlier))[0]


def narrow_sum(values):
    count = lax.axis_size("narrow")
    if count == 2:
        other = lax.ppermute(values, "narrow", [(0, 1), (1, 0)])
        return values.astype(f32) + other.astype(f32)
    return lax.psum(values, "narrow").astype(f32)


def body(
    tokens, cotangent, conv_attn, qkv_weight, out_weight, up_weight, conv_ffn, down_weight,
    ada_weight, class_table, timesteps, labels, layout, counts,
):
    slots, local_tokens, D = tokens.shape
    owners, narrow = lax.axis_size("wide"), lax.axis_size("narrow")
    owner, lane = lax.axis_index("wide"), lax.axis_index("narrow")
    shard = D // owners
    half = lane % 2
    spread = narrow // 2
    balanced = narrow == 2 and slots == 4
    units = 3 if balanced else slots // spread
    hidden_width = up_weight.shape[1]
    columns = hidden_width // PARTS

    loads = (counts > 0).astype(jnp.int32).reshape(owners, slots)

    def all_units(values):
        values = values.reshape((owners, slots) + values.shape[1:])
        if balanced:
            idle = (loads.sum(1) == 0).reshape((owners,) + (1,) * (values.ndim - 2))
            other = jnp.roll(values[:, 3], owners // 2, axis=0)
            return jnp.stack([values[:, 0], values[:, 1], jnp.where(idle, other, values[:, 2])], 1)
        return values

    def my_units(values):
        values = lax.dynamic_index_in_dim(all_units(values), owner, 0, keepdims=False)
        if balanced:
            return values
        values = values.reshape((units, spread) + values.shape[1:])
        return lax.dynamic_index_in_dim(values, lane // 2, 1, keepdims=False)

    def latent_rows(values):
        values = all_units(values)
        if balanced:
            return values.reshape(owners, units, 2, 2).transpose(0, 2, 1, 3).reshape(-1)
        return values.reshape(owners, units, spread, 2, 2).transpose(0, 2, 3, 1, 4).reshape(-1)

    count_float = counts.astype(f32)
    scales = count_float * float(counts.shape[0]) / jnp.sum(count_float)
    my_layout, my_scale = my_units(layout), my_units(scales)
    active = my_units(counts) > 0
    meta = jnp.concatenate([active.astype(jnp.int32), my_layout])
    places = source_places(my_layout, half)

    half_width = D // 2
    my_columns = owner * shard + jnp.arange(shard, dtype=jnp.int32)
    freqs = jnp.exp(-math.log(10000.0) * (my_columns % half_width).astype(f32) / half_width)
    angles = latent_rows(timesteps)[:, None].astype(f32) * freqs
    label_hot = (latent_rows(labels)[:, None] == jnp.arange(class_table.shape[0], dtype=jnp.int32)).astype(bf16)
    embed = jnp.where(my_columns < half_width, jnp.cos(angles), jnp.sin(angles)) + dot(label_hot, class_table)
    activ, silu_back = jax.vjp(jax.nn.silu, embed)
    act_low = activ.astype(bf16)
    mine = lax.dynamic_index_in_dim(act_low.reshape(owners, narrow, units * 2, shard), lane, 1, keepdims=False)
    partial_mod = dot(mine.reshape(-1, shard), ada_weight).astype(bf16).reshape(owners, units * 2, -1)
    both_taps = jnp.concatenate([conv_attn, conv_ffn], 1).reshape(-1)
    tap_size = both_taps.shape[0]
    tap_lanes = -(-tap_size // (units * 2 * 128)) * 128
    both_taps = jnp.pad(both_taps, (0, units * 2 * tap_lanes - tap_size)).reshape(1, units * 2, tap_lanes)
    sent = jnp.concatenate([partial_mod, jnp.broadcast_to(both_taps, (owners, units * 2, tap_lanes))], 2)
    arrived = lax.all_to_all(sent, "wide", 0, 0, tiled=True)
    modulation = jnp.sum(arrived[:, :, : 6 * D].astype(f32), axis=0).reshape(units, 2, 6, D)
    both_taps = arrived[:, :, 6 * D :].reshape(owners, -1)[:, :tap_size].reshape(owners, 9, -1).astype(f32)
    conv_one = both_taps[:, :, :shard].swapaxes(0, 1).reshape(9, D)
    conv_two = both_taps[:, :, shard:].swapaxes(0, 1).reshape(9, hidden_width)
    weight_row = jnp.broadcast_to(my_scale[:, None, None, None], (units, 2, 1, D))
    mod = jnp.concatenate([modulation, weight_row], 2)

    split = 3 * D - GROUP
    weights_p = gathered_rows(qkv_weight[:, :split], False)
    weights_q = gathered_rows(jnp.concatenate([qkv_weight[:, split:], out_weight], 1), True)
    up_full = lax.all_gather(up_weight, "wide", axis=0, tiled=True)
    down_full = lax.all_gather(down_weight, "wide", axis=0, tiled=True)

    def unit_taps(taps):
        return jnp.where((my_layout == 2)[:, None, None], turned(taps), taps)

    taps_one, taps_two = unit_taps(conv_one), unit_taps(conv_two)

    params = pltpu.CompilerParams(vmem_limit_bytes=VMEM_BYTES, dimension_semantics=("arbitrary",))
    any_space = pl.BlockSpec(memory_space=pl.ANY)

    def per_unit(*shape, base=0):
        return pl.BlockSpec((1,) + shape, lambda i, meta: (i + base,) + (0,) * len(shape))

    def whole(*shape):
        return pl.BlockSpec(shape, lambda i, meta: (0,) * len(shape), pipeline_mode=pl.Buffered(1))

    def struct(*shape, kind=bf16):
        return jax.ShapeDtypeStruct(shape, kind)

    def call(kernel, name, count, flags, ins, in_specs, outs, out_specs, scratch=(), flops=0, before=()):
        aliases = {1 + len(ins) + i: i for i in range(len(before))}
        extra = len(before)

        def run(meta, *refs):
            kept = refs[: len(ins)] + refs[len(ins) + extra :]
            kernel(meta, *kept)

        return pl.pallas_call(
            run,
            grid_spec=pltpu.PrefetchScalarGridSpec(
                num_scalar_prefetch=1, grid=(count,), in_specs=list(in_specs) + [any_space] * extra,
                out_specs=out_specs, scratch_shapes=list(scratch),
            ),
            out_shape=outs,
            input_output_aliases=aliases,
            compiler_params=params,
            cost_estimate=pl.CostEstimate(flops=int(flops * count), bytes_accessed=int(8e6 * count), transcendentals=0),
            name=name,
        )(flags, *ins, *before)

    tokens_shape = (HALF, D)

    def arranged(base, count, tok, far, far_base, where, flags):
        return call(
            partial(arrange, base), "arrange", count, flags, [tok, far, where[:, :, None]],
            [per_unit(*tokens_shape, base=base), per_unit(LATENT, D, base=far_base), per_unit(HALF, 1, base=base)],
            struct(count, *tokens_shape), per_unit(*tokens_shape), flops=2e9,
        )

    if balanced:
        own_layout = lax.dynamic_slice_in_dim(layout, owner * slots, slots)
        own_active = lax.dynamic_slice_in_dim(counts, owner * slots, slots) > 0
        own_places = source_places(own_layout, half)
        own_flags = jnp.concatenate([own_active.astype(jnp.int32), own_layout])
        swap = [(0, 1), (1, 0)]
        partner = [(i, (i + owners // 2) % owners) for i in range(owners)]

        def for_other_half(first, count):
            parts = [v.reshape(slots, 16, GRID, D)[first : first + count] for v in (tokens, cotangent)]
            parts = [lax.dynamic_slice_in_dim(v, 16 * (1 - half), 16, axis=2) for v in parts]
            return lax.ppermute(jnp.concatenate(parts, 0).reshape(-1, LATENT, D), "narrow", swap)

        far_last, far_first = for_other_half(3, 1), for_other_half(0, 3)
        own_tok, own_cot = [v.reshape(slots, HALF, D) for v in (tokens, cotangent)]
        x_last = arranged(3, 1, own_tok, far_last, 0, own_places, own_flags)
        x_other = lax.ppermute(x_last, "wide", partner)
        cot_last = arranged(3, 1, own_cot, far_last, 1, own_places, own_flags)
        cot_other = lax.ppermute(cot_last, "wide", partner)
        x_own = arranged(0, 3, own_tok, far_first, 0, own_places, own_flags)
        cot_own = arranged(0, 3, own_cot, far_first, 3, own_places, own_flags)
        cots, cot_specs = [cot_own, cot_other], [per_unit(*tokens_shape), whole(1, *tokens_shape)]
    else:

        def to_units(values):
            full = lax.all_gather(values, "narrow", axis=1, tiled=True)
            full = full.reshape(units, spread, 2, 16, GRID, D)
            full = lax.dynamic_index_in_dim(full, lane // 2, 1, keepdims=False)
            here = lax.dynamic_index_in_dim(full, half, 1, keepdims=False)
            far = lax.dynamic_index_in_dim(full, 1 - half, 1, keepdims=False)
            far = lax.dynamic_slice_in_dim(far, 16 * half, 16, axis=2)
            return arranged(0, units, here.reshape(units, HALF, D), far.reshape(units, LATENT, D), 0, places, meta)

        x_own = to_units(tokens)
        cot_own = to_units(cotangent)
        cots, cot_specs = [cot_own], [per_unit(*tokens_shape)]

    unit_values = struct(units, *tokens_shape)
    unit_floats = struct(units, *tokens_shape, kind=f32)

    def mix_call(base, count, taken, before):
        spec = per_unit(*tokens_shape, base=base)
        ins, specs = [x_own], [spec]
        if taken:
            ins, specs = ins + [x_other], specs + [whole(1, *tokens_shape)]
        return call(
            partial(mix_tokens, base, taken), "mix_tokens", count, meta, ins + [mod, taps_one],
            specs + [per_unit(2, 7, D, base=base), per_unit(9, D, base=base)],
            [unit_values, unit_values], [spec, spec], [pltpu.VMEM(tokens_shape, f32)], 3e9, before,
        )

    def attend_call(base, count, before):
        spec = per_unit(*tokens_shape, base=base)
        return call(
            partial(attend, base), "attend", count, meta, [x, mixed, mod, weights_p, weights_q],
            [spec, spec, per_unit(2, 7, D, base=base), whole(D, split), whole(D, GROUP + D)],
            [struct(units, HALF, 3 * D), unit_values, unit_values, unit_values, unit_floats, unit_values],
            [per_unit(HALF, 3 * D, base=base)] + [spec] * 5, (), 8e9, before,
        )

    if balanced:
        x, mixed = mix_call(0, 2, False, ())
        front = attend_call(0, 2, ())
        x, mixed = mix_call(2, 1, True, (x, mixed))
        front = attend_call(2, 1, front)
    else:
        x, mixed = mix_call(0, units, False, ())
        front = attend_call(0, units, ())
    projected, probs, attended, branch, middle, ffn_in = front

    slot_pair = [pltpu.VMEM((HALF, 256), kind) for kind in (f32, f32, f32, f32, bf16, bf16, bf16, bf16)]
    work = [pltpu.VMEM((D, HALF), bf16), pltpu.VMEM((D, HALF), bf16)]
    work += [pltpu.VMEM((D, columns), f32), pltpu.VMEM((D, columns), f32)]
    unit_spec = per_unit(*tokens_shape)
    tap_grad, tap_spec = struct(2, 72, columns, kind=f32), whole(2, 72, columns)
    spots = places[:, None, :]

    def of_part(part):
        specs = [
            pl.BlockSpec((D, columns), lambda i, meta: (0, part), pipeline_mode=pl.Buffered(1)),
            pl.BlockSpec((columns, D), lambda i, meta: (part, 0), pipeline_mode=pl.Buffered(1)),
            pl.BlockSpec((1, 9, columns), lambda i, meta: (i, 0, part)),
        ]
        return [up_full, down_full, taps_two], specs

    ins, specs = of_part(0)
    gbb, branch_b, grad_ffn, up_grad, down_grad, ffn_taps_0 = call(
        partial(feed_forward, 0, shard, balanced), "feed_forward", units, meta, cots + [mod, ffn_in] + ins,
        cot_specs + [per_unit(2, 7, D), unit_spec] + specs,
        [unit_values, unit_floats, unit_floats, struct(D, columns), struct(D // 2, hidden_width), tap_grad],
        [unit_spec, unit_spec, unit_spec, whole(D, columns), whole(D // 2, hidden_width), tap_spec],
        work + slot_pair, 16e9,
    )

    def owner_sum(values):
        return lax.psum_scatter(values, "wide", scatter_dimension=0, tiled=True)

    sums_up = owner_sum(up_grad)
    ins, specs = of_part(1)
    grad_ffn, y_units, y_own, y_far, ffn_grad, ffn_taps_1, branch_b = call(
        partial(feed_forward, 1, shard, balanced), "feed_forward", units, meta,
        [gbb, ffn_in] + ins + [branch_b, grad_ffn, middle, mod, spots, down_grad],
        [unit_spec, unit_spec] + specs
        + [unit_spec, unit_spec, unit_spec, per_unit(2, 7, D), per_unit(1, HALF), whole(D // 2, hidden_width)],
        [unit_floats, unit_values, unit_values, struct(units, LATENT, D), struct(D, columns + hidden_width),
         tap_grad, unit_floats],
        [unit_spec, unit_spec, unit_spec, per_unit(LATENT, D), whole(D, columns + hidden_width), tap_spec, unit_spec],
        work + slot_pair, 17e9,
    )
    grad_ffn, sums_up = lax.optimization_barrier((grad_ffn, sums_up))
    sums_ffn = owner_sum(ffn_grad)

    grad_mid, grad_att, mod_late, out_grad = call(
        partial(backward_middle, balanced), "backward_middle", units, meta,
        cots + [branch_b, grad_ffn, middle, branch, attended, mod, weights_q],
        cot_specs + [unit_spec] * 5 + [per_unit(2, 7, D), whole(D, GROUP + D)],
        [unit_floats, unit_values, struct(units, 2, 4, D, kind=f32), struct(D, D)],
        [unit_spec, unit_spec, per_unit(2, 4, D), whole(D, D)],
        [pltpu.VMEM(tokens_shape, bf16), pltpu.VMEM((D, D), f32)], 4e9,
    )
    head_grads, attn_grad = call(
        backward_heads, "backward_heads", units, meta, [projected, grad_att, probs, mixed, out_grad],
        [per_unit(HALF, 3 * D), unit_spec, unit_spec, unit_spec, whole(D, D)],
        [struct(units, HALF, 3 * D), struct(D, 4 * D)], [per_unit(HALF, 3 * D), whole(D, 4 * D)],
        [pltpu.VMEM((D, 3 * D), f32)], 12e9,
    )

    def tokens_call(base, count, before):
        spec = per_unit(*tokens_shape, base=base)
        return call(
            partial(backward_tokens, base), "backward_tokens", count, meta,
            [head_grads, x, grad_mid, mod, taps_one, spots, weights_p, weights_q],
            [per_unit(HALF, 3 * D, base=base), spec, spec, per_unit(2, 7, D, base=base), per_unit(9, D, base=base), per_unit(1, HALF, base=base),
             whole(D, split), whole(D, GROUP + D)],
            [unit_values, unit_values, struct(units, LATENT, D), struct(units, 2, 2, D, kind=f32),
             struct(2, 72, D, kind=f32)],
            [spec, spec, per_unit(LATENT, D, base=base), per_unit(2, 2, D, base=base), whole(2, 72, D)],
            [pltpu.VMEM(tokens_shape, f32)] * 3, 6e9, before,
        )

    def finished(pieces):
        pairs = []
        for own, far in pieces:
            count = own.shape[0]
            far = lax.ppermute(far, "narrow", swap).reshape(count, 16, 16, D)
            empty = jnp.zeros_like(far)
            side = jnp.where(half == 0, jnp.concatenate([empty, far], 2), jnp.concatenate([far, empty], 2))
            pairs.append(own.reshape(count, 16, GRID, D) + side)
        total = jnp.concatenate(pairs, 0)
        return jnp.where(own_active[:, None, None, None], total, 0.0).reshape(slots, local_tokens, D)

    def returned(values, later):
        back = lax.ppermute(values, "wide", partner)
        return call(
            place_back, "place_back", 1, after(own_flags, later), [back, own_places[3:, None, :]],
            [unit_spec, per_unit(1, HALF)], [struct(1, *tokens_shape), struct(1, LATENT, D)],
            [unit_spec, per_unit(LATENT, D)], (), 2e9,
        )

    def rows_back(own, far):
        own = jnp.where(active[:, None, None], own, 0.0).reshape(units, 1, 16, GRID, D)
        far = jnp.where(active[:, None, None], far, 0.0).reshape(units, 1, 16, 16, D)
        full = lax.dynamic_update_slice_in_dim(jnp.zeros((units, 2, 16, GRID, D), bf16), own, half, 1)
        other = lax.dynamic_update_slice_in_dim(jnp.zeros((units, 1, 16, GRID, D), bf16), far, 16 * half, 3)
        full = lax.dynamic_update_slice_in_dim(full, other, 1 - half, 1).reshape(units, 1, 2 * HALF, D)
        full = lax.dynamic_update_slice_in_dim(jnp.zeros((units, spread, 2 * HALF, D), bf16), full, lane // 2, 1)
        return lax.psum_scatter(full.reshape(slots, 2 * HALF, D), "narrow", scatter_dimension=1, tiled=True)

    if balanced:
        dx_units, dx_own, dx_far, mod_early, taps_a = tokens_call(2, 1, ())
        y_back = returned(y_units[2:], dx_units)
        dx_last = dx_units[2:]
        head_grads, sums_ffn = lax.optimization_barrier((head_grads, sums_ffn))
        attn_sums = owner_sum(after(attn_grad, sums_ffn))
        _, dx_own, dx_far, mod_early, taps_b = tokens_call(0, 2, (dx_units, dx_own, dx_far, mod_early))
        x_back = returned(dx_last, mod_early)
        work_y = finished([(y_own, y_far), y_back])
        work_x = finished([(dx_own, dx_far), x_back])
        conv_one_grad = tap_sum(taps_a) + tap_sum(taps_b)
    else:
        work_y = rows_back(y_own, y_far)
        dx_units, dx_own, dx_far, mod_early, taps_a = tokens_call(0, units, ())
        attn_sums = owner_sum(after(attn_grad, sums_ffn))
        work_x = rows_back(dx_own, dx_far)
        conv_one_grad = tap_sum(taps_a)

    attn_final = narrow_sum(attn_sums)
    final_qkv, final_out = attn_final[:, : 3 * D], attn_final[:, 3 * D :]
    ffn_final = narrow_sum(sums_ffn)
    final_up = jnp.concatenate([narrow_sum(sums_up), ffn_final[:, :columns]], 1)
    final_down = ffn_final[:, columns:].reshape(shard, -1, D).swapaxes(0, 1).reshape(-1, D)
    conv_two_grad = jnp.concatenate([tap_sum(ffn_taps_0), tap_sum(ffn_taps_1)], 1)
    conv_grads = jnp.concatenate(
        [conv_one_grad.reshape(9, owners, shard), conv_two_grad.reshape(9, owners, -1)], 2
    ).swapaxes(0, 1)
    conv_grads = jnp.broadcast_to(conv_grads[:, None], (owners, narrow) + conv_grads.shape[1:])
    conv_grads = conv_grads.reshape((owners * narrow,) + conv_grads.shape[2:])
    conv_sums = jnp.sum(lax.all_to_all(conv_grads, ("wide", "narrow"), 0, 0, tiled=True), axis=0)

    mod_grads = jnp.concatenate([mod_early, mod_late], 2)
    mod_grads = jnp.where(active[:, None, None, None], mod_grads, 0.0).astype(bf16)
    mod_all = gathered_everywhere(mod_grads.reshape(units * 2, 6 * D)).reshape(-1, 6 * D)
    grad_ada = dot_tn(act_low, mod_all)
    grad_embed = silu_back(dot_nt(mod_all, ada_weight))[0]
    grad_table = dot_tn(label_hot, grad_embed.astype(bf16))
    return (
        work_y, work_x, conv_sums[:, :shard], final_qkv, final_out, final_up,
        conv_sums[:, shard:], final_down, grad_ada, grad_table,
    )


def solution(mesh):
    rows = P("wide", None)
    columns = P(None, "wide")
    canvases = P("wide", "narrow", None)
    return jax.shard_map(
        body,
        mesh=mesh,
        in_specs=(canvases, canvases, columns, rows, rows, rows, columns, rows, rows, columns, P(), P(), P(), P()),
        out_specs=(canvases, canvases, columns, rows, rows, rows, columns, rows, rows, columns),
        check_vma=False,
    )
```

```python
from functools import partial
import math

import jax
import jax.numpy as jnp
import numpy as np
from jax import lax
from jax.experimental import pallas as pl
from jax.experimental.pallas import tpu as pltpu
from jax.sharding import PartitionSpec as P

HEAD_DIM = 64
GRID = 32
LATENT = 256
HALF = 2 * LATENT
PARTS = 2
ROWS = 128
GROUP = 256
VMEM_BYTES = 67000000

norm_eps = 1e-06
bf16 = jnp.bfloat16
f32 = jnp.float32


def dot(a, b):
    return lax.dot_general(a, b, (((1,), (0,)), ((), ())), preferred_element_type=f32)


def dot_nt(a, b):
    return lax.dot_general(a, b, (((1,), (1,)), ((), ())), preferred_element_type=f32)


def dot_tn(a, b):
    return lax.dot_general(a, b, (((0,), (0,)), ((), ())), preferred_element_type=f32)


def norm_parts(values):
    centred = values - jnp.mean(values, axis=-1, keepdims=True)
    inverse = lax.rsqrt(jnp.mean(centred * centred, axis=-1, keepdims=True) + norm_eps)
    return centred * inverse, inverse


def norm_back(grad_normed, normed, inverse):
    return inverse * (
        grad_normed
        - jnp.mean(grad_normed, axis=-1, keepdims=True)
        - normed * jnp.mean(grad_normed * normed, axis=-1, keepdims=True)
    )


def edges(narrow_grid):
    place = lax.broadcasted_iota(jnp.int32, (64, 128), 0)
    place = jnp.where(narrow_grid, place % 8, place % 16)
    return place == 0, place == jnp.where(narrow_grid, 7, 15)


def neighbours(blocks, narrow_grid, ends):
    first, last = ends
    gap = jnp.zeros((16, 128), blocks[0].dtype)

    def earlier(v):
        padded = jnp.concatenate([gap, v], 0)
        return jnp.where(narrow_grid, padded[8:72], padded[:64])

    def later(v):
        padded = jnp.concatenate([v, gap], 0)
        return jnp.where(narrow_grid, padded[8:72], padded[16:80])

    columns, moved = [], []
    for row_parity in range(2):
        even, odd = blocks[2 * row_parity], blocks[2 * row_parity + 1]
        before = jnp.where(first, 0.0, pltpu.roll(odd, 1, 0))
        after = jnp.where(last, 0.0, pltpu.roll(even, 63, 0))
        shift = later if row_parity == 0 else earlier
        b, e, o, a = [shift(v) for v in (before, even, odd, after)]
        columns.append(((before, even, odd), (even, odd, after)))
        moved.append(((b, e, o), (e, o, a)))
    found = []
    for row_parity in range(2):
        for parity in range(2):
            same, other, far = columns[row_parity][parity], columns[1 - row_parity][parity], moved[1 - row_parity][parity]
            found.append((*far, *same, *other) if row_parity == 0 else (*other, *same, *far))
    return found


def weighted(found, taps):
    total = found[0] * taps[0]
    for tap in range(1, 9):
        total = total + found[tap] * taps[tap]
    return total


def phase_rows(latent):
    return [slice(latent * LATENT + 64 * phase, latent * LATENT + 64 * phase + 64) for phase in range(4)]


def add_taps(store, which, lanes, found, grads):
    for tap in range(9):
        total = found[0][tap] * grads[0]
        for phase in range(1, 4):
            total = total + found[phase][tap] * grads[phase]
        store[which, 8 * tap : 8 * tap + 8, lanes] += jnp.sum(total.reshape(8, 8, total.shape[1]), axis=0)


def finish_taps(store, out):
    for tap in range(9):
        other = 3 * (tap % 3) + tap // 3
        total = store[0, 8 * tap : 8 * tap + 8, :] + store[1, 8 * other : 8 * other + 8, :]
        out[tap : tap + 1, :] = jnp.sum(total, axis=0, keepdims=True)


def head_mask():
    rows = lax.broadcasted_iota(jnp.int32, (GROUP, GROUP), 0) // HEAD_DIM
    cols = lax.broadcasted_iota(jnp.int32, (GROUP, GROUP), 1) // HEAD_DIM
    return jnp.where(rows == cols, 1.0, 0.0).astype(bf16)


def spread_heads(values, mask):
    return jnp.concatenate([values] * 4, 0) * mask


def head_max(values):
    low = lax.broadcasted_iota(jnp.int32, values.shape, 1) < HEAD_DIM
    lower = jnp.max(jnp.where(low, values, -jnp.inf), axis=-1, keepdims=True)
    upper = jnp.max(jnp.where(low, -jnp.inf, values), axis=-1, keepdims=True)
    return jnp.where(low, lower, upper)


def row_block(step, size, start=0):
    return pl.ds(pl.multiple_of(start + step * size, size), size)


def arrange(base, meta, tok, far_tok, places, out):
    @pl.when(meta[pl.program_id(0) + base] > 0)
    def _():
        @pl.loop(0, HALF // ROWS)
        def _(step):
            rows = row_block(step, ROWS)
            source = lax.broadcasted_iota(jnp.int32, (ROWS, 3 * LATENT), 1)
            hot = jnp.where(places[0, rows, :] == source, 1.0, 0.0).astype(bf16)
            values = dot(hot[:, :HALF], tok[0]) + dot(hot[:, HALF:], far_tok[0])
            out[0, rows, :] = values.astype(bf16)


def put_back(result, spots, own, far):
    for step in range(3 * LATENT // ROWS):
        target = lax.broadcasted_iota(jnp.int32, (ROWS, HALF), 0) + step * ROWS
        hot = jnp.where(spots[0] == target, 1.0, 0.0).astype(bf16)
        values = dot(hot, result[0]).astype(bf16)
        if step * ROWS < HALF:
            own[0, step * ROWS : (step + 1) * ROWS, :] = values
        else:
            far[0, step * ROWS - HALF : (step + 1) * ROWS - HALF, :] = values


def place_back(meta, result, spots, own, far):
    @pl.when(meta[3] > 0)
    def _():
        put_back(result, spots, own, far)


def mix_tokens(base, taken, meta, *refs):
    if taken:
        x, other, mod, taps, x_o, mix_o, hidden = refs
    else:
        x, mod, taps, x_o, mix_o, hidden = refs
    unit = pl.program_id(0) + base

    @pl.when(meta[unit] > 0)
    def _():
        for latent in range(2):
            shift, scale = mod[0, latent, 0:1, :], 1.0 + mod[0, latent, 1:2, :]

            @pl.loop(0, LATENT // ROWS)
            def _(step):
                rows = row_block(step, ROWS, latent * LATENT)
                values = x[0, rows, :].astype(f32)
                if taken:
                    values = jnp.where(meta[0] > 0, values, other[0, rows, :].astype(f32))
                x_o[0, rows, :] = values.astype(bf16)
                normed, _ = norm_parts(values)
                hidden[rows, :] = (normed * scale + shift).astype(bf16).astype(f32)

        narrow_grid = meta[meta.shape[0] // 2 + unit] == 0
        ends = edges(narrow_grid)

        @pl.loop(0, x.shape[2] // 128)
        def _(step):
            lanes = row_block(step, 128)
            weights = [taps[0, tap : tap + 1, lanes] for tap in range(9)]
            for latent in range(2):
                found = neighbours([hidden[r, lanes] for r in phase_rows(latent)], narrow_grid, ends)
                for rows, near in zip(phase_rows(latent), found):
                    mix_o[0, rows, lanes] = weighted(near, weights).astype(bf16)


def attend(base, meta, x, mix, mod, weights, qkv_o, prob_o, att_o, branch_o, mid_o, ffn_o):
    unit = pl.program_id(0) + base
    width = x.shape[2]
    groups = width // GROUP

    @pl.when(meta[unit] > 0)
    def _():
        @pl.loop(0, 3 * width // 256)
        def _(step):
            lanes = row_block(step, 256)
            qkv_o[0, :, lanes] = dot(mix[0], weights[:, lanes]).astype(bf16)

        mask = head_mask()

        @pl.loop(0, HALF // 128)
        def _(step):
            chains = []
            for block in range(2):
                rows = row_block(step * 2 + block, 64)
                for group in range(groups):
                    at = GROUP * group
                    keys = spread_heads(qkv_o[0, rows, width + at : width + at + GROUP], mask)
                    chains.append((rows, group, dot_nt(qkv_o[0, rows, at : at + GROUP], keys) * 0.125))
            raised = [
                jnp.concatenate([jnp.exp(s[:, c : c + 128] - head_max(s[:, c : c + 128])) for c in (0, 128)], 1)
                for _, _, s in chains
            ]
            totals = [dot(e.astype(bf16), mask) for e in raised]
            for (rows, group, _), e, total in zip(chains, raised, totals):
                probs = (e / total).astype(bf16)
                at = GROUP * group
                values = spread_heads(qkv_o[0, rows, 2 * width + at : 2 * width + at + GROUP], mask)
                prob_o[0, rows, at : at + GROUP] = probs
                att_o[0, rows, at : at + GROUP] = dot(probs, values).astype(bf16)

        for latent in range(2):
            gate_a = mod[0, latent, 2:3, :]
            shift, scale = mod[0, latent, 3:4, :], 1.0 + mod[0, latent, 4:5, :]

            @pl.loop(0, LATENT // ROWS)
            def _(step):
                rows = row_block(step, ROWS, latent * LATENT)
                branch = dot(att_o[0, rows, :], weights[:, 3 * width :])
                branch_o[0, rows, :] = branch.astype(bf16)
                middle = x[0, rows, :].astype(f32) + gate_a * branch
                mid_o[0, rows, :] = middle
                normed, _ = norm_parts(middle)
                ffn_o[0, rows, :] = (normed * scale + shift).astype(bf16)


def feed_forward(part, taken, meta, *refs):
    if part == 0:
        if taken:
            cot, other, mod, ffn, weights, taps, *refs = refs
        else:
            cot, mod, ffn, weights, taps, *refs = refs
        gbb_o, bb_o, gf_o, grad_o, tap_o, *refs = refs
        gbb = gbb_o
    else:
        gbb, ffn, weights, taps, bb_i, gf_i, mid, mod, spots, tap_i, *refs = refs
        gf_o, y_o, own_o, far_o, grad_o, tap_o, bb_o, *refs = refs
    ffn_t, gbb_t, acc_up, acc_down, dtap, *slots = refs
    unit = pl.program_id(0)
    width = ffn.shape[2]
    columns = taps.shape[2]
    items = columns // 256
    per_block = width // 256

    @pl.when(unit == 0)
    def _():
        acc_up[...] = jnp.zeros_like(acc_up)
        acc_down[...] = jnp.zeros_like(acc_down)
        dtap[...] = jnp.zeros_like(dtap)

    @pl.when(meta[unit] > 0)
    def _():
        if part == 0:
            for latent in range(2):
                gate, weight = mod[0, latent, 5:6, :], mod[0, latent, 6:7, :]

                @pl.loop(0, LATENT // 64)
                def _(step):
                    rows = row_block(step, 64, latent * LATENT)
                    grads = cot[0, rows, :].astype(f32)
                    if taken:
                        from_other = jnp.logical_and(unit == 2, meta[0] == 0)
                        grads = jnp.where(from_other, other[0, rows, :].astype(f32), grads)
                    gbb_o[0, rows, :] = (gate * (grads * weight)).astype(bf16)

        ffn_t[...] = ffn[0].T
        gbb_t[...] = gbb[0].T
        layout = meta[meta.shape[0] // 2 + unit]
        which = jnp.where(layout == 2, 1, 0)
        narrow_grid = layout == 0
        ends = edges(narrow_grid)
        uses = [slots[i::2] for i in range(2)]
        uses[1][2][...] = jnp.zeros_like(uses[1][2])
        uses[1][3][...] = jnp.zeros_like(uses[1][3])
        root = math.sqrt(2.0 / math.pi)

        @pl.loop(0, HALF // 128)
        def _(step):
            rows = row_block(step, 128)
            if part == 0:
                bb_o[0, rows, :] = jnp.zeros((128, width), f32)
                gf_o[0, rows, :] = jnp.zeros((128, width), f32)
            else:
                bb_o[0, rows, :] = bb_i[0, rows, :]
                gf_o[0, rows, :] = gf_i[0, rows, :]

        def down_rows(item):
            block = item // per_block
            return row_block(item - block * per_block, 256), row_block(block, width, columns)

        def project(item, use):
            upward, grad_act = use[0], use[1]
            rows, lanes = down_rows(item)
            upward[...] = dot(ffn[0], weights[:, row_block(item, 256)]).astype(bf16).astype(f32)
            grad_act[...] = dot_nt(gbb[0], weights[rows, lanes])

        def collect(item, use):
            act, grad_up = use[2], use[3]
            rows, lanes = down_rows(item)
            here = row_block(item, 256)
            bb_o[0] += dot(act[...], weights[rows, lanes])
            gf_o[0] += dot_nt(grad_up[...], weights[:, here])
            acc_up[:, here] += dot(ffn_t[...], grad_up[...])
            acc_down[:, here] += dot(gbb_t[...], act[...])

        def convolve(item, use):
            upward, grad_act, act, grad_up = use
            for side in range(2):
                cols = slice(128 * side, 128 * side + 128)
                lanes = row_block(2 * item + side, 128)
                taken_taps = [taps[0, tap : tap + 1, lanes] for tap in range(9)]
                for latent in range(2):
                    rows = phase_rows(latent)
                    found = neighbours([upward[r, cols] for r in rows], narrow_grid, ends)
                    grads = []
                    for r, near in zip(rows, found):
                        spread = weighted(near, taken_taps)
                        square = spread * spread
                        bent = jnp.tanh(spread * (root + root * 0.044715 * square))
                        half = 0.5 + 0.5 * bent
                        act[r, cols] = (spread * half).astype(bf16)
                        slope = half + (0.5 * spread) * (1.0 - bent * bent) * (
                            root + 3.0 * root * 0.044715 * square
                        )
                        grads.append((grad_act[r, cols] * slope).astype(bf16).astype(f32))
                    add_taps(dtap, which, lanes, found, grads)
                    for r, near in zip(rows, neighbours(grads, narrow_grid, ends)):
                        grad_up[r, cols] = weighted(near, taken_taps[::-1]).astype(bf16)

        project(0, uses[0])

        @pl.loop(0, items // 2)
        def _(pair):
            for side in range(2):
                item = 2 * pair + side
                convolve(item, uses[side])
                project(jnp.minimum(item + 1, items - 1), uses[1 - side])
                collect(jnp.maximum(item - 1, 0), uses[1 - side])

        collect(items - 1, uses[1])

        if part == PARTS - 1:
            for latent in range(2):
                gate = mod[0, latent, 5:6, :]

                @pl.loop(0, LATENT // 64)
                def _(step):
                    rows = row_block(step, 64, latent * LATENT)
                    y_o[0, rows, :] = (mid[0, rows, :] + gate * bb_o[0, rows, :]).astype(bf16)

            put_back(y_o, spots, own_o, far_o)

    @pl.when(unit == pl.num_programs(0) - 1)
    def _():
        finish_taps(dtap, tap_o)
        if part == PARTS - 1:
            rows = [t[:, at : at + width] for t in (tap_i, tap_o) for at in range(0, columns, width)]
            rows.append(jnp.zeros((128 - 9 * len(rows), width), f32))
            grad_o[:, 2 * columns :] = jnp.concatenate(rows, 0).T.astype(bf16)
        grad_o[:, :columns] = acc_up[...].astype(bf16)
        for at in range(0, columns, width):
            grad_o[:, columns + at : columns + at + width] = acc_down[:, at : at + width].astype(bf16).T


def backward_middle(taken, meta, *refs):
    if taken:
        cot, other, *refs = refs
    else:
        cot, *refs = refs
    bb, gf, mid, branch, att, mod, out_w, grad_mid, grad_att, mod_o, dout_o, gba, acc_out = refs
    unit = pl.program_id(0)
    width = cot.shape[2]

    @pl.when(unit == 0)
    def _():
        acc_out[...] = jnp.zeros_like(acc_out)

    @pl.when(meta[unit] > 0)
    def _():
        mod_o[...] = jnp.zeros_like(mod_o)
        for latent in range(2):
            gate_a, scale_b = mod[0, latent, 2:3, :], 1.0 + mod[0, latent, 4:5, :]
            weight = mod[0, latent, 6:7, :]

            def tally(block, values):
                mod_o[0, latent, block : block + 1, :] += jnp.sum(values, axis=0, keepdims=True)

            @pl.loop(0, 4)
            def _(step):
                rows = row_block(step, 64, latent * LATENT)
                grads = cot[0, rows, :].astype(f32)
                if taken:
                    from_other = jnp.logical_and(unit == 2, meta[0] == 0)
                    grads = jnp.where(from_other, other[0, rows, :].astype(f32), grads)
                grad_out = grads * weight
                tally(3, grad_out * bb[0, rows, :])
                grad_ffn = gf[0, rows, :]
                normed, inverse = norm_parts(mid[0, rows, :])
                tally(1, grad_ffn)
                tally(2, grad_ffn * normed)
                total = grad_out + norm_back(grad_ffn * scale_b, normed, inverse)
                grad_mid[0, rows, :] = total
                tally(0, total * branch[0, rows, :].astype(f32))
                gba[rows, :] = (gate_a * total).astype(bf16)

        @pl.loop(0, width // 256)
        def _(step):
            lanes = row_block(step, 256)
            acc_out[:, lanes] += dot_tn(att[0], gba[:, lanes])
            grad_att[0, :, lanes] = dot_nt(gba[...], out_w[lanes, :]).astype(bf16)

    @pl.when(unit == pl.num_programs(0) - 1)
    def _():
        dout_o[...] = acc_out[...].astype(bf16)


def backward_heads(meta, qkv, grad_att, prob, mix, dout, dqkv_o, grad_o, acc):
    unit = pl.program_id(0)
    width = grad_att.shape[2]

    @pl.when(unit == 0)
    def _():
        acc[...] = jnp.zeros_like(acc)

    @pl.when(meta[unit] > 0)
    def _():
        mask = head_mask()
        low = lax.broadcasted_iota(jnp.int32, (64, 128), 1) < HEAD_DIM

        @pl.loop(0, HALF // 128)
        def _(step):
            chains = []
            for block in range(2):
                rows = row_block(2 * step + block, 64)
                for at in range(0, width, GROUP):
                    grads = grad_att[0, rows, at : at + GROUP]
                    values = spread_heads(qkv[0, rows, 2 * width + at : 2 * width + at + GROUP], mask)
                    chains.append((rows, at, grads, dot_nt(grads, values), prob[0, rows, at : at + GROUP]))
            inners = []
            for _, _, _, grad_probs, probs in chains:
                product = probs.astype(f32) * grad_probs
                high = product.astype(bf16)
                rest = (product - high.astype(f32)).astype(bf16)
                inners.append(dot(high, mask) + dot(rest, mask))
            scores = [
                (probs.astype(f32) * (grad_probs - inner)).astype(bf16)
                for (_, _, _, grad_probs, probs), inner in zip(chains, inners)
            ]
            for (rows, at, grads, _, probs), grad_scores in zip(chains, scores):
                query = qkv[0, rows, at : at + GROUP]
                keys = spread_heads(qkv[0, rows, width + at : width + at + GROUP], mask)
                dqkv_o[0, rows, at : at + GROUP] = (dot(grad_scores, keys) * 0.125).astype(bf16)
                for pair in range(2):
                    lanes = slice(128 * pair, 128 * pair + 128)
                    both = dot_tn(grad_scores[:, lanes], query[:, lanes]) * 0.125
                    to = width + at + 128 * pair
                    dqkv_o[0, rows, to : to + 128] = jnp.where(low, both[:64], both[64:]).astype(bf16)
                    both = dot_tn(probs[:, lanes], grads[:, lanes])
                    to = 2 * width + at + 128 * pair
                    dqkv_o[0, rows, to : to + 128] = jnp.where(low, both[:64], both[64:]).astype(bf16)

        @pl.loop(0, 3 * width // 256)
        def _(step):
            lanes = row_block(step, 256)
            acc[:, lanes] += dot_tn(mix[0], dqkv_o[0, :, lanes])

    @pl.when(unit == pl.num_programs(0) - 1)
    def _():
        grad_o[:, : 3 * width] = acc[...].astype(bf16)
        grad_o[:, 3 * width :] = dout[...]


def backward_tokens(
    base, meta, dqkv, x, gm, mod, taps, spots, qkv_w,
    dx_o, own_o, far_o, mod_o, tap_o, grad_mix, hidden, grad_hidden, dtap,
):
    unit = pl.program_id(0) + base
    width = x.shape[2]

    @pl.when(pl.program_id(0) == 0)
    def _():
        dtap[...] = jnp.zeros_like(dtap)

    @pl.when(meta[unit] > 0)
    def _():
        mod_o[...] = jnp.zeros_like(mod_o)

        @pl.loop(0, width // 256)
        def _(step):
            rows = row_block(step, 256)
            grad_mix[:, rows] = dot_nt(dqkv[0], qkv_w[rows, :]).astype(bf16).astype(f32)

        for latent in range(2):
            shift, scale = mod[0, latent, 0:1, :], 1.0 + mod[0, latent, 1:2, :]

            @pl.loop(0, 4)
            def _(step):
                rows = row_block(step, 64, latent * LATENT)
                normed, _ = norm_parts(x[0, rows, :].astype(f32))
                hidden[rows, :] = (normed * scale + shift).astype(bf16).astype(f32)

        layout = meta[meta.shape[0] // 2 + unit]
        which = jnp.where(layout == 2, 1, 0)
        narrow_grid = layout == 0
        ends = edges(narrow_grid)

        @pl.loop(0, width // 128)
        def _(step):
            lanes = row_block(step, 128)
            weights = [taps[0, tap : tap + 1, lanes] for tap in range(9)]
            for latent in range(2):
                rows = phase_rows(latent)
                grads = [grad_mix[r, lanes] for r in rows]
                found = neighbours([hidden[r, lanes] for r in rows], narrow_grid, ends)
                add_taps(dtap, which, lanes, found, grads)
                for r, near in zip(rows, neighbours(grads, narrow_grid, ends)):
                    grad_hidden[r, lanes] = weighted(near, weights[::-1])

        for latent in range(2):
            scale = 1.0 + mod[0, latent, 1:2, :]

            def tally(block, values):
                mod_o[0, latent, block : block + 1, :] += jnp.sum(values, axis=0, keepdims=True)

            @pl.loop(0, 4)
            def _(step):
                rows = row_block(step, 64, latent * LATENT)
                normed, inverse = norm_parts(x[0, rows, :].astype(f32))
                grads = grad_hidden[rows, :]
                tally(0, grads)
                tally(1, grads * normed)
                total = gm[0, rows, :] + norm_back(grads * scale, normed, inverse)
                dx_o[0, rows, :] = total.astype(bf16)

        put_back(dx_o, spots, own_o, far_o)

    @pl.when(pl.program_id(0) == pl.num_programs(0) - 1)
    def _():
        finish_taps(dtap, tap_o)


def source_places(layouts, half):
    p = jnp.arange(HALF, dtype=jnp.int32)
    latent, q = p // LATENT, p % 64
    row_parity, column_parity = (p // 128) % 2, (p // 64) % 2
    square = (2 * (q // 8) + row_parity) * GRID + 16 * latent + 2 * (q % 8) + column_parity
    low_row, wide_col = 2 * (q // 16) + row_parity, 2 * (q % 16) + column_parity
    across = (8 * latent + low_row) * GRID + wide_col
    column = 8 * latent + low_row
    own = (wide_col - 16 * half) * GRID + 16 * half + column
    other = HALF + (wide_col - 16 * (1 - half)) * 16 + column
    downward = jnp.where(wide_col // 16 == half, own, other)
    kind = layouts[:, None]
    return jnp.where(kind == 0, square, jnp.where(kind == 1, across, downward))


def turned(taps):
    return taps.reshape(taps.shape[:-2] + (3, 3, taps.shape[-1])).swapaxes(-3, -2).reshape(taps.shape)


def bit_of(index, bit):
    return (index // bit) % 2


def swapped(values, bit):
    count = lax.axis_size("wide")
    return lax.ppermute(values, "wide", [(i, i ^ bit) for i in range(count)])


def bits_of(count):
    return [1 << b for b in range(count.bit_length() - 1)]


def ordered(values, other, bit):
    low = bit_of(lax.axis_index("wide"), bit) == 0
    return jnp.where(low, values, other), jnp.where(low, other, values)


def gathered_far(values):
    count = lax.axis_size("wide")
    found = {0: values}
    for mask in range(4, count, 4):
        found[mask] = swapped(values, mask)
    for bit in bits_of(count)[2:]:
        found = {
            mask: jnp.stack(ordered(found[mask], found[mask | bit], bit), 0) for mask in found if not mask & bit
        }
    return found[0].reshape((count // 4,) + values.shape)


def gathered_near(values, bit, axis, *waits):
    other = swapped(values, bit)
    values, *waits = joined(values, *waits)
    return jnp.stack(ordered(values, other, bit), axis), *waits


def gathered_everywhere(values, wait):
    lane, count = lax.axis_index("narrow"), lax.axis_size("narrow")
    if count == 2:
        other = lax.ppermute(values, "narrow", [(0, 1), (1, 0)])
        values = jnp.where(lane == 0, jnp.stack([values, other]), jnp.stack([other, values]))
    else:
        values = lax.all_gather(values, "narrow", axis=0)
    values = values[None]
    for bit in reversed(bits_of(lax.axis_size("wide"))):
        if bit == 2:
            values = after(values, wait)
        values = jnp.stack(ordered(values, swapped(values, bit), bit), 1)
        values = values.reshape((-1,) + values.shape[2:])
    return values


def joined(*values):
    return lax.optimization_barrier(values)


def after(value, *earlier):
    return lax.optimization_barrier((value, *earlier))[0]


def narrow_sum(values):
    count = lax.axis_size("narrow")
    if count == 2:
        other = lax.ppermute(values, "narrow", [(0, 1), (1, 0)])
        return values.astype(f32) + other.astype(f32)
    return lax.psum(values, "narrow").astype(f32)


def body(
    tokens, cotangent, conv_attn, qkv_weight, out_weight, up_weight, conv_ffn, down_weight,
    ada_weight, class_table, timesteps, labels, layout, counts,
):
    slots, local_tokens, D = tokens.shape
    owners, narrow = lax.axis_size("wide"), lax.axis_size("narrow")
    owner, lane = lax.axis_index("wide"), lax.axis_index("narrow")
    shard = D // owners
    half = lane % 2
    spread = narrow // 2
    balanced = narrow == 2 and slots == 4
    units = 3 if balanced else slots // spread
    hidden_width = up_weight.shape[1]
    columns = hidden_width // PARTS
    per_part = columns // D

    loads = (counts > 0).astype(jnp.int32).reshape(owners, slots)

    def all_units(values):
        values = values.reshape((owners, slots) + values.shape[1:])
        if balanced:
            idle = (loads.sum(1) == 0).reshape((owners,) + (1,) * (values.ndim - 2))
            other = jnp.roll(values[:, 3], owners // 2, axis=0)
            return jnp.stack([values[:, 0], values[:, 1], jnp.where(idle, other, values[:, 2])], 1)
        return values

    def my_units(values):
        values = lax.dynamic_index_in_dim(all_units(values), owner, 0, keepdims=False)
        if balanced:
            return values
        values = values.reshape((units, spread) + values.shape[1:])
        return lax.dynamic_index_in_dim(values, lane // 2, 1, keepdims=False)

    rows_here = units * 2

    def latent_rows(values):
        values = all_units(values)
        if balanced:
            values = values.reshape(owners, units, 2, 2).transpose(0, 2, 1, 3)
        else:
            values = values.reshape(owners, units, spread, 2, 2).transpose(0, 2, 3, 1, 4)
        values = values.reshape(owners, narrow, rows_here)
        return jnp.pad(values, ((0, 0), (0, 0), (0, 2)), constant_values=-1).reshape(-1)

    count_float = counts.astype(f32)
    scales = count_float * float(counts.shape[0]) / jnp.sum(count_float)
    my_layout, my_scale = my_units(layout), my_units(scales)
    active = my_units(counts) > 0
    meta = jnp.concatenate([active.astype(jnp.int32), my_layout])
    places = source_places(my_layout, half)

    half_width = D // 2
    my_columns = owner * shard + jnp.arange(shard, dtype=jnp.int32)
    freqs = jnp.exp(-math.log(10000.0) * (my_columns % half_width).astype(f32) / half_width)
    angles = latent_rows(timesteps)[:, None].astype(f32) * freqs
    label_hot = (latent_rows(labels)[:, None] == jnp.arange(class_table.shape[0], dtype=jnp.int32)).astype(bf16)
    embed = jnp.where(my_columns < half_width, jnp.cos(angles), jnp.sin(angles)) + dot(label_hot, class_table)
    activ, silu_back = jax.vjp(jax.nn.silu, embed)
    real_row = (latent_rows(labels) >= 0)[:, None]
    act_low = jnp.where(real_row, activ, 0.0).astype(bf16)
    mine = act_low.reshape(owners, narrow, rows_here + 2, shard)[:, :, :rows_here]
    mine = lax.dynamic_index_in_dim(mine, lane, 1, keepdims=False)
    partial_mod = dot(mine.reshape(-1, shard), ada_weight).astype(bf16).reshape(owners, rows_here, -1)
    both_taps = jnp.concatenate([conv_attn, conv_ffn], 1).reshape(-1)
    tap_size = both_taps.shape[0]
    tap_lanes = -(-tap_size // (units * 2 * 128)) * 128
    both_taps = jnp.pad(both_taps, (0, units * 2 * tap_lanes - tap_size)).reshape(1, units * 2, tap_lanes)
    sent = jnp.concatenate([partial_mod, jnp.broadcast_to(both_taps, (owners, units * 2, tap_lanes))], 2)
    arrived = lax.all_to_all(sent, "wide", 0, 0, tiled=True)
    modulation = jnp.sum(arrived[:, :, : 6 * D].astype(f32), axis=0).reshape(units, 2, 6, D)
    both_taps = arrived[:, :, 6 * D :].reshape(owners, -1)[:, :tap_size].reshape(owners, 9, -1).astype(f32)
    conv_one = both_taps[:, :, :shard].swapaxes(0, 1).reshape(9, D)
    conv_two = both_taps[:, :, shard:].reshape(owners, 9, PARTS, per_part, shard).transpose(2, 1, 3, 0, 4)
    conv_two = conv_two.reshape(PARTS, 9, columns)
    weight_row = jnp.broadcast_to(my_scale[:, None, None, None], (units, 2, 1, D))
    mod = jnp.concatenate([modulation, weight_row], 2)

    attn_far = gathered_far(jnp.concatenate([qkv_weight, out_weight], 1))
    up_parts = up_weight.reshape(shard, owners, PARTS, per_part, shard).transpose(2, 0, 3, 1, 4)
    up_parts = up_parts.reshape(PARTS, shard, columns)
    down_parts = down_weight.reshape(PARTS, per_part, shard, D).swapaxes(1, 2).reshape(PARTS, shard, columns)
    ffn_parts = jnp.concatenate([up_parts, down_parts], 2)

    def all_rows(values):
        return lax.all_gather(values, "wide", axis=0, tiled=True)


    def unit_taps(taps):
        return jnp.where((my_layout == 2)[:, None, None], turned(taps), taps)

    taps_one = unit_taps(conv_one)

    params = pltpu.CompilerParams(vmem_limit_bytes=VMEM_BYTES, dimension_semantics=("arbitrary",))
    any_space = pl.BlockSpec(memory_space=pl.ANY)

    def per_unit(*shape, base=0):
        return pl.BlockSpec((1,) + shape, lambda i, meta: (i + base,) + (0,) * len(shape))

    def whole(*shape):
        return pl.BlockSpec(shape, lambda i, meta: (0,) * len(shape), pipeline_mode=pl.Buffered(1))

    def struct(*shape, kind=bf16):
        return jax.ShapeDtypeStruct(shape, kind)

    def call(kernel, name, count, flags, ins, in_specs, outs, out_specs, scratch=(), flops=0, before=()):
        aliases = {1 + len(ins) + i: i for i in range(len(before))}
        extra = len(before)

        def run(meta, *refs):
            kept = refs[: len(ins)] + refs[len(ins) + extra :]
            kernel(meta, *kept)

        return pl.pallas_call(
            run,
            grid_spec=pltpu.PrefetchScalarGridSpec(
                num_scalar_prefetch=1, grid=(count,), in_specs=list(in_specs) + [any_space] * extra,
                out_specs=out_specs, scratch_shapes=list(scratch),
            ),
            out_shape=outs,
            input_output_aliases=aliases,
            compiler_params=params,
            cost_estimate=pl.CostEstimate(flops=int(flops * count * 0.25), bytes_accessed=int(1e6 * count), transcendentals=0),
            name=name,
        )(flags, *ins, *before)

    tokens_shape = (HALF, D)

    def arranged(base, count, tok, far, far_base, where, flags):
        return call(
            partial(arrange, base), "arrange", count, flags, [tok, far, where[:, :, None]],
            [per_unit(*tokens_shape, base=base), per_unit(LATENT, D, base=far_base), per_unit(HALF, 1, base=base)],
            struct(count, *tokens_shape), per_unit(*tokens_shape), flops=2e9,
        )

    if balanced:
        own_layout = lax.dynamic_slice_in_dim(layout, owner * slots, slots)
        own_active = lax.dynamic_slice_in_dim(counts, owner * slots, slots) > 0
        own_places = source_places(own_layout, half)
        own_flags = jnp.concatenate([own_active.astype(jnp.int32), own_layout])
        swap = [(0, 1), (1, 0)]
        partner = [(i, (i + owners // 2) % owners) for i in range(owners)]

        def for_other_half(values, first, count):
            part = values.reshape(slots, 16, GRID, D)[first : first + count]
            part = lax.dynamic_slice_in_dim(part, 16 * (1 - half), 16, axis=2)
            return lax.ppermute(part.reshape(-1, LATENT, D), "narrow", swap)

        own_tok, own_cot = [v.reshape(slots, HALF, D) for v in (tokens, cotangent)]
        x_last = arranged(3, 1, own_tok, for_other_half(tokens, 3, 1), 0, own_places, own_flags)
        attn_far, x_last, cot_far_last = joined(attn_far, x_last, for_other_half(cotangent, 3, 1))
        x_other = lax.ppermute(x_last, "wide", partner)
        x_own = arranged(0, 3, own_tok, for_other_half(tokens, 0, 3), 0, own_places, own_flags)
        cot_far = for_other_half(after(cotangent, attn_far), 0, 3)
    else:

        def to_units(values):
            full = lax.all_gather(values, "narrow", axis=1, tiled=True)
            full = full.reshape(units, spread, 2, 16, GRID, D)
            full = lax.dynamic_index_in_dim(full, lane // 2, 1, keepdims=False)
            here = lax.dynamic_index_in_dim(full, half, 1, keepdims=False)
            far = lax.dynamic_index_in_dim(full, 1 - half, 1, keepdims=False)
            far = lax.dynamic_slice_in_dim(far, 16 * half, 16, axis=2)
            return arranged(0, units, here.reshape(units, HALF, D), far.reshape(units, LATENT, D), 0, places, meta)

        x_own = to_units(tokens)
        cot_own = to_units(cotangent)
        ffn_first = all_rows(after(ffn_parts[0], attn_far))
        cots, cot_specs = [cot_own], [per_unit(*tokens_shape)]

    unit_values = struct(units, *tokens_shape)
    unit_floats = struct(units, *tokens_shape, kind=f32)

    def mix_call(base, count, taken, before):
        spec = per_unit(*tokens_shape, base=base)
        ins, specs = [x_own], [spec]
        if taken:
            ins, specs = ins + [x_other], specs + [whole(1, *tokens_shape)]
        return call(
            partial(mix_tokens, base, taken), "mix_tokens", count, meta, ins + [mod, taps_one],
            specs + [per_unit(2, 7, D, base=base), per_unit(9, D, base=base)],
            [unit_values, unit_values], [spec, spec], [pltpu.VMEM(tokens_shape, f32)], 3e9, before,
        )

    def attend_call(base, count, before):
        spec = per_unit(*tokens_shape, base=base)
        return call(
            partial(attend, base), "attend", count, meta, [x, mixed, mod, attn_full],
            [spec, spec, per_unit(2, 7, D, base=base), whole(D, 4 * D)],
            [struct(units, HALF, 3 * D), unit_values, unit_values, unit_values, unit_floats, unit_values],
            [per_unit(HALF, 3 * D, base=base)] + [spec] * 5, (), 8e9, before,
        )

    if balanced:
        x, mixed = mix_call(0, 2, False, ())
        attn_near, mixed, x_other, cot_far = gathered_near(attn_far, 2, 1, mixed, x_other, cot_far)
        cot_own = arranged(0, 3, own_cot, cot_far, 0, own_places, own_flags)
        ffn_first = all_rows(after(ffn_parts[0], attn_near))
        cot_last = arranged(3, 1, own_cot, cot_far_last, 0, own_places, after(own_flags, attn_near))
        cot_other = lax.ppermute(cot_last, "wide", partner)
        attn_full, cot_own = gathered_near(attn_near, 1, 2, cot_own)
        attn_full = attn_full.reshape(D, 4 * D)
        front = attend_call(0, 2, ())
        ffn_second = all_rows(after(ffn_parts[1], attn_full))
        x, mixed = mix_call(2, 1, True, (x, mixed))
        front = attend_call(2, 1, front)
        cots, cot_specs = [cot_own, cot_other], [per_unit(*tokens_shape), whole(1, *tokens_shape)]
    else:
        x, mixed = mix_call(0, units, False, ())
        (attn_near,) = gathered_near(attn_far, 2, 1)
        (attn_full,) = gathered_near(attn_near, 1, 2)
        attn_full = attn_full.reshape(D, 4 * D)
        front = attend_call(0, units, ())
        ffn_second = all_rows(after(ffn_parts[1], attn_full))
    projected, probs, attended, branch, middle, ffn_in = front

    slot_pair = [pltpu.VMEM((HALF, 256), kind) for kind in (f32, f32, f32, f32, bf16, bf16, bf16, bf16)]
    work = [pltpu.VMEM((D, HALF), bf16), pltpu.VMEM((D, HALF), bf16)]
    work += [pltpu.VMEM((D, columns), f32), pltpu.VMEM((D, columns), f32), pltpu.VMEM((2, 72, columns), f32)]
    unit_spec = per_unit(*tokens_shape)
    tap_grad, tap_spec = struct(9, columns, kind=f32), whole(9, columns)
    weight_grad, weight_spec = struct(D, 2 * columns), whole(D, 2 * columns)
    spots = places[:, None, :]
    gbb, branch_b, grad_ffn, ffn_grad_0, ffn_taps_0 = call(
        partial(feed_forward, 0, balanced), "feed_forward", units, meta,
        cots + [mod, ffn_in, ffn_first, unit_taps(conv_two[0])],
        cot_specs + [per_unit(2, 7, D), unit_spec, weight_spec, per_unit(9, columns)],
        [unit_values, unit_floats, unit_floats, weight_grad, tap_grad],
        [unit_spec, unit_spec, unit_spec, weight_spec, tap_spec], work + slot_pair, 16e9,
    )

    def owner_sum(values):
        return lax.psum_scatter(values, "wide", scatter_dimension=0, tiled=True)

    sums_0 = owner_sum(ffn_grad_0)
    grad_ffn, y_units, y_own, y_far, ffn_grad_1, ffn_taps_1, branch_b = call(
        partial(feed_forward, 1, balanced), "feed_forward", units, meta,
        [gbb, ffn_in, ffn_second, unit_taps(conv_two[1]), branch_b, grad_ffn, middle, mod, spots, ffn_taps_0],
        [unit_spec, unit_spec, weight_spec, per_unit(9, columns), unit_spec, unit_spec, unit_spec,
         per_unit(2, 7, D), per_unit(1, HALF), tap_spec],
        [unit_floats, unit_values, unit_values, struct(units, LATENT, D), struct(D, 2 * columns + 128), tap_grad,
         unit_floats],
        [unit_spec, unit_spec, unit_spec, per_unit(LATENT, D), whole(D, 2 * columns + 128), tap_spec, unit_spec],
        work + slot_pair, 17e9,
    )
    sums_1 = owner_sum(after(ffn_grad_1, sums_0))
    grad_ffn = after(grad_ffn, sums_0)

    grad_mid, grad_att, mod_late, out_grad = call(
        partial(backward_middle, balanced), "backward_middle", units, meta,
        cots + [branch_b, grad_ffn, middle, branch, attended, mod, attn_full],
        cot_specs + [unit_spec] * 5 + [per_unit(2, 7, D),
         pl.BlockSpec((D, D), lambda i, meta: (0, 3), pipeline_mode=pl.Buffered(1))],
        [unit_floats, unit_values, struct(units, 2, 4, D, kind=f32), struct(D, D)],
        [unit_spec, unit_spec, per_unit(2, 4, D), whole(D, D)],
        [pltpu.VMEM(tokens_shape, bf16), pltpu.VMEM((D, D), f32)], 4e9,
    )
    head_grads, attn_grad = call(
        backward_heads, "backward_heads", units, meta, [projected, grad_att, probs, mixed, out_grad],
        [per_unit(HALF, 3 * D), unit_spec, unit_spec, unit_spec, whole(D, D)],
        [struct(units, HALF, 3 * D), struct(D, 4 * D)], [per_unit(HALF, 3 * D), whole(D, 4 * D)],
        [pltpu.VMEM((D, 3 * D), f32)], 12e9,
    )
    attn_sums = owner_sum(after(attn_grad, sums_1))

    def tokens_call(base, count, before):
        spec = per_unit(*tokens_shape, base=base)
        return call(
            partial(backward_tokens, base), "backward_tokens", count, meta,
            [head_grads, x, grad_mid, mod, taps_one, spots, attn_full],
            [per_unit(HALF, 3 * D, base=base), spec, spec, per_unit(2, 7, D, base=base), per_unit(9, D, base=base), per_unit(1, HALF, base=base),
             whole(D, 3 * D)],
            [unit_values, unit_values, struct(units, LATENT, D), struct(units, 2, 2, D, kind=f32),
             struct(9, D, kind=f32)],
            [spec, spec, per_unit(LATENT, D, base=base), per_unit(2, 2, D, base=base), whole(9, D)],
            [pltpu.VMEM(tokens_shape, f32)] * 3 + [pltpu.VMEM((2, 72, D), f32)], 6e9, before,
        )

    def finished(pieces):
        pairs = []
        for own, far in pieces:
            count = own.shape[0]
            far = far.reshape(count, 16, 16, D)
            empty = jnp.zeros_like(far)
            side = jnp.where(half == 0, jnp.concatenate([empty, far], 2), jnp.concatenate([far, empty], 2))
            pairs.append(own.reshape(count, 16, GRID, D) + side)
        total = jnp.concatenate(pairs, 0)
        return jnp.where(own_active[:, None, None, None], total, 0.0).reshape(slots, local_tokens, D)

    def placed(back):
        return call(
            place_back, "place_back", 1, own_flags, [back, own_places[3:, None, :]],
            [unit_spec, per_unit(1, HALF)], [struct(1, *tokens_shape), struct(1, LATENT, D)],
            [unit_spec, per_unit(LATENT, D)], (), 2e9,
        )

    def rows_back(own, far):
        own = jnp.where(active[:, None, None], own, 0.0).reshape(units, 1, 16, GRID, D)
        far = jnp.where(active[:, None, None], far, 0.0).reshape(units, 1, 16, 16, D)
        full = lax.dynamic_update_slice_in_dim(jnp.zeros((units, 2, 16, GRID, D), bf16), own, half, 1)
        other = lax.dynamic_update_slice_in_dim(jnp.zeros((units, 1, 16, GRID, D), bf16), far, 16 * half, 3)
        full = lax.dynamic_update_slice_in_dim(full, other, 1 - half, 1).reshape(units, 1, 2 * HALF, D)
        full = lax.dynamic_update_slice_in_dim(jnp.zeros((units, spread, 2 * HALF, D), bf16), full, lane // 2, 1)
        return lax.psum_scatter(full.reshape(slots, 2 * HALF, D), "narrow", scatter_dimension=1, tiled=True)

    if balanced:
        y_back = lax.ppermute(y_units[2:], "wide", partner)
        y_far = lax.ppermute(y_far, "narrow", swap)
        head_grads, y_back, y_far = lax.optimization_barrier((head_grads, y_back, y_far))
        y_last, y_last_far = placed(y_back)
        dx_units, dx_own, dx_far, mod_early, taps_a = tokens_call(2, 1, ())
        x_back = lax.ppermute(dx_units[2:], "wide", partner)
        y_last_far = lax.ppermute(y_last_far, "narrow", swap)
        work_y = finished([(y_own, y_far), (y_last, y_last_far)])
        head_grads, sums_1, work_y = lax.optimization_barrier((head_grads, sums_1, work_y))
        _, dx_own, dx_far, mod_early, taps_b = tokens_call(0, 2, (dx_units, dx_own, dx_far, mod_early))
        mod_early, x_back, dx_far = lax.optimization_barrier((mod_early, x_back, dx_far))
        x_last, x_last_far = placed(x_back)
        dx_far, x_last_far = [lax.ppermute(v, "narrow", swap) for v in (dx_far, x_last_far)]
        work_x = finished([(dx_own, dx_far), (x_last, x_last_far)])
        conv_one_grad = taps_a + taps_b
    else:
        work_y = rows_back(y_own, y_far)
        dx_units, dx_own, dx_far, mod_early, taps_a = tokens_call(0, units, ())
        work_x = rows_back(dx_own, dx_far)
        conv_one_grad = taps_a

    attn_final = narrow_sum(attn_sums)
    final_qkv, final_out = attn_final[:, : 3 * D], attn_final[:, 3 * D :]
    second = narrow_sum(sums_1)
    ffn_final = jnp.stack([narrow_sum(sums_0), second[:, : 2 * columns]])
    final_up = ffn_final[:, :, :columns].reshape(PARTS, shard, per_part, owners, shard)
    final_up = final_up.transpose(1, 3, 0, 2, 4).reshape(shard, hidden_width)
    final_down = ffn_final[:, :, columns:].reshape(PARTS, shard, per_part, D).swapaxes(1, 2).reshape(-1, D)
    final_taps = second[:, 2 * columns : 2 * columns + 9 * PARTS * per_part].reshape(shard, PARTS, per_part, 9)
    final_taps = final_taps.transpose(3, 1, 2, 0).reshape(9, -1)

    mod_grads = jnp.concatenate([mod_early, mod_late], 2)
    mod_grads = jnp.where(active[:, None, None, None], mod_grads, 0.0).astype(bf16).reshape(rows_here, 6 * D)
    tap_rows = jnp.pad(conv_one_grad.astype(bf16).reshape(-1), (0, 3 * D)).reshape(2, 6 * D)
    gathered = gathered_everywhere(jnp.concatenate([mod_grads, tap_rows], 0), attn_sums)
    conv_one_sum = gathered[:, :, rows_here:].astype(f32).sum((0, 1)).reshape(-1)[: 9 * D].reshape(9, D)
    conv_one_sum = lax.dynamic_slice_in_dim(conv_one_sum, owner * shard, shard, axis=1)
    mod_all = gathered.reshape(-1, 6 * D)
    grad_ada = dot_tn(act_low, mod_all)
    grad_embed = jnp.where(real_row, silu_back(dot_nt(mod_all, ada_weight))[0], 0.0)
    grad_table = dot_tn(label_hot, grad_embed.astype(bf16))
    return (
        work_y, work_x, conv_one_sum, final_qkv, final_out, final_up,
        final_taps, final_down, grad_ada, grad_table,
    )


def solution(mesh):
    rows = P("wide", None)
    columns = P(None, "wide")
    canvases = P("wide", "narrow", None)
    return jax.shard_map(
        body,
        mesh=mesh,
        in_specs=(canvases, canvases, columns, rows, rows, rows, columns, rows, rows, columns, P(), P(), P(), P()),
        out_specs=(canvases, canvases, columns, rows, rows, rows, columns, rows, rows, columns),
        check_vma=False,
    )
```

```python
from functools import partial
import math

import jax
import jax.numpy as jnp
import numpy as np
from jax import lax
from jax.experimental import pallas as pl
from jax.experimental.pallas import tpu as pltpu
from jax.sharding import PartitionSpec as P

HEAD_DIM = 64
GRID = 32
LATENT = 256
HALF = 2 * LATENT
PARTS = 2
ROWS = 128
GROUP = 256
VMEM_BYTES = 67000000

norm_eps = 1e-06
bf16 = jnp.bfloat16
f32 = jnp.float32


def dot(a, b):
    return lax.dot_general(a, b, (((1,), (0,)), ((), ())), preferred_element_type=f32)


def dot_nt(a, b):
    return lax.dot_general(a, b, (((1,), (1,)), ((), ())), preferred_element_type=f32)


def dot_tn(a, b):
    return lax.dot_general(a, b, (((0,), (0,)), ((), ())), preferred_element_type=f32)


def norm_parts(values):
    centred = values - jnp.mean(values, axis=-1, keepdims=True)
    inverse = lax.rsqrt(jnp.mean(centred * centred, axis=-1, keepdims=True) + norm_eps)
    return centred * inverse, inverse


def norm_back(grad_normed, normed, inverse):
    return inverse * (
        grad_normed
        - jnp.mean(grad_normed, axis=-1, keepdims=True)
        - normed * jnp.mean(grad_normed * normed, axis=-1, keepdims=True)
    )


def edges(narrow_grid):
    place = lax.broadcasted_iota(jnp.int32, (64, 128), 0)
    place = jnp.where(narrow_grid, place % 8, place % 16)
    return place == 0, place == jnp.where(narrow_grid, 7, 15)


def neighbours(blocks, narrow_grid, ends):
    first, last = ends
    gap = jnp.zeros((16, 128), blocks[0].dtype)

    def earlier(v):
        padded = jnp.concatenate([gap, v], 0)
        return jnp.where(narrow_grid, padded[8:72], padded[:64])

    def later(v):
        padded = jnp.concatenate([v, gap], 0)
        return jnp.where(narrow_grid, padded[8:72], padded[16:80])

    columns, moved = [], []
    for row_parity in range(2):
        even, odd = blocks[2 * row_parity], blocks[2 * row_parity + 1]
        before = jnp.where(first, 0.0, pltpu.roll(odd, 1, 0))
        after = jnp.where(last, 0.0, pltpu.roll(even, 63, 0))
        shift = later if row_parity == 0 else earlier
        b, e, o, a = [shift(v) for v in (before, even, odd, after)]
        columns.append(((before, even, odd), (even, odd, after)))
        moved.append(((b, e, o), (e, o, a)))
    found = []
    for row_parity in range(2):
        for parity in range(2):
            same, other, far = columns[row_parity][parity], columns[1 - row_parity][parity], moved[1 - row_parity][parity]
            found.append((*far, *same, *other) if row_parity == 0 else (*other, *same, *far))
    return found


def weighted(found, taps):
    total = found[0] * taps[0]
    for tap in range(1, 9):
        total = total + found[tap] * taps[tap]
    return total


def phase_rows(latent):
    return [slice(latent * LATENT + 64 * phase, latent * LATENT + 64 * phase + 64) for phase in range(4)]


def add_taps(store, which, lanes, found, grads):
    for tap in range(9):
        total = found[0][tap] * grads[0]
        for phase in range(1, 4):
            total = total + found[phase][tap] * grads[phase]
        store[which, 8 * tap : 8 * tap + 8, lanes] += jnp.sum(total.reshape(8, 8, total.shape[1]), axis=0)


def finish_taps(store, out):
    for tap in range(9):
        other = 3 * (tap % 3) + tap // 3
        total = store[0, 8 * tap : 8 * tap + 8, :] + store[1, 8 * other : 8 * other + 8, :]
        out[tap : tap + 1, :] = jnp.sum(total, axis=0, keepdims=True)


def head_mask():
    rows = lax.broadcasted_iota(jnp.int32, (GROUP, GROUP), 0) // HEAD_DIM
    cols = lax.broadcasted_iota(jnp.int32, (GROUP, GROUP), 1) // HEAD_DIM
    return jnp.where(rows == cols, 1.0, 0.0).astype(bf16)


def spread_heads(values, mask):
    return jnp.concatenate([values] * 4, 0) * mask


def head_max(values):
    low = lax.broadcasted_iota(jnp.int32, values.shape, 1) < HEAD_DIM
    lower = jnp.max(jnp.where(low, values, -jnp.inf), axis=-1, keepdims=True)
    upper = jnp.max(jnp.where(low, -jnp.inf, values), axis=-1, keepdims=True)
    return jnp.where(low, lower, upper)


def row_block(step, size, start=0):
    return pl.ds(pl.multiple_of(start + step * size, size), size)


def arrange(base, meta, tok, far_tok, places, out):
    @pl.when(meta[pl.program_id(0) + base] > 0)
    def _():
        @pl.loop(0, HALF // ROWS)
        def _(step):
            rows = row_block(step, ROWS)
            source = lax.broadcasted_iota(jnp.int32, (ROWS, 3 * LATENT), 1)
            hot = jnp.where(places[0, rows, :] == source, 1.0, 0.0).astype(bf16)
            values = dot(hot[:, :HALF], tok[0]) + dot(hot[:, HALF:], far_tok[0])
            out[0, rows, :] = values.astype(bf16)


def put_back(result, spots, own, far):
    for step in range(3 * LATENT // ROWS):
        target = lax.broadcasted_iota(jnp.int32, (ROWS, HALF), 0) + step * ROWS
        hot = jnp.where(spots[0] == target, 1.0, 0.0).astype(bf16)
        values = dot(hot, result[0]).astype(bf16)
        if step * ROWS < HALF:
            own[0, step * ROWS : (step + 1) * ROWS, :] = values
        else:
            far[0, step * ROWS - HALF : (step + 1) * ROWS - HALF, :] = values


def place_back(meta, result, spots, own, far):
    @pl.when(meta[3] > 0)
    def _():
        put_back(result, spots, own, far)


def mix_tokens(base, taken, meta, *refs):
    if taken:
        x, other, mod, taps, x_o, mix_o, hidden = refs
    else:
        x, mod, taps, x_o, mix_o, hidden = refs
    unit = pl.program_id(0) + base

    @pl.when(meta[unit] > 0)
    def _():
        for latent in range(2):
            shift, scale = mod[0, latent, 0:1, :], 1.0 + mod[0, latent, 1:2, :]

            @pl.loop(0, LATENT // ROWS)
            def _(step):
                rows = row_block(step, ROWS, latent * LATENT)
                values = x[0, rows, :].astype(f32)
                if taken:
                    values = jnp.where(meta[0] > 0, values, other[0, rows, :].astype(f32))
                x_o[0, rows, :] = values.astype(bf16)
                normed, _ = norm_parts(values)
                hidden[rows, :] = (normed * scale + shift).astype(bf16).astype(f32)

        narrow_grid = meta[meta.shape[0] // 2 + unit] == 0
        ends = edges(narrow_grid)

        @pl.loop(0, x.shape[2] // 128)
        def _(step):
            lanes = row_block(step, 128)
            weights = [taps[0, tap : tap + 1, lanes] for tap in range(9)]
            for latent in range(2):
                found = neighbours([hidden[r, lanes] for r in phase_rows(latent)], narrow_grid, ends)
                for rows, near in zip(phase_rows(latent), found):
                    mix_o[0, rows, lanes] = weighted(near, weights).astype(bf16)


def attend(base, meta, x, mix, mod, weights, qkv_o, prob_o, att_o, branch_o, mid_o, ffn_o):
    unit = pl.program_id(0) + base
    width = x.shape[2]
    groups = width // GROUP

    @pl.when(meta[unit] > 0)
    def _():
        @pl.loop(0, 3 * width // 256)
        def _(step):
            lanes = row_block(step, 256)
            qkv_o[0, :, lanes] = dot(mix[0], weights[:, lanes]).astype(bf16)

        mask = head_mask()

        @pl.loop(0, HALF // 128)
        def _(step):
            chains = []
            for block in range(2):
                rows = row_block(step * 2 + block, 64)
                for group in range(groups):
                    at = GROUP * group
                    keys = spread_heads(qkv_o[0, rows, width + at : width + at + GROUP], mask)
                    chains.append((rows, group, dot_nt(qkv_o[0, rows, at : at + GROUP], keys) * 0.125))
            raised = [
                jnp.concatenate([jnp.exp(s[:, c : c + 128] - head_max(s[:, c : c + 128])) for c in (0, 128)], 1)
                for _, _, s in chains
            ]
            totals = [dot(e.astype(bf16), mask) for e in raised]
            for (rows, group, _), e, total in zip(chains, raised, totals):
                probs = (e / total).astype(bf16)
                at = GROUP * group
                values = spread_heads(qkv_o[0, rows, 2 * width + at : 2 * width + at + GROUP], mask)
                prob_o[0, rows, at : at + GROUP] = probs
                att_o[0, rows, at : at + GROUP] = dot(probs, values).astype(bf16)

        for latent in range(2):
            gate_a = mod[0, latent, 2:3, :]
            shift, scale = mod[0, latent, 3:4, :], 1.0 + mod[0, latent, 4:5, :]

            @pl.loop(0, LATENT // ROWS)
            def _(step):
                rows = row_block(step, ROWS, latent * LATENT)
                branch = dot(att_o[0, rows, :], weights[:, 3 * width :])
                branch_o[0, rows, :] = branch.astype(bf16)
                middle = x[0, rows, :].astype(f32) + gate_a * branch
                mid_o[0, rows, :] = middle
                normed, _ = norm_parts(middle)
                ffn_o[0, rows, :] = (normed * scale + shift).astype(bf16)


def feed_forward(part, taken, meta, *refs):
    if part == 0:
        if taken:
            cot, other, mod, ffn, weights, taps, *refs = refs
        else:
            cot, mod, ffn, weights, taps, *refs = refs
        gbb_o, bb_o, gf_o, grad_o, tap_o, *refs = refs
        gbb = gbb_o
    else:
        gbb, ffn, weights, taps, bb_i, gf_i, mid, mod, spots, tap_i, *refs = refs
        gf_o, y_o, own_o, far_o, grad_o, tap_o, bb_o, *refs = refs
    ffn_t, gbb_t, acc_up, acc_down, dtap, *slots = refs
    unit = pl.program_id(0)
    width = ffn.shape[2]
    columns = taps.shape[2]
    items = columns // 256
    per_block = width // 256

    @pl.when(unit == 0)
    def _():
        acc_up[...] = jnp.zeros_like(acc_up)
        acc_down[...] = jnp.zeros_like(acc_down)
        dtap[...] = jnp.zeros_like(dtap)

    @pl.when(meta[unit] > 0)
    def _():
        if part == 0:
            for latent in range(2):
                gate, weight = mod[0, latent, 5:6, :], mod[0, latent, 6:7, :]

                @pl.loop(0, LATENT // 64)
                def _(step):
                    rows = row_block(step, 64, latent * LATENT)
                    grads = cot[0, rows, :].astype(f32)
                    if taken:
                        from_other = jnp.logical_and(unit == 2, meta[0] == 0)
                        grads = jnp.where(from_other, other[0, rows, :].astype(f32), grads)
                    gbb_o[0, rows, :] = (gate * (grads * weight)).astype(bf16)

        ffn_t[...] = ffn[0].T
        gbb_t[...] = gbb[0].T
        layout = meta[meta.shape[0] // 2 + unit]
        which = jnp.where(layout == 2, 1, 0)
        narrow_grid = layout == 0
        ends = edges(narrow_grid)
        uses = [slots[i::2] for i in range(2)]
        uses[1][2][...] = jnp.zeros_like(uses[1][2])
        uses[1][3][...] = jnp.zeros_like(uses[1][3])
        root = math.sqrt(2.0 / math.pi)

        @pl.loop(0, HALF // 128)
        def _(step):
            rows = row_block(step, 128)
            if part == 0:
                bb_o[0, rows, :] = jnp.zeros((128, width), f32)
                gf_o[0, rows, :] = jnp.zeros((128, width), f32)
            else:
                bb_o[0, rows, :] = bb_i[0, rows, :]
                gf_o[0, rows, :] = gf_i[0, rows, :]

        def down_rows(item):
            block = item // per_block
            return row_block(item - block * per_block, 256), row_block(block, width, columns)

        def project(item, use):
            upward, grad_act = use[0], use[1]
            rows, lanes = down_rows(item)
            upward[...] = dot(ffn[0], weights[:, row_block(item, 256)]).astype(bf16).astype(f32)
            grad_act[...] = dot_nt(gbb[0], weights[rows, lanes])

        def collect(item, use):
            act, grad_up = use[2], use[3]
            rows, lanes = down_rows(item)
            here = row_block(item, 256)
            bb_o[0] += dot(act[...], weights[rows, lanes])
            gf_o[0] += dot_nt(grad_up[...], weights[:, here])
            acc_up[:, here] += dot(ffn_t[...], grad_up[...])
            acc_down[:, here] += dot(gbb_t[...], act[...])

        def convolve(item, use):
            upward, grad_act, act, grad_up = use
            for side in range(2):
                cols = slice(128 * side, 128 * side + 128)
                lanes = row_block(2 * item + side, 128)
                taken_taps = [taps[0, tap : tap + 1, lanes] for tap in range(9)]
                for latent in range(2):
                    rows = phase_rows(latent)
                    found = neighbours([upward[r, cols] for r in rows], narrow_grid, ends)
                    grads = []
                    for r, near in zip(rows, found):
                        spread = weighted(near, taken_taps)
                        square = spread * spread
                        bent = jnp.tanh(spread * (root + root * 0.044715 * square))
                        half = 0.5 + 0.5 * bent
                        act[r, cols] = (spread * half).astype(bf16)
                        slope = half + (0.5 * spread) * (1.0 - bent * bent) * (
                            root + 3.0 * root * 0.044715 * square
                        )
                        grads.append((grad_act[r, cols] * slope).astype(bf16).astype(f32))
                    add_taps(dtap, which, lanes, found, grads)
                    for r, near in zip(rows, neighbours(grads, narrow_grid, ends)):
                        grad_up[r, cols] = weighted(near, taken_taps[::-1]).astype(bf16)

        project(0, uses[0])

        @pl.loop(0, items // 2)
        def _(pair):
            for side in range(2):
                item = 2 * pair + side
                convolve(item, uses[side])
                project(jnp.minimum(item + 1, items - 1), uses[1 - side])
                collect(jnp.maximum(item - 1, 0), uses[1 - side])

        collect(items - 1, uses[1])

        if part == PARTS - 1:
            for latent in range(2):
                gate = mod[0, latent, 5:6, :]

                @pl.loop(0, LATENT // 64)
                def _(step):
                    rows = row_block(step, 64, latent * LATENT)
                    y_o[0, rows, :] = (mid[0, rows, :] + gate * bb_o[0, rows, :]).astype(bf16)

            put_back(y_o, spots, own_o, far_o)

    @pl.when(unit == pl.num_programs(0) - 1)
    def _():
        finish_taps(dtap, tap_o)
        if part == PARTS - 1:
            rows = [t[:, at : at + width] for t in (tap_i, tap_o) for at in range(0, columns, width)]
            rows.append(jnp.zeros((128 - 9 * len(rows), width), f32))
            grad_o[:, 2 * columns :] = jnp.concatenate(rows, 0).T.astype(bf16)
        grad_o[:, :columns] = acc_up[...].astype(bf16)
        for at in range(0, columns, width):
            grad_o[:, columns + at : columns + at + width] = acc_down[:, at : at + width].astype(bf16).T


def backward_middle(taken, meta, *refs):
    if taken:
        cot, other, *refs = refs
    else:
        cot, *refs = refs
    bb, gf, mid, branch, att, mod, out_w, grad_mid, grad_att, mod_o, dout_o, gba, acc_out = refs
    unit = pl.program_id(0)
    width = cot.shape[2]

    @pl.when(unit == 0)
    def _():
        acc_out[...] = jnp.zeros_like(acc_out)

    @pl.when(meta[unit] > 0)
    def _():
        mod_o[...] = jnp.zeros_like(mod_o)
        for latent in range(2):
            gate_a, scale_b = mod[0, latent, 2:3, :], 1.0 + mod[0, latent, 4:5, :]
            weight = mod[0, latent, 6:7, :]

            def tally(block, values):
                mod_o[0, latent, block : block + 1, :] += jnp.sum(values, axis=0, keepdims=True)

            @pl.loop(0, 4)
            def _(step):
                rows = row_block(step, 64, latent * LATENT)
                grads = cot[0, rows, :].astype(f32)
                if taken:
                    from_other = jnp.logical_and(unit == 2, meta[0] == 0)
                    grads = jnp.where(from_other, other[0, rows, :].astype(f32), grads)
                grad_out = grads * weight
                tally(3, grad_out * bb[0, rows, :])
                grad_ffn = gf[0, rows, :]
                normed, inverse = norm_parts(mid[0, rows, :])
                tally(1, grad_ffn)
                tally(2, grad_ffn * normed)
                total = grad_out + norm_back(grad_ffn * scale_b, normed, inverse)
                grad_mid[0, rows, :] = total
                tally(0, total * branch[0, rows, :].astype(f32))
                gba[rows, :] = (gate_a * total).astype(bf16)

        @pl.loop(0, width // 256)
        def _(step):
            lanes = row_block(step, 256)
            acc_out[:, lanes] += dot_tn(att[0], gba[:, lanes])
            grad_att[0, :, lanes] = dot_nt(gba[...], out_w[lanes, :]).astype(bf16)

    @pl.when(unit == pl.num_programs(0) - 1)
    def _():
        dout_o[...] = acc_out[...].astype(bf16)


def backward_heads(shard, meta, odd, qkv, grad_att, prob, mix, dout, dqkv_o, keep_o, send_o, acc):
    unit = pl.program_id(0)
    width = grad_att.shape[2]

    @pl.when(unit == 0)
    def _():
        acc[...] = jnp.zeros_like(acc)

    @pl.when(meta[unit] > 0)
    def _():
        mask = head_mask()
        low = lax.broadcasted_iota(jnp.int32, (64, 128), 1) < HEAD_DIM

        @pl.loop(0, HALF // 128)
        def _(step):
            chains = []
            for block in range(2):
                rows = row_block(2 * step + block, 64)
                for at in range(0, width, GROUP):
                    grads = grad_att[0, rows, at : at + GROUP]
                    values = spread_heads(qkv[0, rows, 2 * width + at : 2 * width + at + GROUP], mask)
                    chains.append((rows, at, grads, dot_nt(grads, values), prob[0, rows, at : at + GROUP]))
            inners = []
            for _, _, _, grad_probs, probs in chains:
                product = probs.astype(f32) * grad_probs
                high = product.astype(bf16)
                rest = (product - high.astype(f32)).astype(bf16)
                inners.append(dot(high, mask) + dot(rest, mask))
            scores = [
                (probs.astype(f32) * (grad_probs - inner)).astype(bf16)
                for (_, _, _, grad_probs, probs), inner in zip(chains, inners)
            ]
            for (rows, at, grads, _, probs), grad_scores in zip(chains, scores):
                query = qkv[0, rows, at : at + GROUP]
                keys = spread_heads(qkv[0, rows, width + at : width + at + GROUP], mask)
                dqkv_o[0, rows, at : at + GROUP] = (dot(grad_scores, keys) * 0.125).astype(bf16)
                for pair in range(2):
                    lanes = slice(128 * pair, 128 * pair + 128)
                    both = dot_tn(grad_scores[:, lanes], query[:, lanes]) * 0.125
                    to = width + at + 128 * pair
                    dqkv_o[0, rows, to : to + 128] = jnp.where(low, both[:64], both[64:]).astype(bf16)
                    both = dot_tn(probs[:, lanes], grads[:, lanes])
                    to = 2 * width + at + 128 * pair
                    dqkv_o[0, rows, to : to + 128] = jnp.where(low, both[:64], both[64:]).astype(bf16)

        @pl.loop(0, 3 * width // 256)
        def _(step):
            lanes = row_block(step, 256)
            acc[:, lanes] += dot_tn(mix[0], dqkv_o[0, :, lanes])

    @pl.when(unit == pl.num_programs(0) - 1)
    def _():
        def put(parity):
            for owner in range(width // shard):
                out = keep_o if owner % 2 == parity else send_o
                rows, to = slice(owner * shard, (owner + 1) * shard), slice(owner // 2 * shard, (owner // 2 + 1) * shard)
                out[to, : 3 * width] = acc[rows, :].astype(bf16)
                out[to, 3 * width :] = dout[rows, :]

        @pl.when(odd[0] == 0)
        def _():
            put(0)

        @pl.when(odd[0] != 0)
        def _():
            put(1)


def backward_tokens(
    base, meta, dqkv, x, gm, mod, taps, spots, qkv_w,
    own_o, far_o, mod_o, dx_o, tap_o, grad_mix, hidden, grad_hidden, dtap,
):
    unit = pl.program_id(0) + base
    width = x.shape[2]

    @pl.when(pl.program_id(0) == 0)
    def _():
        dtap[...] = jnp.zeros_like(dtap)

    @pl.when(meta[unit] > 0)
    def _():
        mod_o[...] = jnp.zeros_like(mod_o)

        @pl.loop(0, width // 256)
        def _(step):
            rows = row_block(step, 256)
            grad_mix[:, rows] = dot_nt(dqkv[0], qkv_w[rows, :]).astype(bf16).astype(f32)

        for latent in range(2):
            shift, scale = mod[0, latent, 0:1, :], 1.0 + mod[0, latent, 1:2, :]

            @pl.loop(0, 4)
            def _(step):
                rows = row_block(step, 64, latent * LATENT)
                normed, _ = norm_parts(x[0, rows, :].astype(f32))
                hidden[rows, :] = (normed * scale + shift).astype(bf16).astype(f32)

        layout = meta[meta.shape[0] // 2 + unit]
        which = jnp.where(layout == 2, 1, 0)
        narrow_grid = layout == 0
        ends = edges(narrow_grid)

        @pl.loop(0, width // 128)
        def _(step):
            lanes = row_block(step, 128)
            weights = [taps[0, tap : tap + 1, lanes] for tap in range(9)]
            for latent in range(2):
                rows = phase_rows(latent)
                grads = [grad_mix[r, lanes] for r in rows]
                found = neighbours([hidden[r, lanes] for r in rows], narrow_grid, ends)
                add_taps(dtap, which, lanes, found, grads)
                for r, near in zip(rows, neighbours(grads, narrow_grid, ends)):
                    grad_hidden[r, lanes] = weighted(near, weights[::-1])

        for latent in range(2):
            scale = 1.0 + mod[0, latent, 1:2, :]

            def tally(block, values):
                mod_o[0, latent, block : block + 1, :] += jnp.sum(values, axis=0, keepdims=True)

            @pl.loop(0, 4)
            def _(step):
                rows = row_block(step, 64, latent * LATENT)
                normed, inverse = norm_parts(x[0, rows, :].astype(f32))
                grads = grad_hidden[rows, :]
                tally(0, grads)
                tally(1, grads * normed)
                total = gm[0, rows, :] + norm_back(grads * scale, normed, inverse)
                dx_o[0, rows, :] = total.astype(bf16)

        put_back(dx_o, spots, own_o, far_o)

    @pl.when(pl.program_id(0) == pl.num_programs(0) - 1)
    def _():
        finish_taps(dtap, tap_o)


def source_places(layouts, half):
    p = jnp.arange(HALF, dtype=jnp.int32)
    latent, q = p // LATENT, p % 64
    row_parity, column_parity = (p // 128) % 2, (p // 64) % 2
    square = (2 * (q // 8) + row_parity) * GRID + 16 * latent + 2 * (q % 8) + column_parity
    low_row, wide_col = 2 * (q // 16) + row_parity, 2 * (q % 16) + column_parity
    across = (8 * latent + low_row) * GRID + wide_col
    column = 8 * latent + low_row
    own = (wide_col - 16 * half) * GRID + 16 * half + column
    other = HALF + (wide_col - 16 * (1 - half)) * 16 + column
    downward = jnp.where(wide_col // 16 == half, own, other)
    kind = layouts[:, None]
    return jnp.where(kind == 0, square, jnp.where(kind == 1, across, downward))


def turned(taps):
    return taps.reshape(taps.shape[:-2] + (3, 3, taps.shape[-1])).swapaxes(-3, -2).reshape(taps.shape)


def bit_of(index, bit):
    return (index // bit) % 2


def swapped(values, bit):
    count = lax.axis_size("wide")
    return lax.ppermute(values, "wide", [(i, i ^ bit) for i in range(count)])


def bits_of(count):
    return [1 << b for b in range(count.bit_length() - 1)]


def ordered(values, other, bit):
    low = bit_of(lax.axis_index("wide"), bit) == 0
    return jnp.where(low, values, other), jnp.where(low, other, values)


def gathered_far(values):
    count = lax.axis_size("wide")
    found = {0: values}
    for mask in range(4, count, 4):
        found[mask] = swapped(values, mask)
    for bit in bits_of(count)[2:]:
        found = {
            mask: jnp.stack(ordered(found[mask], found[mask | bit], bit), 0) for mask in found if not mask & bit
        }
    return found[0].reshape((count // 4,) + values.shape)


def gathered_near(values, bit, axis, *waits):
    other = swapped(values, bit)
    values, *waits = joined(values, *waits)
    return jnp.stack(ordered(values, other, bit), axis), *waits


def summed(keep, other):
    return (keep.astype(f32) + other.astype(f32)).astype(keep.dtype)


def between_pair(values, bit):
    pairs = values.reshape((values.shape[0] // 2, 2) + values.shape[1:])
    keep, send = ordered(pairs[:, 0], pairs[:, 1], bit)
    return summed(keep, swapped(send, bit))


def between_far(values):
    place = lax.axis_index("wide") // 4
    total = lax.dynamic_index_in_dim(values, place, 0, keepdims=False).astype(f32)
    for mask in range(4, lax.axis_size("wide"), 4):
        send = lax.dynamic_index_in_dim(values, place ^ (mask // 4), 0, keepdims=False)
        total = total + swapped(send, mask).astype(f32)
    return total.astype(values.dtype)


def gathered_everywhere(values, *waits):
    lane, count = lax.axis_index("narrow"), lax.axis_size("narrow")
    if count == 2:
        other = lax.ppermute(values, "narrow", [(0, 1), (1, 0)])
        values = jnp.where(lane == 0, jnp.stack([values, other]), jnp.stack([other, values]))
    else:
        values = lax.all_gather(values, "narrow", axis=0)
    values = values[None]
    for bit in reversed(bits_of(lax.axis_size("wide"))):
        if bit == 2:
            values, *waits = joined(values, *waits)
        values = jnp.stack(ordered(values, swapped(values, bit), bit), 1)
        values = values.reshape((-1,) + values.shape[2:])
    return values, *waits


def joined(*values):
    return lax.optimization_barrier(values)


def after(value, *earlier):
    return lax.optimization_barrier((value, *earlier))[0]


def narrow_other(values):
    return lax.ppermute(values, "narrow", [(0, 1), (1, 0)])


def narrow_sum(values, other):
    if other is None:
        return lax.psum(values, "narrow").astype(f32)
    return values.astype(f32) + other.astype(f32)


def body(
    tokens, cotangent, conv_attn, qkv_weight, out_weight, up_weight, conv_ffn, down_weight,
    ada_weight, class_table, timesteps, labels, layout, counts,
):
    slots, local_tokens, D = tokens.shape
    owners, narrow = lax.axis_size("wide"), lax.axis_size("narrow")
    owner, lane = lax.axis_index("wide"), lax.axis_index("narrow")
    shard = D // owners
    half = lane % 2
    spread = narrow // 2
    balanced = narrow == 2 and slots == 4
    units = 3 if balanced else slots // spread
    hidden_width = up_weight.shape[1]
    columns = hidden_width // PARTS
    per_part = columns // D

    loads = (counts > 0).astype(jnp.int32).reshape(owners, slots)

    def all_units(values):
        values = values.reshape((owners, slots) + values.shape[1:])
        if balanced:
            idle = (loads.sum(1) == 0).reshape((owners,) + (1,) * (values.ndim - 2))
            other = jnp.roll(values[:, 3], owners // 2, axis=0)
            return jnp.stack([values[:, 0], values[:, 1], jnp.where(idle, other, values[:, 2])], 1)
        return values

    def my_units(values):
        values = lax.dynamic_index_in_dim(all_units(values), owner, 0, keepdims=False)
        if balanced:
            return values
        values = values.reshape((units, spread) + values.shape[1:])
        return lax.dynamic_index_in_dim(values, lane // 2, 1, keepdims=False)

    rows_here = units * 2

    def latent_rows(values):
        values = all_units(values)
        if balanced:
            values = values.reshape(owners, units, 2, 2).transpose(0, 2, 1, 3)
        else:
            values = values.reshape(owners, units, spread, 2, 2).transpose(0, 2, 3, 1, 4)
        values = values.reshape(owners, narrow, rows_here)
        return jnp.pad(values, ((0, 0), (0, 0), (0, 2)), constant_values=-1).reshape(-1)

    count_float = counts.astype(f32)
    scales = count_float * float(counts.shape[0]) / jnp.sum(count_float)
    my_layout, my_scale = my_units(layout), my_units(scales)
    active = my_units(counts) > 0
    meta = jnp.concatenate([active.astype(jnp.int32), my_layout])
    places = source_places(my_layout, half)

    half_width = D // 2
    my_columns = owner * shard + jnp.arange(shard, dtype=jnp.int32)
    freqs = jnp.exp(-math.log(10000.0) * (my_columns % half_width).astype(f32) / half_width)
    angles = latent_rows(timesteps)[:, None].astype(f32) * freqs
    label_hot = (latent_rows(labels)[:, None] == jnp.arange(class_table.shape[0], dtype=jnp.int32)).astype(bf16)
    embed = jnp.where(my_columns < half_width, jnp.cos(angles), jnp.sin(angles)) + dot(label_hot, class_table)
    activ, silu_back = jax.vjp(jax.nn.silu, embed)
    real_row = (latent_rows(labels) >= 0)[:, None]
    act_low = jnp.where(real_row, activ, 0.0).astype(bf16)
    mine = act_low.reshape(owners, narrow, rows_here + 2, shard)[:, :, :rows_here]
    mine = lax.dynamic_index_in_dim(mine, lane, 1, keepdims=False)
    partial_mod = dot(mine.reshape(-1, shard), ada_weight).astype(bf16).reshape(owners, rows_here, -1)
    both_taps = jnp.concatenate([conv_attn, conv_ffn], 1).reshape(-1)
    tap_size = both_taps.shape[0]
    tap_lanes = -(-tap_size // (units * 2 * 128)) * 128
    both_taps = jnp.pad(both_taps, (0, units * 2 * tap_lanes - tap_size)).reshape(1, units * 2, tap_lanes)
    sent = jnp.concatenate([partial_mod, jnp.broadcast_to(both_taps, (owners, units * 2, tap_lanes))], 2)
    arrived = lax.all_to_all(sent, "wide", 0, 0, tiled=True)
    modulation = jnp.sum(arrived[:, :, : 6 * D].astype(f32), axis=0).reshape(units, 2, 6, D)
    both_taps = arrived[:, :, 6 * D :].reshape(owners, -1)[:, :tap_size].reshape(owners, 9, -1).astype(f32)
    conv_one = both_taps[:, :, :shard].swapaxes(0, 1).reshape(9, D)
    conv_two = both_taps[:, :, shard:].reshape(owners, 9, PARTS, per_part, shard).transpose(2, 1, 3, 0, 4)
    conv_two = conv_two.reshape(PARTS, 9, columns)
    weight_row = jnp.broadcast_to(my_scale[:, None, None, None], (units, 2, 1, D))
    mod = jnp.concatenate([modulation, weight_row], 2)

    attn_far = gathered_far(jnp.concatenate([qkv_weight, out_weight], 1))
    up_parts = up_weight.reshape(shard, owners, PARTS, per_part, shard).transpose(2, 0, 3, 1, 4)
    up_parts = up_parts.reshape(PARTS, shard, columns)
    down_parts = down_weight.reshape(PARTS, per_part, shard, D).swapaxes(1, 2).reshape(PARTS, shard, columns)
    ffn_parts = jnp.concatenate([up_parts, down_parts], 2)

    def all_rows(values):
        return lax.all_gather(values, "wide", axis=0, tiled=True)


    def unit_taps(taps):
        return jnp.where((my_layout == 2)[:, None, None], turned(taps), taps)

    taps_one = unit_taps(conv_one)

    params = pltpu.CompilerParams(vmem_limit_bytes=VMEM_BYTES, dimension_semantics=("arbitrary",))
    any_space = pl.BlockSpec(memory_space=pl.ANY)

    def per_unit(*shape, base=0):
        return pl.BlockSpec((1,) + shape, lambda i, meta: (i + base,) + (0,) * len(shape))

    def whole(*shape):
        return pl.BlockSpec(shape, lambda i, meta: (0,) * len(shape), pipeline_mode=pl.Buffered(1))

    def struct(*shape, kind=bf16):
        return jax.ShapeDtypeStruct(shape, kind)

    def call(kernel, name, count, flags, ins, in_specs, outs, out_specs, scratch=(), flops=0, before=()):
        aliases = {1 + len(ins) + i: i for i in range(len(before))}
        extra = len(before)

        def run(meta, *refs):
            kept = refs[: len(ins)] + refs[len(ins) + extra :]
            kernel(meta, *kept)

        return pl.pallas_call(
            run,
            grid_spec=pltpu.PrefetchScalarGridSpec(
                num_scalar_prefetch=1, grid=(count,), in_specs=list(in_specs) + [any_space] * extra,
                out_specs=out_specs, scratch_shapes=list(scratch),
            ),
            out_shape=outs,
            input_output_aliases=aliases,
            compiler_params=params,
            cost_estimate=pl.CostEstimate(flops=int(flops * count * 0.25), bytes_accessed=int(1e6 * count), transcendentals=0),
            name=name,
        )(flags, *ins, *before)

    tokens_shape = (HALF, D)

    def arranged(base, count, tok, far, far_base, where, flags):
        return call(
            partial(arrange, base), "arrange", count, flags, [tok, far, where[:, :, None]],
            [per_unit(*tokens_shape, base=base), per_unit(LATENT, D, base=far_base), per_unit(HALF, 1, base=base)],
            struct(count, *tokens_shape), per_unit(*tokens_shape), flops=2e9,
        )

    if balanced:
        own_layout = lax.dynamic_slice_in_dim(layout, owner * slots, slots)
        own_active = lax.dynamic_slice_in_dim(counts, owner * slots, slots) > 0
        own_places = source_places(own_layout, half)
        own_flags = jnp.concatenate([own_active.astype(jnp.int32), own_layout])
        swap = [(0, 1), (1, 0)]
        partner = [(i, (i + owners // 2) % owners) for i in range(owners)]

        def for_other_half(values, first, count):
            part = values.reshape(slots, 16, GRID, D)[first : first + count]
            part = lax.dynamic_slice_in_dim(part, 16 * (1 - half), 16, axis=2)
            return lax.ppermute(part.reshape(-1, LATENT, D), "narrow", swap)

        own_tok, own_cot = [v.reshape(slots, HALF, D) for v in (tokens, cotangent)]
        x_last = arranged(3, 1, own_tok, for_other_half(tokens, 3, 1), 0, own_places, own_flags)
        attn_far, x_last, cot_far_last = joined(attn_far, x_last, for_other_half(cotangent, 3, 1))
        x_other = lax.ppermute(x_last, "wide", partner)
        x_own = arranged(0, 3, own_tok, for_other_half(tokens, 0, 3), 0, own_places, own_flags)
        cot_far = for_other_half(after(cotangent, attn_far), 0, 3)
    else:

        def to_units(values):
            full = lax.all_gather(values, "narrow", axis=1, tiled=True)
            full = full.reshape(units, spread, 2, 16, GRID, D)
            full = lax.dynamic_index_in_dim(full, lane // 2, 1, keepdims=False)
            here = lax.dynamic_index_in_dim(full, half, 1, keepdims=False)
            far = lax.dynamic_index_in_dim(full, 1 - half, 1, keepdims=False)
            far = lax.dynamic_slice_in_dim(far, 16 * half, 16, axis=2)
            return arranged(0, units, here.reshape(units, HALF, D), far.reshape(units, LATENT, D), 0, places, meta)

        x_own = to_units(tokens)
        cot_own = to_units(cotangent)
        ffn_first = all_rows(after(ffn_parts[0], attn_far))
        cots, cot_specs = [cot_own], [per_unit(*tokens_shape)]

    unit_values = struct(units, *tokens_shape)
    unit_floats = struct(units, *tokens_shape, kind=f32)

    def mix_call(base, count, taken, before):
        spec = per_unit(*tokens_shape, base=base)
        ins, specs = [x_own], [spec]
        if taken:
            ins, specs = ins + [x_other], specs + [whole(1, *tokens_shape)]
        return call(
            partial(mix_tokens, base, taken), "mix_tokens", count, meta, ins + [mod, taps_one],
            specs + [per_unit(2, 7, D, base=base), per_unit(9, D, base=base)],
            [unit_values, unit_values], [spec, spec], [pltpu.VMEM(tokens_shape, f32)], 3e9, before,
        )

    def attend_call(base, count, before):
        spec = per_unit(*tokens_shape, base=base)
        return call(
            partial(attend, base), "attend", count, meta, [x, mixed, mod, attn_full],
            [spec, spec, per_unit(2, 7, D, base=base), whole(D, 4 * D)],
            [struct(units, HALF, 3 * D), unit_values, unit_values, unit_values, unit_floats, unit_values],
            [per_unit(HALF, 3 * D, base=base)] + [spec] * 5, (), 8e9, before,
        )

    if balanced:
        x, mixed = mix_call(0, 2, False, ())
        attn_near, mixed, x_other, cot_far = gathered_near(attn_far, 2, 1, mixed, x_other, cot_far)
        cot_own = arranged(0, 3, own_cot, cot_far, 0, own_places, own_flags)
        ffn_first = all_rows(after(ffn_parts[0], attn_near))
        cot_last = arranged(3, 1, own_cot, cot_far_last, 0, own_places, after(own_flags, attn_near))
        cot_other = lax.ppermute(cot_last, "wide", partner)
        attn_full, cot_own = gathered_near(attn_near, 1, 2, cot_own)
        attn_full = attn_full.reshape(D, 4 * D)
        front = attend_call(0, 2, ())
        ffn_second = all_rows(after(ffn_parts[1], attn_full))
        x, mixed = mix_call(2, 1, True, (x, mixed))
        front = attend_call(2, 1, front)
        cots, cot_specs = [cot_own, cot_other], [per_unit(*tokens_shape), whole(1, *tokens_shape)]
    else:
        x, mixed = mix_call(0, units, False, ())
        (attn_near,) = gathered_near(attn_far, 2, 1)
        (attn_full,) = gathered_near(attn_near, 1, 2)
        attn_full = attn_full.reshape(D, 4 * D)
        front = attend_call(0, units, ())
        ffn_second = all_rows(after(ffn_parts[1], attn_full))
    projected, probs, attended, branch, middle, ffn_in = front

    slot_pair = [pltpu.VMEM((HALF, 256), kind) for kind in (f32, f32, f32, f32, bf16, bf16, bf16, bf16)]
    work = [pltpu.VMEM((D, HALF), bf16), pltpu.VMEM((D, HALF), bf16)]
    work += [pltpu.VMEM((D, columns), f32), pltpu.VMEM((D, columns), f32), pltpu.VMEM((2, 72, columns), f32)]
    unit_spec = per_unit(*tokens_shape)
    tap_grad, tap_spec = struct(9, columns, kind=f32), whole(9, columns)
    weight_grad, weight_spec = struct(D, 2 * columns), whole(D, 2 * columns)
    spots = places[:, None, :]
    gbb, branch_b, grad_ffn, ffn_grad_0, ffn_taps_0 = call(
        partial(feed_forward, 0, balanced), "feed_forward", units, meta,
        cots + [mod, ffn_in, ffn_first, unit_taps(conv_two[0])],
        cot_specs + [per_unit(2, 7, D), unit_spec, weight_spec, per_unit(9, columns)],
        [unit_values, unit_floats, unit_floats, weight_grad, tap_grad],
        [unit_spec, unit_spec, unit_spec, weight_spec, tap_spec], work + slot_pair, 16e9,
    )

    def owner_sum(values):
        return lax.psum_scatter(values, "wide", scatter_dimension=0, tiled=True)

    sums_0 = owner_sum(ffn_grad_0)
    grad_ffn, y_units, y_own, y_far, ffn_grad_1, ffn_taps_1, branch_b = call(
        partial(feed_forward, 1, balanced), "feed_forward", units, meta,
        [gbb, ffn_in, ffn_second, unit_taps(conv_two[1]), branch_b, grad_ffn, middle, mod, spots, ffn_taps_0],
        [unit_spec, unit_spec, weight_spec, per_unit(9, columns), unit_spec, unit_spec, unit_spec,
         per_unit(2, 7, D), per_unit(1, HALF), tap_spec],
        [unit_floats, struct(1, *tokens_shape), unit_values, struct(units, LATENT, D), struct(D, 2 * columns + 128),
         tap_grad, unit_floats],
        [unit_spec, whole(1, *tokens_shape), unit_spec, per_unit(LATENT, D), whole(D, 2 * columns + 128), tap_spec,
         unit_spec],
        work + slot_pair, 17e9,
    )
    sums_1 = owner_sum(after(ffn_grad_1, sums_0))
    grad_ffn = after(grad_ffn, sums_0)

    grad_mid, grad_att, mod_late, out_grad = call(
        partial(backward_middle, balanced), "backward_middle", units, meta,
        cots + [branch_b, grad_ffn, middle, branch, attended, mod, attn_full],
        cot_specs + [unit_spec] * 5 + [per_unit(2, 7, D),
         pl.BlockSpec((D, D), lambda i, meta: (0, 3), pipeline_mode=pl.Buffered(1))],
        [unit_floats, unit_values, struct(units, 2, 4, D, kind=f32), struct(D, D)],
        [unit_spec, unit_spec, per_unit(2, 4, D), whole(D, D)],
        [pltpu.VMEM(tokens_shape, bf16), pltpu.VMEM((D, D), f32)], 4e9,
    )
    head_grads, attn_keep, attn_send = call(
        partial(backward_heads, shard), "backward_heads", units, meta,
        [(owner % 2).reshape(1), projected, grad_att, probs, mixed, out_grad],
        [pl.BlockSpec(memory_space=pltpu.SMEM), per_unit(HALF, 3 * D), unit_spec, unit_spec, unit_spec, whole(D, D)],
        [struct(units, HALF, 3 * D), struct(D // 2, 4 * D), struct(D // 2, 4 * D)],
        [per_unit(HALF, 3 * D), whole(D // 2, 4 * D), whole(D // 2, 4 * D)],
        [pltpu.VMEM((D, 3 * D), f32)], 12e9,
    )
    attn_sums = summed(attn_keep, swapped(attn_send, 1)).reshape(owners // 2, shard, 4 * D)

    def tokens_call(base, count, before):
        spec = per_unit(*tokens_shape, base=base)
        return call(
            partial(backward_tokens, base), "backward_tokens", count, meta,
            [head_grads, x, grad_mid, mod, taps_one, spots, attn_full],
            [per_unit(HALF, 3 * D, base=base), spec, spec, per_unit(2, 7, D, base=base), per_unit(9, D, base=base), per_unit(1, HALF, base=base),
             whole(D, 3 * D)],
            [unit_values, struct(units, LATENT, D), struct(units, 2, 2, D, kind=f32), struct(1, *tokens_shape),
             struct(9, D, kind=f32)],
            [spec, per_unit(LATENT, D, base=base), per_unit(2, 2, D, base=base), whole(1, *tokens_shape), whole(9, D)],
            [pltpu.VMEM(tokens_shape, f32)] * 3 + [pltpu.VMEM((2, 72, D), f32)], 60e9, before,
        )

    def finished(pieces):
        pairs = []
        for own, far in pieces:
            count = own.shape[0]
            far = far.reshape(count, 16, 16, D)
            empty = jnp.zeros_like(far)
            side = jnp.where(half == 0, jnp.concatenate([empty, far], 2), jnp.concatenate([far, empty], 2))
            pairs.append(own.reshape(count, 16, GRID, D) + side)
        total = jnp.concatenate(pairs, 0)
        return jnp.where(own_active[:, None, None, None], total, 0.0).reshape(slots, local_tokens, D)

    def placed(back):
        return call(
            place_back, "place_back", 1, own_flags, [back, own_places[3:, None, :]],
            [unit_spec, per_unit(1, HALF)], [struct(1, *tokens_shape), struct(1, LATENT, D)],
            [unit_spec, per_unit(LATENT, D)], (), 2e9,
        )

    def rows_back(own, far):
        own = jnp.where(active[:, None, None], own, 0.0).reshape(units, 1, 16, GRID, D)
        far = jnp.where(active[:, None, None], far, 0.0).reshape(units, 1, 16, 16, D)
        full = lax.dynamic_update_slice_in_dim(jnp.zeros((units, 2, 16, GRID, D), bf16), own, half, 1)
        other = lax.dynamic_update_slice_in_dim(jnp.zeros((units, 1, 16, GRID, D), bf16), far, 16 * half, 3)
        full = lax.dynamic_update_slice_in_dim(full, other, 1 - half, 1).reshape(units, 1, 2 * HALF, D)
        full = lax.dynamic_update_slice_in_dim(jnp.zeros((units, spread, 2 * HALF, D), bf16), full, lane // 2, 1)
        return lax.psum_scatter(full.reshape(slots, 2 * HALF, D), "narrow", scatter_dimension=1, tiled=True)

    if balanced:
        y_back = lax.ppermute(y_units, "wide", partner)
        y_far = lax.ppermute(y_far, "narrow", swap)
        head_grads, y_back, y_far, other_0 = joined(head_grads, y_back, y_far, narrow_other(sums_0))
        y_last, y_last_far = placed(y_back)
        dx_own, dx_far, mod_early, dx_last, taps_a = tokens_call(2, 1, ())
        x_back = lax.ppermute(dx_last, "wide", partner)
        y_last_far = lax.ppermute(y_last_far, "narrow", swap)
        head_grads, sums_1, attn_sums = joined(head_grads, sums_1, attn_sums)
        attn_sums = between_pair(attn_sums, 2)
        other_1 = narrow_other(sums_1)
        dx_own, dx_far, mod_early, _, taps_b = tokens_call(0, 2, (dx_own, dx_far, mod_early))
        mod_early, x_back, dx_far, attn_sums, y_own, sums_0, other_1 = joined(
            mod_early, x_back, dx_far, attn_sums, y_own, sums_0, other_1
        )
        attn_sums = between_far(attn_sums)
        x_last, x_last_far = placed(x_back)
        dx_far, x_last_far = [lax.ppermute(v, "narrow", swap) for v in (dx_far, x_last_far)]
        work_y = finished([(y_own, y_far), (y_last, y_last_far)])
        conv_one_grad = taps_a + taps_b
    else:
        work_y = rows_back(y_own, y_far)
        dx_own, dx_far, mod_early, _, taps_a = tokens_call(0, units, ())
        attn_sums, dx_far, other_0, other_1 = between_far(between_pair(attn_sums, 2)), dx_far, None, None
        work_x = rows_back(dx_own, dx_far)
        conv_one_grad = taps_a

    mod_grads = jnp.concatenate([mod_early, mod_late], 2)
    mod_grads = jnp.where(active[:, None, None, None], mod_grads, 0.0).astype(bf16).reshape(rows_here, 6 * D)
    tap_rows = jnp.pad(conv_one_grad.astype(bf16).reshape(-1), (0, 3 * D)).reshape(2, 6 * D)
    gathered, attn_sums, dx_far = gathered_everywhere(jnp.concatenate([mod_grads, tap_rows], 0), attn_sums, dx_far)
    if balanced:
        work_x = finished([(dx_own, dx_far), (x_last, x_last_far)])
    conv_one_sum = gathered[:, :, rows_here:].astype(f32).sum((0, 1)).reshape(-1)[: 9 * D].reshape(9, D)
    conv_one_sum = lax.dynamic_slice_in_dim(conv_one_sum, owner * shard, shard, axis=1)
    mod_all = gathered.reshape(-1, 6 * D)
    grad_ada = dot_tn(act_low, mod_all)
    grad_embed = jnp.where(real_row, silu_back(dot_nt(mod_all, ada_weight))[0], 0.0)
    grad_table = dot_tn(label_hot, grad_embed.astype(bf16))

    attn_final = narrow_sum(attn_sums, narrow_other(attn_sums) if balanced else None)
    final_qkv, final_out = attn_final[:, : 3 * D], attn_final[:, 3 * D :]
    second = narrow_sum(sums_1, other_1)
    ffn_final = jnp.stack([narrow_sum(sums_0, other_0), second[:, : 2 * columns]])
    final_up = ffn_final[:, :, :columns].reshape(PARTS, shard, per_part, owners, shard)
    final_up = final_up.transpose(1, 3, 0, 2, 4).reshape(shard, hidden_width)
    final_down = ffn_final[:, :, columns:].reshape(PARTS, shard, per_part, D).swapaxes(1, 2).reshape(-1, D)
    final_taps = second[:, 2 * columns : 2 * columns + 9 * PARTS * per_part].reshape(shard, PARTS, per_part, 9)
    final_taps = final_taps.transpose(3, 1, 2, 0).reshape(9, -1)
    return (
        work_y, work_x, conv_one_sum, final_qkv, final_out, final_up,
        final_taps, final_down, grad_ada, grad_table,
    )


def solution(mesh):
    rows = P("wide", None)
    columns = P(None, "wide")
    canvases = P("wide", "narrow", None)
    return jax.shard_map(
        body,
        mesh=mesh,
        in_specs=(canvases, canvases, columns, rows, rows, rows, columns, rows, rows, columns, P(), P(), P(), P()),
        out_specs=(canvases, canvases, columns, rows, rows, rows, columns, rows, rows, columns),
        check_vma=False,
    )
```

```python
from functools import partial
import math

import jax
import jax.numpy as jnp
import numpy as np
from jax import lax
from jax.experimental import pallas as pl
from jax.experimental.pallas import tpu as pltpu
from jax.sharding import PartitionSpec as P

HEAD_DIM = 64
GRID = 32
LATENT = 256
HALF = 2 * LATENT
PARTS = 2
ROWS = 128
GROUP = 256
VMEM_BYTES = 67000000

norm_eps = 1e-06
bf16 = jnp.bfloat16
f32 = jnp.float32


def dot(a, b):
    return lax.dot_general(a, b, (((1,), (0,)), ((), ())), preferred_element_type=f32)


def dot_nt(a, b):
    return lax.dot_general(a, b, (((1,), (1,)), ((), ())), preferred_element_type=f32)


def dot_tn(a, b):
    return lax.dot_general(a, b, (((0,), (0,)), ((), ())), preferred_element_type=f32)


def norm_parts(values):
    centred = values - jnp.mean(values, axis=-1, keepdims=True)
    inverse = lax.rsqrt(jnp.mean(centred * centred, axis=-1, keepdims=True) + norm_eps)
    return centred * inverse, inverse


def norm_back(grad_normed, normed, inverse):
    return inverse * (
        grad_normed
        - jnp.mean(grad_normed, axis=-1, keepdims=True)
        - normed * jnp.mean(grad_normed * normed, axis=-1, keepdims=True)
    )


def edges(narrow_grid):
    place = lax.broadcasted_iota(jnp.int32, (64, 128), 0)
    place = jnp.where(narrow_grid, place % 8, place % 16)
    return place == 0, place == jnp.where(narrow_grid, 7, 15)


def neighbours(blocks, narrow_grid, ends, kind=f32):
    first, last = ends
    gap = jnp.zeros((16, 128), blocks[0].dtype)

    def earlier(v):
        padded = jnp.concatenate([gap, v], 0)
        return jnp.where(narrow_grid, padded[8:72], padded[:64])

    def later(v):
        padded = jnp.concatenate([v, gap], 0)
        return jnp.where(narrow_grid, padded[8:72], padded[16:80])

    columns, moved = [], []
    for row_parity in range(2):
        even, odd = blocks[2 * row_parity], blocks[2 * row_parity + 1]
        before = jnp.where(first, 0.0, pltpu.roll(odd, 1, 0))
        after = jnp.where(last, 0.0, pltpu.roll(even, 63, 0))
        shift = later if row_parity == 0 else earlier
        b, e, o, a = [shift(v).astype(kind) for v in (before, even, odd, after)]
        before, even, odd, after = [v.astype(kind) for v in (before, even, odd, after)]
        columns.append(((before, even, odd), (even, odd, after)))
        moved.append(((b, e, o), (e, o, a)))
    found = []
    for row_parity in range(2):
        for parity in range(2):
            same, other, far = columns[row_parity][parity], columns[1 - row_parity][parity], moved[1 - row_parity][parity]
            found.append((*far, *same, *other) if row_parity == 0 else (*other, *same, *far))
    return found


def weighted(found, taps):
    total = found[0] * taps[0]
    for tap in range(1, 9):
        total = total + found[tap] * taps[tap]
    return total


def phase_rows(latent):
    return [slice(latent * LATENT + 64 * phase, latent * LATENT + 64 * phase + 64) for phase in range(4)]


def add_taps(store, which, lanes, found, grads):
    for tap in range(9):
        total = found[0][tap] * grads[0]
        for phase in range(1, 4):
            total = total + found[phase][tap] * grads[phase]
        store[which, 8 * tap : 8 * tap + 8, lanes] += jnp.sum(total.astype(f32).reshape(8, 8, total.shape[1]), axis=0)


def finish_taps(store, out):
    for tap in range(9):
        other = 3 * (tap % 3) + tap // 3
        total = store[0, 8 * tap : 8 * tap + 8, :] + store[1, 8 * other : 8 * other + 8, :]
        out[tap : tap + 1, :] = jnp.sum(total, axis=0, keepdims=True)


def head_mask():
    rows = lax.broadcasted_iota(jnp.int32, (GROUP, GROUP), 0) // HEAD_DIM
    cols = lax.broadcasted_iota(jnp.int32, (GROUP, GROUP), 1) // HEAD_DIM
    return jnp.where(rows == cols, 1.0, 0.0).astype(bf16)


def spread_heads(values, mask):
    return jnp.concatenate([values] * 4, 0) * mask


def head_max(values):
    low = lax.broadcasted_iota(jnp.int32, values.shape, 1) < HEAD_DIM
    lower = jnp.max(jnp.where(low, values, -jnp.inf), axis=-1, keepdims=True)
    upper = jnp.max(jnp.where(low, -jnp.inf, values), axis=-1, keepdims=True)
    return jnp.where(low, lower, upper)


def row_block(step, size, start=0):
    return pl.ds(pl.multiple_of(start + step * size, size), size)


def arrange(base, meta, tok, far_tok, places, out):
    @pl.when(meta[pl.program_id(0) + base] > 0)
    def _():
        @pl.loop(0, HALF // ROWS)
        def _(step):
            rows = row_block(step, ROWS)
            source = lax.broadcasted_iota(jnp.int32, (ROWS, 3 * LATENT), 1)
            hot = jnp.where(places[0, rows, :] == source, 1.0, 0.0).astype(bf16)
            values = dot(hot[:, :HALF], tok[0]) + dot(hot[:, HALF:], far_tok[0])
            out[0, rows, :] = values.astype(bf16)


def put_back(result, spots, own, far):
    for step in range(3 * LATENT // ROWS):
        target = lax.broadcasted_iota(jnp.int32, (ROWS, HALF), 0) + step * ROWS
        hot = jnp.where(spots[0] == target, 1.0, 0.0).astype(bf16)
        values = dot(hot, result[0]).astype(bf16)
        if step * ROWS < HALF:
            own[0, step * ROWS : (step + 1) * ROWS, :] = values
        else:
            far[0, step * ROWS - HALF : (step + 1) * ROWS - HALF, :] = values


def place_back(meta, result, spots, own, far):
    @pl.when(meta[3] > 0)
    def _():
        put_back(result, spots, own, far)


def mix_tokens(base, taken, meta, *refs):
    if taken:
        x, other, mod, taps, x_o, mix_o, hidden = refs
    else:
        x, mod, taps, x_o, mix_o, hidden = refs
    unit = pl.program_id(0) + base

    @pl.when(meta[unit] > 0)
    def _():
        for latent in range(2):
            shift, scale = mod[0, latent, 0:1, :], 1.0 + mod[0, latent, 1:2, :]

            @pl.loop(0, LATENT // ROWS)
            def _(step):
                rows = row_block(step, ROWS, latent * LATENT)
                values = x[0, rows, :].astype(f32)
                if taken:
                    values = jnp.where(meta[0] > 0, values, other[0, rows, :].astype(f32))
                x_o[0, rows, :] = values.astype(bf16)
                normed, _ = norm_parts(values)
                hidden[rows, :] = (normed * scale + shift).astype(bf16).astype(f32)

        narrow_grid = meta[meta.shape[0] // 2 + unit] == 0
        ends = edges(narrow_grid)

        @pl.loop(0, x.shape[2] // 128)
        def _(step):
            lanes = row_block(step, 128)
            weights = [taps[0, tap : tap + 1, lanes] for tap in range(9)]
            for latent in range(2):
                found = neighbours([hidden[r, lanes] for r in phase_rows(latent)], narrow_grid, ends)
                for rows, near in zip(phase_rows(latent), found):
                    mix_o[0, rows, lanes] = weighted(near, weights).astype(bf16)


def attend(base, meta, x, mix, mod, weights, qkv_o, prob_o, att_o, branch_o, mid_o, ffn_o):
    unit = pl.program_id(0) + base
    width = x.shape[2]
    groups = width // GROUP

    @pl.when(meta[unit] > 0)
    def _():
        @pl.loop(0, 3 * width // 256)
        def _(step):
            lanes = row_block(step, 256)
            qkv_o[0, :, lanes] = dot(mix[0], weights[:, lanes]).astype(bf16)

        mask = head_mask()

        @pl.loop(0, HALF // 256)
        def _(step):
            chains = []
            for block in range(4):
                rows = row_block(step * 4 + block, 64)
                for group in range(groups):
                    at = GROUP * group
                    keys = spread_heads(qkv_o[0, rows, width + at : width + at + GROUP], mask)
                    chains.append((rows, group, dot_nt(qkv_o[0, rows, at : at + GROUP], keys) * 0.125))
            raised = [
                jnp.concatenate([jnp.exp(s[:, c : c + 128] - head_max(s[:, c : c + 128])) for c in (0, 128)], 1)
                for _, _, s in chains
            ]
            totals = [dot(e.astype(bf16), mask) for e in raised]
            for (rows, group, _), e, total in zip(chains, raised, totals):
                probs = (e / total).astype(bf16)
                at = GROUP * group
                values = spread_heads(qkv_o[0, rows, 2 * width + at : 2 * width + at + GROUP], mask)
                prob_o[0, rows, at : at + GROUP] = probs
                att_o[0, rows, at : at + GROUP] = dot(probs, values).astype(bf16)

        for latent in range(2):
            gate_a = mod[0, latent, 2:3, :]
            shift, scale = mod[0, latent, 3:4, :], 1.0 + mod[0, latent, 4:5, :]

            @pl.loop(0, LATENT // ROWS)
            def _(step):
                rows = row_block(step, ROWS, latent * LATENT)
                branch = dot(att_o[0, rows, :], weights[:, 3 * width :])
                branch_o[0, rows, :] = branch.astype(bf16)
                middle = x[0, rows, :].astype(f32) + gate_a * branch
                mid_o[0, rows, :] = middle
                normed, _ = norm_parts(middle)
                ffn_o[0, rows, :] = (normed * scale + shift).astype(bf16)


def feed_forward(part, taken, meta, *refs):
    if part == 0:
        if taken:
            cot, other, mod, ffn, weights, taps, *refs = refs
        else:
            cot, mod, ffn, weights, taps, *refs = refs
        gbb_o, bb_o, gf_o, grad_o, tap_o, *refs = refs
        gbb = gbb_o
    else:
        gbb, ffn, weights, taps, bb_i, gf_i, mid, mod, spots, tap_i, *refs = refs
        gf_o, y_o, own_o, far_o, grad_o, tap_o, bb_o, *refs = refs
    ffn_t, gbb_t, acc_up, acc_down, dtap, *slots = refs
    unit = pl.program_id(0)
    width = ffn.shape[2]
    columns = taps.shape[2]
    items = columns // 256
    per_block = width // 256

    @pl.when(unit == 0)
    def _():
        acc_up[...] = jnp.zeros_like(acc_up)
        acc_down[...] = jnp.zeros_like(acc_down)
        dtap[...] = jnp.zeros_like(dtap)

    @pl.when(meta[unit] > 0)
    def _():
        if part == 0:
            for latent in range(2):
                gate, weight = mod[0, latent, 5:6, :], mod[0, latent, 6:7, :]

                @pl.loop(0, LATENT // 64)
                def _(step):
                    rows = row_block(step, 64, latent * LATENT)
                    grads = cot[0, rows, :].astype(f32)
                    if taken:
                        from_other = jnp.logical_and(unit == 2, meta[0] == 0)
                        grads = jnp.where(from_other, other[0, rows, :].astype(f32), grads)
                    gbb_o[0, rows, :] = (gate * (grads * weight)).astype(bf16)

        layout = meta[meta.shape[0] // 2 + unit]
        which = jnp.where(layout == 2, 1, 0)
        narrow_grid = layout == 0
        ends = edges(narrow_grid)
        uses = [slots[i::2] for i in range(2)]
        uses[1][2][...] = jnp.zeros_like(uses[1][2])
        uses[1][3][...] = jnp.zeros_like(uses[1][3])
        root = math.sqrt(2.0 / math.pi)

        @pl.loop(0, HALF // 128)
        def _(step):
            rows = row_block(step, 128)
            if part == 0:
                bb_o[0, rows, :] = jnp.zeros((128, width), f32)
                gf_o[0, rows, :] = jnp.zeros((128, width), f32)
            else:
                bb_o[0, rows, :] = bb_i[0, rows, :]
                gf_o[0, rows, :] = gf_i[0, rows, :]

        def down_rows(item):
            block = item // per_block
            return row_block(item - block * per_block, 256), row_block(block, width, columns)

        def project(item, use):
            upward, grad_act = use[0], use[1]
            rows, lanes = down_rows(item)
            upward[...] = dot(ffn[0], weights[:, row_block(item, 256)]).astype(bf16).astype(f32)
            grad_act[...] = dot_nt(gbb[0], weights[rows, lanes])

        def collect(item, use):
            act, grad_up = use[2], use[3]
            rows, lanes = down_rows(item)
            here = row_block(item, 256)
            bb_o[0] += dot(act[...], weights[rows, lanes])
            gf_o[0] += dot_nt(grad_up[...], weights[:, here])
            acc_up[:, here] += dot(ffn_t[...], grad_up[...])
            acc_down[:, here] += dot(gbb_t[...], act[...])

        def convolve(item, use):
            upward, grad_act, act, grad_up = use
            for side in range(2):
                cols = slice(128 * side, 128 * side + 128)
                lanes = row_block(2 * item + side, 128)
                taken_taps = [taps[0, tap : tap + 1, lanes].astype(bf16) for tap in range(9)]
                for latent in range(2):
                    rows = phase_rows(latent)
                    found = neighbours([upward[r, cols] for r in rows], narrow_grid, ends, bf16)
                    grads = []
                    for r, near in zip(rows, found):
                        spread = weighted(near, taken_taps).astype(f32)
                        square = spread * spread
                        bent = jnp.tanh(spread * (root + root * 0.044715 * square))
                        half = 0.5 + 0.5 * bent
                        curve = spread * half
                        act[r, cols] = curve.astype(bf16)
                        slope = half + (curve * (1.0 - half)) * (2.0 * root + 6.0 * root * 0.044715 * square)
                        grads.append((grad_act[r, cols] * slope).astype(bf16).astype(f32))
                    add_taps(dtap, which, lanes, found, [g.astype(bf16) for g in grads])
                    for r, near in zip(rows, neighbours(grads, narrow_grid, ends, bf16)):
                        grad_up[r, cols] = weighted(near, taken_taps[::-1]).astype(bf16)

        ffn_t[...] = ffn[0].T
        gbb_t[...] = gbb[0].T
        project(0, uses[0])

        @pl.loop(0, items // 2)
        def _(pair):
            for side in range(2):
                item = 2 * pair + side
                convolve(item, uses[side])
                project(jnp.minimum(item + 1, items - 1), uses[1 - side])
                collect(jnp.maximum(item - 1, 0), uses[1 - side])

        collect(items - 1, uses[1])

        if part == PARTS - 1:
            for latent in range(2):
                gate = mod[0, latent, 5:6, :]

                @pl.loop(0, LATENT // 64)
                def _(step):
                    rows = row_block(step, 64, latent * LATENT)
                    y_o[0, rows, :] = (mid[0, rows, :] + gate * bb_o[0, rows, :]).astype(bf16)

            put_back(y_o, spots, own_o, far_o)

    @pl.when(unit == pl.num_programs(0) - 1)
    def _():
        finish_taps(dtap, tap_o)
        if part == PARTS - 1:
            rows = [t[:, at : at + width] for t in (tap_i, tap_o) for at in range(0, columns, width)]
            rows.append(jnp.zeros((128 - 9 * len(rows), width), f32))
            grad_o[:, 2 * columns :] = jnp.concatenate(rows, 0).T.astype(bf16)
        grad_o[:, :columns] = acc_up[...].astype(bf16)
        for at in range(0, columns, width):
            grad_o[:, columns + at : columns + at + width] = acc_down[:, at : at + width].astype(bf16).T


def backward_middle(taken, meta, *refs):
    if taken:
        cot, other, *refs = refs
    else:
        cot, *refs = refs
    bb, gf, mid, branch, att, mod, out_w, grad_mid, grad_att, mod_o, dout_o, gba, acc_out, att_t = refs
    unit = pl.program_id(0)
    width = cot.shape[2]

    @pl.when(unit == 0)
    def _():
        acc_out[...] = jnp.zeros_like(acc_out)

    @pl.when(meta[unit] > 0)
    def _():
        mod_o[...] = jnp.zeros_like(mod_o)
        for latent in range(2):
            gate_a, scale_b = mod[0, latent, 2:3, :], 1.0 + mod[0, latent, 4:5, :]
            weight = mod[0, latent, 6:7, :]

            def tally(block, values):
                mod_o[0, latent, block : block + 1, :] += jnp.sum(values, axis=0, keepdims=True)

            @pl.loop(0, 4)
            def _(step):
                rows = row_block(step, 64, latent * LATENT)
                grads = cot[0, rows, :].astype(f32)
                if taken:
                    from_other = jnp.logical_and(unit == 2, meta[0] == 0)
                    grads = jnp.where(from_other, other[0, rows, :].astype(f32), grads)
                grad_out = grads * weight
                tally(3, grad_out * bb[0, rows, :])
                grad_ffn = gf[0, rows, :]
                normed, inverse = norm_parts(mid[0, rows, :])
                tally(1, grad_ffn)
                tally(2, grad_ffn * normed)
                total = grad_out + norm_back(grad_ffn * scale_b, normed, inverse)
                grad_mid[0, rows, :] = total
                tally(0, total * branch[0, rows, :].astype(f32))
                gba[rows, :] = (gate_a * total).astype(bf16)

        att_t[...] = att[0].T

        @pl.loop(0, width // 256)
        def _(step):
            lanes = row_block(step, 256)
            acc_out[:, lanes] += dot(att_t[...], gba[:, lanes])
            grad_att[0, :, lanes] = dot_nt(gba[...], out_w[lanes, :]).astype(bf16)

    @pl.when(unit == pl.num_programs(0) - 1)
    def _():
        dout_o[...] = acc_out[...].astype(bf16)


def backward_heads(shard, meta, odd, qkv, grad_att, prob, mix, dout, dqkv_o, keep_o, send_o, acc, mix_t):
    unit = pl.program_id(0)
    width = grad_att.shape[2]

    @pl.when(unit == 0)
    def _():
        acc[...] = jnp.zeros_like(acc)

    @pl.when(meta[unit] > 0)
    def _():
        mask = head_mask()
        low = lax.broadcasted_iota(jnp.int32, (64, 128), 1) < HEAD_DIM
        mix_t[...] = mix[0].T

        @pl.loop(0, HALF // 256)
        def _(step):
            chains = []
            for block in range(4):
                rows = row_block(4 * step + block, 64)
                for at in range(0, width, GROUP):
                    grads = grad_att[0, rows, at : at + GROUP]
                    values = spread_heads(qkv[0, rows, 2 * width + at : 2 * width + at + GROUP], mask)
                    chains.append((rows, at, grads, dot_nt(grads, values), prob[0, rows, at : at + GROUP]))
            inners = []
            for _, _, _, grad_probs, probs in chains:
                product = probs.astype(f32) * grad_probs
                high = product.astype(bf16)
                rest = (product - high.astype(f32)).astype(bf16)
                inners.append(dot(high, mask) + dot(rest, mask))
            scores = [
                (probs.astype(f32) * (grad_probs - inner)).astype(bf16)
                for (_, _, _, grad_probs, probs), inner in zip(chains, inners)
            ]
            for (rows, at, grads, _, probs), grad_scores in zip(chains, scores):
                query = qkv[0, rows, at : at + GROUP]
                keys = spread_heads(qkv[0, rows, width + at : width + at + GROUP], mask)
                dqkv_o[0, rows, at : at + GROUP] = (dot(grad_scores, keys) * 0.125).astype(bf16)
                for pair in range(2):
                    lanes = slice(128 * pair, 128 * pair + 128)
                    both = dot_tn(grad_scores[:, lanes], query[:, lanes]) * 0.125
                    to = width + at + 128 * pair
                    dqkv_o[0, rows, to : to + 128] = jnp.where(low, both[:64], both[64:]).astype(bf16)
                    both = dot_tn(probs[:, lanes], grads[:, lanes])
                    to = 2 * width + at + 128 * pair
                    dqkv_o[0, rows, to : to + 128] = jnp.where(low, both[:64], both[64:]).astype(bf16)

        @pl.loop(0, 3 * width // 256)
        def _(step):
            lanes = row_block(step, 256)
            acc[:, lanes] += dot(mix_t[...], dqkv_o[0, :, lanes])

    @pl.when(unit == pl.num_programs(0) - 1)
    def _():
        def put(parity):
            for owner in range(width // shard):
                out = keep_o if owner % 2 == parity else send_o
                rows, to = slice(owner * shard, (owner + 1) * shard), slice(owner // 2 * shard, (owner // 2 + 1) * shard)
                out[to, : 3 * width] = acc[rows, :].astype(bf16)
                out[to, 3 * width :] = dout[rows, :]

        @pl.when(odd[0] == 0)
        def _():
            put(0)

        @pl.when(odd[0] != 0)
        def _():
            put(1)


def backward_tokens(
    base, meta, dqkv, x, gm, mod, taps, spots, qkv_w,
    own_o, far_o, mod_o, dx_o, tap_o, grad_mix, hidden, grad_hidden, dtap,
):
    unit = pl.program_id(0) + base
    width = x.shape[2]

    @pl.when(pl.program_id(0) == 0)
    def _():
        dtap[...] = jnp.zeros_like(dtap)

    @pl.when(meta[unit] > 0)
    def _():
        mod_o[...] = jnp.zeros_like(mod_o)

        @pl.loop(0, width // 256)
        def _(step):
            rows = row_block(step, 256)
            grad_mix[:, rows] = dot_nt(dqkv[0], qkv_w[rows, :]).astype(bf16).astype(f32)

        for latent in range(2):
            shift, scale = mod[0, latent, 0:1, :], 1.0 + mod[0, latent, 1:2, :]

            @pl.loop(0, 4)
            def _(step):
                rows = row_block(step, 64, latent * LATENT)
                normed, _ = norm_parts(x[0, rows, :].astype(f32))
                hidden[rows, :] = (normed * scale + shift).astype(bf16).astype(f32)

        layout = meta[meta.shape[0] // 2 + unit]
        which = jnp.where(layout == 2, 1, 0)
        narrow_grid = layout == 0
        ends = edges(narrow_grid)

        @pl.loop(0, width // 128)
        def _(step):
            lanes = row_block(step, 128)
            weights = [taps[0, tap : tap + 1, lanes] for tap in range(9)]
            for latent in range(2):
                rows = phase_rows(latent)
                grads = [grad_mix[r, lanes] for r in rows]
                found = neighbours([hidden[r, lanes] for r in rows], narrow_grid, ends)
                add_taps(dtap, which, lanes, found, grads)
                for r, near in zip(rows, neighbours(grads, narrow_grid, ends)):
                    grad_hidden[r, lanes] = weighted(near, weights[::-1])

        for latent in range(2):
            scale = 1.0 + mod[0, latent, 1:2, :]

            def tally(block, values):
                mod_o[0, latent, block : block + 1, :] += jnp.sum(values, axis=0, keepdims=True)

            @pl.loop(0, 4)
            def _(step):
                rows = row_block(step, 64, latent * LATENT)
                normed, inverse = norm_parts(x[0, rows, :].astype(f32))
                grads = grad_hidden[rows, :]
                tally(0, grads)
                tally(1, grads * normed)
                total = gm[0, rows, :] + norm_back(grads * scale, normed, inverse)
                dx_o[0, rows, :] = total.astype(bf16)

        put_back(dx_o, spots, own_o, far_o)

    @pl.when(pl.program_id(0) == pl.num_programs(0) - 1)
    def _():
        finish_taps(dtap, tap_o)


def source_places(layouts, half):
    p = jnp.arange(HALF, dtype=jnp.int32)
    latent, q = p // LATENT, p % 64
    row_parity, column_parity = (p // 128) % 2, (p // 64) % 2
    square = (2 * (q // 8) + row_parity) * GRID + 16 * latent + 2 * (q % 8) + column_parity
    low_row, wide_col = 2 * (q // 16) + row_parity, 2 * (q % 16) + column_parity
    across = (8 * latent + low_row) * GRID + wide_col
    column = 8 * latent + low_row
    own = (wide_col - 16 * half) * GRID + 16 * half + column
    other = HALF + (wide_col - 16 * (1 - half)) * 16 + column
    downward = jnp.where(wide_col // 16 == half, own, other)
    kind = layouts[:, None]
    return jnp.where(kind == 0, square, jnp.where(kind == 1, across, downward))


def turned(taps):
    return taps.reshape(taps.shape[:-2] + (3, 3, taps.shape[-1])).swapaxes(-3, -2).reshape(taps.shape)


def bit_of(index, bit):
    return (index // bit) % 2


def swapped(values, bit):
    count = lax.axis_size("wide")
    return lax.ppermute(values, "wide", [(i, i ^ bit) for i in range(count)])


def bits_of(count):
    return [1 << b for b in range(count.bit_length() - 1)]


def ordered(values, other, bit):
    low = bit_of(lax.axis_index("wide"), bit) == 0
    return jnp.where(low, values, other), jnp.where(low, other, values)


def gathered_far(values):
    count = lax.axis_size("wide")
    found = {0: values}
    for mask in range(4, count, 4):
        found[mask] = swapped(values, mask)
    for bit in bits_of(count)[2:]:
        found = {
            mask: jnp.stack(ordered(found[mask], found[mask | bit], bit), 0) for mask in found if not mask & bit
        }
    return found[0].reshape((count // 4,) + values.shape)


def gathered_near(values, bit, axis, *waits):
    other = swapped(values, bit)
    values, *waits = joined(values, *waits)
    return jnp.stack(ordered(values, other, bit), axis), *waits


def summed(keep, other):
    return (keep.astype(f32) + other.astype(f32)).astype(keep.dtype)


def between_pair(values, bit):
    pairs = values.reshape((values.shape[0] // 2, 2) + values.shape[1:])
    keep, send = ordered(pairs[:, 0], pairs[:, 1], bit)
    return summed(keep, swapped(send, bit))


def between_far(values):
    place = lax.axis_index("wide") // 4
    total = lax.dynamic_index_in_dim(values, place, 0, keepdims=False).astype(f32)
    for mask in range(4, lax.axis_size("wide"), 4):
        send = lax.dynamic_index_in_dim(values, place ^ (mask // 4), 0, keepdims=False)
        total = total + swapped(send, mask).astype(f32)
    return total.astype(values.dtype)


def gathered_everywhere(values, *waits):
    lane, count = lax.axis_index("narrow"), lax.axis_size("narrow")
    if count == 2:
        other = lax.ppermute(values, "narrow", [(0, 1), (1, 0)])
        values = jnp.where(lane == 0, jnp.stack([values, other]), jnp.stack([other, values]))
    else:
        values = lax.all_gather(values, "narrow", axis=0)
    values = values[None]
    for bit in reversed(bits_of(lax.axis_size("wide"))):
        if bit == 2:
            values, *waits = joined(values, *waits)
        values = jnp.stack(ordered(values, swapped(values, bit), bit), 1)
        values = values.reshape((-1,) + values.shape[2:])
    return values, *waits


def joined(*values):
    return lax.optimization_barrier(values)


def after(value, *earlier):
    return lax.optimization_barrier((value, *earlier))[0]


def narrow_other(values):
    return lax.ppermute(values, "narrow", [(0, 1), (1, 0)])


def narrow_sum(values, other):
    if other is None:
        return lax.psum(values, "narrow").astype(f32)
    return values.astype(f32) + other.astype(f32)


def body(
    tokens, cotangent, conv_attn, qkv_weight, out_weight, up_weight, conv_ffn, down_weight,
    ada_weight, class_table, timesteps, labels, layout, counts,
):
    slots, local_tokens, D = tokens.shape
    owners, narrow = lax.axis_size("wide"), lax.axis_size("narrow")
    owner, lane = lax.axis_index("wide"), lax.axis_index("narrow")
    shard = D // owners
    half = lane % 2
    spread = narrow // 2
    balanced = narrow == 2 and slots == 4
    units = 3 if balanced else slots // spread
    hidden_width = up_weight.shape[1]
    columns = hidden_width // PARTS
    per_part = columns // D

    loads = (counts > 0).astype(jnp.int32).reshape(owners, slots)

    def all_units(values):
        values = values.reshape((owners, slots) + values.shape[1:])
        if balanced:
            idle = (loads.sum(1) == 0).reshape((owners,) + (1,) * (values.ndim - 2))
            other = jnp.roll(values[:, 3], owners // 2, axis=0)
            return jnp.stack([values[:, 0], values[:, 1], jnp.where(idle, other, values[:, 2])], 1)
        return values

    def my_units(values):
        values = lax.dynamic_index_in_dim(all_units(values), owner, 0, keepdims=False)
        if balanced:
            return values
        values = values.reshape((units, spread) + values.shape[1:])
        return lax.dynamic_index_in_dim(values, lane // 2, 1, keepdims=False)

    rows_here = units * 2

    def latent_rows(values):
        values = all_units(values)
        if balanced:
            values = values.reshape(owners, units, 2, 2).transpose(0, 2, 1, 3)
        else:
            values = values.reshape(owners, units, spread, 2, 2).transpose(0, 2, 3, 1, 4)
        values = values.reshape(owners, narrow, rows_here)
        return jnp.pad(values, ((0, 0), (0, 0), (0, 2)), constant_values=-1).reshape(-1)

    count_float = counts.astype(f32)
    scales = count_float * float(counts.shape[0]) / jnp.sum(count_float)
    my_layout, my_scale = my_units(layout), my_units(scales)
    active = my_units(counts) > 0
    meta = jnp.concatenate([active.astype(jnp.int32), my_layout])
    places = source_places(my_layout, half)

    half_width = D // 2
    my_columns = owner * shard + jnp.arange(shard, dtype=jnp.int32)
    freqs = jnp.exp(-math.log(10000.0) * (my_columns % half_width).astype(f32) / half_width)
    angles = latent_rows(timesteps)[:, None].astype(f32) * freqs
    label_hot = (latent_rows(labels)[:, None] == jnp.arange(class_table.shape[0], dtype=jnp.int32)).astype(bf16)
    embed = jnp.where(my_columns < half_width, jnp.cos(angles), jnp.sin(angles)) + dot(label_hot, class_table)
    activ, silu_back = jax.vjp(jax.nn.silu, embed)
    real_row = (latent_rows(labels) >= 0)[:, None]
    act_low = jnp.where(real_row, activ, 0.0).astype(bf16)
    mine = act_low.reshape(owners, narrow, rows_here + 2, shard)[:, :, :rows_here]
    mine = lax.dynamic_index_in_dim(mine, lane, 1, keepdims=False)
    partial_mod = dot(mine.reshape(-1, shard), ada_weight).astype(bf16).reshape(owners, rows_here, -1)
    both_taps = jnp.concatenate([conv_attn, conv_ffn], 1).reshape(-1)
    tap_size = both_taps.shape[0]
    tap_lanes = -(-tap_size // (units * 2 * 128)) * 128
    both_taps = jnp.pad(both_taps, (0, units * 2 * tap_lanes - tap_size)).reshape(1, units * 2, tap_lanes)
    sent = jnp.concatenate([partial_mod, jnp.broadcast_to(both_taps, (owners, units * 2, tap_lanes))], 2)
    arrived = lax.all_to_all(sent, "wide", 0, 0, tiled=True)
    modulation = jnp.sum(arrived[:, :, : 6 * D].astype(f32), axis=0).reshape(units, 2, 6, D)
    both_taps = arrived[:, :, 6 * D :].reshape(owners, -1)[:, :tap_size].reshape(owners, 9, -1).astype(f32)
    conv_one = both_taps[:, :, :shard].swapaxes(0, 1).reshape(9, D)
    conv_two = both_taps[:, :, shard:].reshape(owners, 9, PARTS, per_part, shard).transpose(2, 1, 3, 0, 4)
    conv_two = conv_two.reshape(PARTS, 9, columns)
    weight_row = jnp.broadcast_to(my_scale[:, None, None, None], (units, 2, 1, D))
    mod = jnp.concatenate([modulation, weight_row], 2)

    attn_far = gathered_far(jnp.concatenate([qkv_weight, out_weight], 1))
    up_parts = up_weight.reshape(shard, owners, PARTS, per_part, shard).transpose(2, 0, 3, 1, 4)
    up_parts = up_parts.reshape(PARTS, shard, columns)
    down_parts = down_weight.reshape(PARTS, per_part, shard, D).swapaxes(1, 2).reshape(PARTS, shard, columns)
    ffn_parts = jnp.concatenate([up_parts, down_parts], 2)

    def all_rows(values):
        return lax.all_gather(values, "wide", axis=0, tiled=True)


    def unit_taps(taps):
        return jnp.where((my_layout == 2)[:, None, None], turned(taps), taps)

    taps_one = unit_taps(conv_one)

    params = pltpu.CompilerParams(vmem_limit_bytes=VMEM_BYTES, dimension_semantics=("arbitrary",))
    any_space = pl.BlockSpec(memory_space=pl.ANY)

    def per_unit(*shape, base=0):
        return pl.BlockSpec((1,) + shape, lambda i, meta: (i + base,) + (0,) * len(shape))

    def whole(*shape):
        return pl.BlockSpec(shape, lambda i, meta: (0,) * len(shape), pipeline_mode=pl.Buffered(1))

    def struct(*shape, kind=bf16):
        return jax.ShapeDtypeStruct(shape, kind)

    def call(kernel, name, count, flags, ins, in_specs, outs, out_specs, scratch=(), flops=0, before=()):
        aliases = {1 + len(ins) + i: i for i in range(len(before))}
        extra = len(before)

        def run(meta, *refs):
            kept = refs[: len(ins)] + refs[len(ins) + extra :]
            kernel(meta, *kept)

        return pl.pallas_call(
            run,
            grid_spec=pltpu.PrefetchScalarGridSpec(
                num_scalar_prefetch=1, grid=(count,), in_specs=list(in_specs) + [any_space] * extra,
                out_specs=out_specs, scratch_shapes=list(scratch),
            ),
            out_shape=outs,
            input_output_aliases=aliases,
            compiler_params=params,
            cost_estimate=pl.CostEstimate(flops=int(flops * count * 0.25), bytes_accessed=int(1e6 * count), transcendentals=0),
            name=name,
        )(flags, *ins, *before)

    tokens_shape = (HALF, D)

    def arranged(base, count, tok, far, far_base, where, flags):
        return call(
            partial(arrange, base), "arrange", count, flags, [tok, far, where[:, :, None]],
            [per_unit(*tokens_shape, base=base), per_unit(LATENT, D, base=far_base), per_unit(HALF, 1, base=base)],
            struct(count, *tokens_shape), per_unit(*tokens_shape), flops=2e9,
        )

    if balanced:
        own_layout = lax.dynamic_slice_in_dim(layout, owner * slots, slots)
        own_active = lax.dynamic_slice_in_dim(counts, owner * slots, slots) > 0
        own_places = source_places(own_layout, half)
        own_flags = jnp.concatenate([own_active.astype(jnp.int32), own_layout])
        swap = [(0, 1), (1, 0)]
        partner = [(i, (i + owners // 2) % owners) for i in range(owners)]

        def for_other_half(values, first, count):
            part = values.reshape(slots, 16, GRID, D)[first : first + count]
            part = lax.dynamic_slice_in_dim(part, 16 * (1 - half), 16, axis=2)
            return lax.ppermute(part.reshape(-1, LATENT, D), "narrow", swap)

        own_tok, own_cot = [v.reshape(slots, HALF, D) for v in (tokens, cotangent)]
        x_last = arranged(3, 1, own_tok, for_other_half(tokens, 3, 1), 0, own_places, own_flags)
        attn_far, x_last, cot_far_last = joined(attn_far, x_last, for_other_half(cotangent, 3, 1))
        x_other = lax.ppermute(x_last, "wide", partner)
        x_own = arranged(0, 3, own_tok, for_other_half(tokens, 0, 3), 0, own_places, own_flags)
        cot_far = for_other_half(after(cotangent, attn_far), 0, 3)
    else:

        def to_units(values):
            full = lax.all_gather(values, "narrow", axis=1, tiled=True)
            full = full.reshape(units, spread, 2, 16, GRID, D)
            full = lax.dynamic_index_in_dim(full, lane // 2, 1, keepdims=False)
            here = lax.dynamic_index_in_dim(full, half, 1, keepdims=False)
            far = lax.dynamic_index_in_dim(full, 1 - half, 1, keepdims=False)
            far = lax.dynamic_slice_in_dim(far, 16 * half, 16, axis=2)
            return arranged(0, units, here.reshape(units, HALF, D), far.reshape(units, LATENT, D), 0, places, meta)

        x_own = to_units(tokens)
        cot_own = to_units(cotangent)
        ffn_first = all_rows(after(ffn_parts[0], attn_far))
        cots, cot_specs = [cot_own], [per_unit(*tokens_shape)]

    unit_values = struct(units, *tokens_shape)
    unit_floats = struct(units, *tokens_shape, kind=f32)

    def mix_call(base, count, taken, before):
        spec = per_unit(*tokens_shape, base=base)
        ins, specs = [x_own], [spec]
        if taken:
            ins, specs = ins + [x_other], specs + [whole(1, *tokens_shape)]
        return call(
            partial(mix_tokens, base, taken), "mix_tokens", count, meta, ins + [mod, taps_one],
            specs + [per_unit(2, 7, D, base=base), per_unit(9, D, base=base)],
            [unit_values, unit_values], [spec, spec], [pltpu.VMEM(tokens_shape, f32)], 3e9, before,
        )

    def attend_call(base, count, before):
        spec = per_unit(*tokens_shape, base=base)
        return call(
            partial(attend, base), "attend", count, meta, [x, mixed, mod, attn_full],
            [spec, spec, per_unit(2, 7, D, base=base), whole(D, 4 * D)],
            [struct(units, HALF, 3 * D), unit_values, unit_values, unit_values, unit_floats, unit_values],
            [per_unit(HALF, 3 * D, base=base)] + [spec] * 5, (), 8e9, before,
        )

    if balanced:
        x, mixed = mix_call(0, 2, False, ())
        attn_near, mixed, x_other, cot_far = gathered_near(attn_far, 2, 1, mixed, x_other, cot_far)
        cot_own = arranged(0, 3, own_cot, cot_far, 0, own_places, own_flags)
        ffn_first = all_rows(after(ffn_parts[0], attn_near))
        cot_last = arranged(3, 1, own_cot, cot_far_last, 0, own_places, after(own_flags, attn_near))
        cot_other = lax.ppermute(cot_last, "wide", partner)
        attn_full, cot_own = gathered_near(attn_near, 1, 2, cot_own)
        attn_full = attn_full.reshape(D, 4 * D)
        front = attend_call(0, 2, ())
        ffn_second = all_rows(after(ffn_parts[1], attn_full))
        x, mixed = mix_call(2, 1, True, (x, mixed))
        front = attend_call(2, 1, front)
        cots, cot_specs = [cot_own, cot_other], [per_unit(*tokens_shape), whole(1, *tokens_shape)]
    else:
        x, mixed = mix_call(0, units, False, ())
        (attn_near,) = gathered_near(attn_far, 2, 1)
        (attn_full,) = gathered_near(attn_near, 1, 2)
        attn_full = attn_full.reshape(D, 4 * D)
        front = attend_call(0, units, ())
        ffn_second = all_rows(after(ffn_parts[1], attn_full))
    projected, probs, attended, branch, middle, ffn_in = front

    slot_pair = [pltpu.VMEM((HALF, 256), kind) for kind in (f32, f32, f32, f32, bf16, bf16, bf16, bf16)]
    work = [pltpu.VMEM((D, HALF), bf16), pltpu.VMEM((D, HALF), bf16)]
    work += [pltpu.VMEM((D, columns), f32), pltpu.VMEM((D, columns), f32), pltpu.VMEM((2, 72, columns), f32)]
    unit_spec = per_unit(*tokens_shape)
    tap_grad, tap_spec = struct(9, columns, kind=f32), whole(9, columns)
    weight_grad, weight_spec = struct(D, 2 * columns), whole(D, 2 * columns)
    spots = places[:, None, :]
    gbb, branch_b, grad_ffn, ffn_grad_0, ffn_taps_0 = call(
        partial(feed_forward, 0, balanced), "feed_forward", units, meta,
        cots + [mod, ffn_in, ffn_first, unit_taps(conv_two[0])],
        cot_specs + [per_unit(2, 7, D), unit_spec, weight_spec, per_unit(9, columns)],
        [unit_values, unit_floats, unit_floats, weight_grad, tap_grad],
        [unit_spec, unit_spec, unit_spec, weight_spec, tap_spec], work + slot_pair, 16e9,
    )

    def owner_sum(values):
        return lax.psum_scatter(values, "wide", scatter_dimension=0, tiled=True)

    sums_0 = owner_sum(ffn_grad_0)
    grad_ffn, y_units, y_own, y_far, ffn_grad_1, ffn_taps_1, branch_b = call(
        partial(feed_forward, 1, balanced), "feed_forward", units, meta,
        [gbb, ffn_in, ffn_second, unit_taps(conv_two[1]), branch_b, grad_ffn, middle, mod, spots, ffn_taps_0],
        [unit_spec, unit_spec, weight_spec, per_unit(9, columns), unit_spec, unit_spec, unit_spec,
         per_unit(2, 7, D), per_unit(1, HALF), tap_spec],
        [unit_floats, struct(1, *tokens_shape), unit_values, struct(units, LATENT, D), struct(D, 2 * columns + 128),
         tap_grad, unit_floats],
        [unit_spec, whole(1, *tokens_shape), unit_spec, per_unit(LATENT, D), whole(D, 2 * columns + 128), tap_spec,
         unit_spec],
        work + slot_pair, 17e9,
    )
    sums_1 = owner_sum(after(ffn_grad_1, sums_0))
    grad_ffn = after(grad_ffn, sums_0)

    grad_mid, grad_att, mod_late, out_grad = call(
        partial(backward_middle, balanced), "backward_middle", units, meta,
        cots + [branch_b, grad_ffn, middle, branch, attended, mod, attn_full],
        cot_specs + [unit_spec] * 5 + [per_unit(2, 7, D),
         pl.BlockSpec((D, D), lambda i, meta: (0, 3), pipeline_mode=pl.Buffered(1))],
        [unit_floats, unit_values, struct(units, 2, 4, D, kind=f32), struct(D, D)],
        [unit_spec, unit_spec, per_unit(2, 4, D), whole(D, D)],
        [pltpu.VMEM(tokens_shape, bf16), pltpu.VMEM((D, D), f32), pltpu.VMEM((D, HALF), bf16)], 4e9,
    )
    head_grads, attn_keep, attn_send = call(
        partial(backward_heads, shard), "backward_heads", units, meta,
        [(owner % 2).reshape(1), projected, grad_att, probs, mixed, out_grad],
        [pl.BlockSpec(memory_space=pltpu.SMEM), per_unit(HALF, 3 * D), unit_spec, unit_spec, unit_spec, whole(D, D)],
        [struct(units, HALF, 3 * D), struct(D // 2, 4 * D), struct(D // 2, 4 * D)],
        [per_unit(HALF, 3 * D), whole(D // 2, 4 * D), whole(D // 2, 4 * D)],
        [pltpu.VMEM((D, 3 * D), f32), pltpu.VMEM((D, HALF), bf16)], 12e9,
    )
    attn_sums = summed(attn_keep, swapped(attn_send, 1)).reshape(owners // 2, shard, 4 * D)

    def tokens_call(base, count, before):
        spec = per_unit(*tokens_shape, base=base)
        return call(
            partial(backward_tokens, base), "backward_tokens", count, meta,
            [head_grads, x, grad_mid, mod, taps_one, spots, attn_full],
            [per_unit(HALF, 3 * D, base=base), spec, spec, per_unit(2, 7, D, base=base), per_unit(9, D, base=base), per_unit(1, HALF, base=base),
             whole(D, 3 * D)],
            [unit_values, struct(units, LATENT, D), struct(units, 2, 2, D, kind=f32), struct(1, *tokens_shape),
             struct(9, D, kind=f32)],
            [spec, per_unit(LATENT, D, base=base), per_unit(2, 2, D, base=base), whole(1, *tokens_shape), whole(9, D)],
            [pltpu.VMEM(tokens_shape, f32)] * 3 + [pltpu.VMEM((2, 72, D), f32)], 60e9, before,
        )

    def finished(pieces):
        pairs = []
        for own, far in pieces:
            count = own.shape[0]
            far = far.reshape(count, 16, 16, D)
            empty = jnp.zeros_like(far)
            side = jnp.where(half == 0, jnp.concatenate([empty, far], 2), jnp.concatenate([far, empty], 2))
            pairs.append(own.reshape(count, 16, GRID, D) + side)
        total = jnp.concatenate(pairs, 0)
        return jnp.where(own_active[:, None, None, None], total, 0.0).reshape(slots, local_tokens, D)

    def placed(back):
        return call(
            place_back, "place_back", 1, own_flags, [back, own_places[3:, None, :]],
            [unit_spec, per_unit(1, HALF)], [struct(1, *tokens_shape), struct(1, LATENT, D)],
            [unit_spec, per_unit(LATENT, D)], (), 2e9,
        )

    def rows_back(own, far):
        own = jnp.where(active[:, None, None], own, 0.0).reshape(units, 1, 16, GRID, D)
        far = jnp.where(active[:, None, None], far, 0.0).reshape(units, 1, 16, 16, D)
        full = lax.dynamic_update_slice_in_dim(jnp.zeros((units, 2, 16, GRID, D), bf16), own, half, 1)
        other = lax.dynamic_update_slice_in_dim(jnp.zeros((units, 1, 16, GRID, D), bf16), far, 16 * half, 3)
        full = lax.dynamic_update_slice_in_dim(full, other, 1 - half, 1).reshape(units, 1, 2 * HALF, D)
        full = lax.dynamic_update_slice_in_dim(jnp.zeros((units, spread, 2 * HALF, D), bf16), full, lane // 2, 1)
        return lax.psum_scatter(full.reshape(slots, 2 * HALF, D), "narrow", scatter_dimension=1, tiled=True)

    if balanced:
        y_back = lax.ppermute(y_units, "wide", partner)
        y_far = lax.ppermute(y_far, "narrow", swap)
        head_grads, y_back, y_far, other_0 = joined(head_grads, y_back, y_far, narrow_other(sums_0))
        y_last, y_last_far = placed(y_back)
        dx_own, dx_far, mod_early, dx_last, taps_a = tokens_call(2, 1, ())
        x_back = lax.ppermute(dx_last, "wide", partner)
        y_last_far = lax.ppermute(y_last_far, "narrow", swap)
        head_grads, sums_1, attn_sums = joined(head_grads, sums_1, attn_sums)
        attn_sums = between_pair(attn_sums, 2)
        other_1 = narrow_other(sums_1)
        dx_own, dx_far, mod_early, _, taps_b = tokens_call(0, 2, (dx_own, dx_far, mod_early))
        mod_early, x_back, dx_far, attn_sums, y_own, sums_0, other_1 = joined(
            mod_early, x_back, dx_far, attn_sums, y_own, sums_0, other_1
        )
        attn_sums = between_far(attn_sums)
        x_last, x_last_far = placed(x_back)
        dx_far, x_last_far = [lax.ppermute(v, "narrow", swap) for v in (dx_far, x_last_far)]
        work_y = finished([(y_own, y_far), (y_last, y_last_far)])
        conv_one_grad = taps_a + taps_b
    else:
        work_y = rows_back(y_own, y_far)
        dx_own, dx_far, mod_early, _, taps_a = tokens_call(0, units, ())
        attn_sums, dx_far, other_0, other_1 = between_far(between_pair(attn_sums, 2)), dx_far, None, None
        work_x = rows_back(dx_own, dx_far)
        conv_one_grad = taps_a

    mod_grads = jnp.concatenate([mod_early, mod_late], 2)
    mod_grads = jnp.where(active[:, None, None, None], mod_grads, 0.0).astype(bf16).reshape(rows_here, 6 * D)
    tap_rows = jnp.pad(conv_one_grad.astype(bf16).reshape(-1), (0, 3 * D)).reshape(2, 6 * D)
    gathered, attn_sums, dx_far = gathered_everywhere(jnp.concatenate([mod_grads, tap_rows], 0), attn_sums, dx_far)
    if balanced:
        work_x = finished([(dx_own, dx_far), (x_last, x_last_far)])
    conv_one_sum = gathered[:, :, rows_here:].astype(f32).sum((0, 1)).reshape(-1)[: 9 * D].reshape(9, D)
    conv_one_sum = lax.dynamic_slice_in_dim(conv_one_sum, owner * shard, shard, axis=1)
    mod_all = gathered.reshape(-1, 6 * D)
    grad_ada = dot_tn(act_low, mod_all)
    grad_embed = jnp.where(real_row, silu_back(dot_nt(mod_all, ada_weight))[0], 0.0)
    grad_table = dot_tn(label_hot, grad_embed.astype(bf16))

    attn_final = narrow_sum(attn_sums, narrow_other(attn_sums) if balanced else None)
    final_qkv, final_out = attn_final[:, : 3 * D], attn_final[:, 3 * D :]
    second = narrow_sum(sums_1, other_1)
    ffn_final = jnp.stack([narrow_sum(sums_0, other_0), second[:, : 2 * columns]])
    final_up = ffn_final[:, :, :columns].reshape(PARTS, shard, per_part, owners, shard)
    final_up = final_up.transpose(1, 3, 0, 2, 4).reshape(shard, hidden_width)
    final_down = ffn_final[:, :, columns:].reshape(PARTS, shard, per_part, D).swapaxes(1, 2).reshape(-1, D)
    final_taps = second[:, 2 * columns : 2 * columns + 9 * PARTS * per_part].reshape(shard, PARTS, per_part, 9)
    final_taps = final_taps.transpose(3, 1, 2, 0).reshape(9, -1)
    return (
        work_y, work_x, conv_one_sum, final_qkv, final_out, final_up,
        final_taps, final_down, grad_ada, grad_table,
    )


def solution(mesh):
    rows = P("wide", None)
    columns = P(None, "wide")
    canvases = P("wide", "narrow", None)
    return jax.shard_map(
        body,
        mesh=mesh,
        in_specs=(canvases, canvases, columns, rows, rows, rows, columns, rows, rows, columns, P(), P(), P(), P()),
        out_specs=(canvases, canvases, columns, rows, rows, rows, columns, rows, rows, columns),
        check_vma=False,
    )
```
